32 devices in a mesh: uv: 16 (over z, y, core), freq: 2 (over x).
Axes of the slice: x: 2, y: 2, z: 4, core: 2. Of those that a mesh axis runs over, the one named last changes fastest.
Arguments:
- visibility: float32 [2, 512, 8, 128], P('freq', 'uv'), may hold values from -6 to 6
- uv_offset: float32 [2, 512, 2, 128], P('freq', 'uv'), may hold values from -12 to 12
- w_offset: float32 [2, 512, 128], P('freq', 'uv'), may hold values from -40 to 40
- taper: float32 [32, 32], replicated, may hold values from 0.2 to 1
- row_count: int32 [2, 512], P('freq', 'uv'), may hold values from 1 to 128, as said below
- block_owner: int32 [2, 512, 1], P('freq', 'uv'), may hold values from 0 to 15; in each aligned block of 32 rows (0 to 31, 32 to 63, ..., all dimensions but the last counted through in order) at most 4 rows name the same one
- block_slot: int32 [2, 512], P('freq', 'uv'), may hold values from 0 to 15
- subgrid_offset: int32 [256, 2], P('uv'), may hold values from 0 to 96
Outputs:
- grid: float32 [2048, 8, 128], P(('uv', 'freq'))
The draws below stay inside these ranges and needn't reach their ends.
Inputs may be any that keep to these rules, and one draw needn't show every extreme that they name: `block_owner`: among the 32 blocks of one device at most 4 name the same owner, a bound that some block reaches of them. `row_count`: some block has all 128 rows live.
All inputs are finite; a program needn't handle non-finite values.
Results may differ from the reference program's by a relative error of at most 0.0003.
Values sent between devices are 32-bit elements; how exact they have to be, the bound alone decides.
No kernel may reach another device: no remote copies, remote signals or barrier semaphores. Data moves between devices by JAX's collectives and lax.ppermute only.
A program may use at most 64 MiB of HBM per device.

```python
import math
import jax
import jax.numpy as jnp
import numpy as np
from jax import lax

SUB = 32
BLK = 128
NB_DEV = 32
SUB_DEV = 16
TILE = 128
OWNERS = 16
CAP = 4
NF = 2
NBT = 512
SUBGRIDS = 256
N_UV = 16


def draw_row_count(key, part):
    counts = jax.random.randint(key, (NF, NBT), 1, BLK + 1, dtype=jnp.int32)
    return counts.at[0, 0].set(BLK)


def plant(values, key, least, top_value):
    shape = values.shape
    index_at = [jax.random.randint(jax.random.fold_in(key, axis), (), 0, shape[axis]) for axis in range(len(shape))]
    values = values.at[tuple(index_at)].set(least)
    longest = shape.index(max(shape))
    index_at[longest] = (index_at[longest] + 1) % shape[longest]
    return values.at[tuple(index_at)].set(top_value)


def shard_levels(key, dims, shards, low, top_value):
    gain, own = 1.0, jax.random.fold_in(key, 6)
    for position, shards_of in shards:
        draws = jnp.exp(jax.random.uniform(jax.random.fold_in(own, position), (shards_of,), jnp.float32, low / len(shards), top_value / len(shards)))
        gain = gain * jnp.repeat(draws, dims[position] // shards_of).reshape([-1 if axis == position else 1 for axis in range(len(dims))])
    return gain


def deal_out(stream_key, own, number, rows, number_of, top, most, slope):
    ranking = jax.random.permutation(stream_key, number_of)
    packed, usual = load_shares(number_of, rows * top, most, slope, True), load_shares(number_of, rows * top, most, slope, False)
    places = jnp.arange(number_of)

    def named(sizes, rotation):
        used = int((sizes > 0).sum())
        fixed = max(1, used // 4)
        passed = fixed + (places - fixed + rotation * (used - fixed)) % max(1, number_of - fixed)
        return jnp.zeros((number_of,), jnp.int32).at[ranking[jnp.where(places < fixed, places, passed)]].set(jnp.asarray(sizes, jnp.int32))

    sizes = jnp.where(number % 4 == 0, named(packed, number // 4), named(usual, number - number // 4 - 1))
    mixed = jax.random.permutation(jax.random.fold_in(own, 3), number_of)
    source_of, receiver = mixed[0:number_of // 2 * 2:2], mixed[1:number_of // 2 * 2:2]
    slack = jnp.minimum(sizes[source_of] - 1, most - sizes[receiver]) // 2
    slack = jnp.where((source_of == ranking[0]) | (receiver == ranking[0]) | (sizes[receiver] == 0), 0, jnp.maximum(slack, 0))
    passed = jax.random.randint(jax.random.fold_in(own, 4), (number_of // 2,), 0, 1 << 20) % (slack + 1)
    sizes = sizes.at[source_of].add(-passed).at[receiver].add(passed)
    members = jnp.searchsorted(jnp.cumsum(sizes), jnp.arange(rows * top), side="right").astype(jnp.int32)
    grid = members.reshape(top, rows).T
    grid = grid[jax.random.permutation(jax.random.fold_in(own, 1), rows)]
    rotation = jax.random.randint(jax.random.fold_in(own, 2), (rows, 1), 0, top)
    return jnp.take_along_axis(grid, (jnp.arange(top)[None, :] + rotation) % top, axis=1)


def load_shares(count, total, bound, slope, full):
    portions = [(1 << 20) // math.isqrt(rank ** slope) + 1 for rank in range(1, count + 1)]
    largest = bound if full else min(bound, max(-(-total // count), total * portions[0] // sum(portions)))
    least = 1 if total - largest >= count - 1 else 0
    holding, surplus = [largest] + [least] * (count - 1), total - largest - least * (count - 1)
    while surplus > 0:
        candidates = [i for i in range(1, count) if holding[i] < largest] or [i for i in range(1, count) if holding[i] < bound]
        whole, remaining = sum([portions[i] for i in candidates]), surplus
        for i in candidates:
            extra = min(bound - holding[i], max(1, remaining * portions[i] // whole), surplus)
            holding[i] = holding[i] + extra
            surplus = surplus - extra
    return np.array(holding)


def noise(stream_key, shape, scale, reach, split=(), kind=jnp.bfloat16):
    array = jax.random.normal(stream_key, shape, jnp.float32) * scale
    if len(split) > 0:
        array = shard_levels(stream_key, shape, split, -0.22, 0.18) * array
    return jnp.clip(array, min=-reach, max=reach).astype(kind)


def setup_inputs(seed: int = 0) -> dict:
    streams_of = jax.random.split(jax.random.key(seed), 9)
    visibility = noise(streams_of[0], (NF, NBT, 8, BLK), 1.0, 6.0, ((0, 2), (1, 16)), jnp.float32)
    uv_offset = jnp.clip(jax.random.uniform(streams_of[1], (NF, NBT, 2, BLK), jnp.float32, -12.0, 12.0) * shard_levels(streams_of[1], (NF, NBT, 2, BLK), ((0, 2), (1, 16)), -0.4, 0.0), -12.0, 12.0)
    w_offset = jnp.clip(jax.random.uniform(streams_of[2], (NF, NBT, BLK), jnp.float32, -40.0, 40.0) * shard_levels(streams_of[2], (NF, NBT, BLK), ((0, 2), (1, 16)), -0.4, 0.0), -40.0, 40.0)
    taper = jnp.clip(jax.random.uniform(streams_of[3], (SUB, SUB), jnp.float32, 0.2, 1.0), 0.2, 1.0)
    row_count = draw_row_count(jax.random.fold_in(streams_of[8], 71), 0)
    block_owner_keys = jax.random.split(jax.random.fold_in(streams_of[5], 1), NF * NBT // NB_DEV)
    block_owner_turns = jax.random.permutation(jax.random.fold_in(streams_of[5], 3), NF * NBT // NB_DEV)
    block_owner = jax.vmap(lambda own, number: deal_out(jax.random.fold_in(streams_of[5], 2), own, number, NB_DEV, OWNERS, 1, CAP, 2))(block_owner_keys, block_owner_turns).reshape((NF, NBT, 1))
    block_slot = plant(jax.random.randint(streams_of[6], (NF, NBT), 0, SUB_DEV), jax.random.fold_in(streams_of[6], 1), 0, SUB_DEV - 1).astype(jnp.int32)
    subgrid_offset = plant(jax.random.randint(streams_of[7], (SUBGRIDS, 2), 0, TILE - SUB + 1), jax.random.fold_in(streams_of[7], 1), 0, TILE - SUB).astype(jnp.int32)
    return dict(visibility=visibility, uv_offset=uv_offset, w_offset=w_offset, taper=taper, row_count=row_count, block_owner=block_owner, block_slot=block_slot, subgrid_offset=subgrid_offset)


field_width = 0.5

def phase_images(data, counts, taper):
    blk = data.shape[2]
    sub = taper.shape[0]
    pix = sub * sub
    index = jnp.arange(pix, dtype=jnp.int32)
    xs = (index % sub).astype(jnp.float32)
    ys = (index // sub).astype(jnp.float32)
    lpos = field_width * (xs - sub / 2) / sub
    mpos = field_width * (ys - sub / 2) / sub
    npos = 1.0 - jnp.sqrt(1.0 - lpos * lpos - mpos * mpos)
    live = (jnp.arange(blk, dtype=jnp.int32)[None, :] < counts[:, None]).astype(jnp.float32)
    theta = 2.0 * math.pi * (data[:, 8, :, None] * lpos + data[:, 9, :, None] * mpos + data[:, 10, :, None] * npos)
    real_part = data[:, 0:4] * live[:, None, :]
    imag_part = data[:, 4:8] * live[:, None, :]
    left = jnp.concatenate([jnp.concatenate([real_part, imag_part], 2), jnp.concatenate([imag_part, -real_part], 2)], 1)
    right = jnp.concatenate([jnp.cos(theta), jnp.sin(theta)], 1)
    images = jnp.einsum('gak,gkp->gap', left, right, precision=lax.Precision.HIGHEST)
    return images * (taper.reshape(pix) * (1.0 / math.sqrt(blk)))

def reference(visibility, uv_offset, w_offset, taper, row_count, block_owner, block_slot, subgrid_offset):
    blocks = NF * NBT
    data = jnp.concatenate([visibility, uv_offset, w_offset[:, :, None, :]], 2).reshape(blocks, 11, BLK)
    counts = row_count.reshape(blocks)
    group = math.gcd(blocks, 64)

    def one_group(pieces):
        return phase_images(pieces[0], pieces[1], taper)
    images = lax.map(one_group, (data.reshape(blocks // group, group, 11, BLK), counts.reshape(blocks // group, group)))
    images = images.reshape(blocks, 8, SUB, SUB)
    spectrum = jnp.fft.fft2(images[:, 0:4] + 1j * images[:, 4:8]) / SUB
    grids = jnp.concatenate([jnp.real(spectrum), jnp.imag(spectrum)], 1).astype(jnp.float32)
    owner = block_owner.reshape(blocks).astype(jnp.int32)
    subgrid = owner * SUB_DEV + block_slot.reshape(blocks).astype(jnp.int32)
    corner_row = subgrid_offset[subgrid, 0]
    corner_col = subgrid_offset[subgrid, 1]
    steps = jnp.arange(SUB, dtype=jnp.int32)
    rows = corner_row[:, None, None] + steps[None, :, None]
    cols = corner_col[:, None, None] + steps[None, None, :]
    flat = ((owner[:, None, None] * TILE + rows) * TILE + cols).reshape(-1).astype(jnp.int32)
    values = jnp.transpose(grids, (0, 2, 3, 1)).reshape(-1, 8)
    summed = jax.ops.segment_sum(values, flat, num_segments=N_UV * TILE * TILE)
    return jnp.transpose(summed.reshape(N_UV * TILE, TILE, 8), (0, 2, 1))
```

```python
import functools
import math

import jax
import jax.numpy as jnp
import numpy as np
from jax import lax
from jax.experimental import pallas as pl
from jax.experimental.pallas import tpu as pltpu
from jax.sharding import PartitionSpec as P

TILE = 128
LANES = 128
COMPS = 8
field_width = 0.5

F32 = jnp.float32
BF16 = jnp.bfloat16


def fit_even(function, degree):
    points = np.cos(np.pi * (np.arange(400) + 0.5) / 400) * 0.125 + 0.125
    fit = np.polynomial.chebyshev.Chebyshev.fit(points, function(np.sqrt(points)), degree, domain=[0, 0.25])
    return [float(c) for c in fit.convert(kind=np.polynomial.Polynomial).coef]


COS_COEF = fit_even(lambda f: np.cos(2 * np.pi * f), 5)
SIN_COEF = fit_even(lambda f: np.sin(2 * np.pi * f) / f, 5)


def cos_sin_turns(turns):
    frac = turns - jnp.round(turns)
    square = frac * frac
    cos_out = COS_COEF[-1] * square + COS_COEF[-2]
    sin_out = SIN_COEF[-1] * square + SIN_COEF[-2]
    for c in COS_COEF[-3::-1]:
        cos_out = cos_out * square + c
    for c in SIN_COEF[-3::-1]:
        sin_out = sin_out * square + c
    return cos_out, sin_out * frac


def split(x):
    high = x.astype(BF16)
    return high, (x - high.astype(F32)).astype(BF16)


def iota(shape, axis):
    return lax.broadcasted_iota(jnp.int32, shape, axis)


def pack_kernel(count_ref, owner_ref, slot_ref, vis_ref, uv_ref, w_ref, out_ref, used_ref, *, cap):
    owners = out_ref.shape[0]
    blk = vis_ref.shape[2]
    blocks = vis_ref.shape[0]
    extra = out_ref.shape[1] - cap
    shape = (8, blk)
    row, lane = iota(shape, 0), iota(shape, 1)

    def clear(o, carry):
        used_ref[o] = 0
        for t in range(extra):
            out_ref[o, cap + t] = jnp.zeros(shape, F32)
        return carry

    lax.fori_loop(0, owners, clear, 0)

    def place(j, carry):
        o = owner_ref[j]
        r = used_ref[o]
        used_ref[o] = r + 1
        count = count_ref[j]
        out_ref[o, r] = vis_ref[j]
        u, v, w = uv_ref[j, 0:1, :], uv_ref[j, 1:2, :], w_ref[pl.ds(j, 1), :]
        part = row % 4
        coords = jnp.where(part == 0, u, jnp.where(part == 1, v, w))
        t = cap + r // 2
        mine = (row // 4 == r % 2) & (part < 3)
        out_ref[o, t] = jnp.where(mine, coords, out_ref[o, t])
        meta = jnp.where(lane == 2 * r, count.astype(F32), slot_ref[j].astype(F32))
        here = (row == 3) & (lane // 2 == r)
        out_ref[o, cap] = jnp.where(here, meta, out_ref[o, cap])
        return carry

    lax.fori_loop(0, blocks, place, 0)


def pack(counts, owner, slot, vis, uv, w, owners, cap):
    extra = (cap + 1) // 2
    blk = vis.shape[2]
    smem = pl.BlockSpec(memory_space=pltpu.SMEM)
    vmem = pl.BlockSpec(memory_space=pltpu.VMEM)
    return pl.pallas_call(
        functools.partial(pack_kernel, cap=cap),
        out_shape=jax.ShapeDtypeStruct((owners, cap + extra, 8, blk), F32),
        in_specs=[smem] * 3 + [vmem] * 3,
        out_specs=vmem,
        scratch_shapes=[pltpu.SMEM((owners,), jnp.int32)],
        name="pack",
    )(counts, owner, slot, vis, uv, w)


def transform_constants(sub, blk):
    half = sub // 2
    scale = 1.0 / math.sqrt(blk) / sub
    k = np.arange(sub)
    plus = np.zeros((4, half, sub), np.complex128)
    minus = np.zeros((4, half, sub), np.complex128)
    for a in range(half):
        up = np.exp(-2j * np.pi * k * (half + a) / sub) * scale
        down = np.exp(-2j * np.pi * k * (half - a) / sub) * scale
        if a == 0:
            plus[0, 0], plus[1, 0] = up, -1j * up
            minus[2, 0], minus[3, 0] = -1j * scale, scale
        else:
            plus[:, a] = [up, -1j * up, -1j * up, -up]
            minus[:, a] = [down, -1j * down, 1j * down, down]
    both = np.stack([plus, minus]).reshape(2, 4 * half, sub)
    blank = np.zeros((2, 4 * half, LANES - 2 * sub))
    coef = np.concatenate([both.real, both.imag, blank], 2).astype(np.float32)
    pick = np.zeros((2, 4, half, sub), np.float32)
    for a in range(half):
        pick[0, :, a, half + a] = 1
        pick[1, :, a, half - a if a else 0] = 1
    return coef, pick.reshape(2, 4 * half, sub)


def tables_kernel(taper_ref, coef_ref, pick_ref, high_ref, low_ref):
    sub = taper_ref.shape[0]
    dims = (((1,), (1,)), ((), ()))
    plus, minus = [
        lax.dot_general(pick_ref[i], taper_ref[...], dims, precision=lax.Precision.HIGHEST)
        for i in range(2)
    ]
    for y in range(sub):
        m = plus[:, y : y + 1] * coef_ref[0] + minus[:, y : y + 1] * coef_ref[1]
        high_ref[y], low_ref[y] = split(m)


def tables(taper, blk):
    sub = taper.shape[0]
    coef, pick = transform_constants(sub, blk)
    vmem = pl.BlockSpec(memory_space=pltpu.VMEM)
    shape = jax.ShapeDtypeStruct((sub, 2 * sub, LANES), BF16)
    return pl.pallas_call(
        tables_kernel,
        out_shape=[shape, shape],
        in_specs=[vmem] * 3,
        out_specs=[vmem] * 2,
        name="tables",
    )(taper, jnp.asarray(coef), jnp.asarray(pick))


def turn_by_i(x):
    return jnp.where(iota(x.shape, 0) < 4, -1.0, 1.0) * pltpu.roll(x, 4, 0)


def times(x, c):
    if abs(c - 1) < 1e-12:
        return x
    if abs(c + 1j) < 1e-12:
        return jnp.where(iota(x.shape, 0) < 4, 1.0, -1.0) * pltpu.roll(x, 4, 0)
    sign = jnp.where(iota(x.shape, 0) < 4, -c.imag, c.imag)
    return c.real * x + sign * pltpu.roll(x, 4, 0)


def fourier(values):
    count = len(values)
    if count == 1:
        return values
    even, odd = fourier(values[0::2]), fourier(values[1::2])
    odd = [times(x, np.exp(-2j * np.pi * k / count)) for k, x in enumerate(odd)]
    return [e + o for e, o in zip(even, odd)] + [e - o for e, o in zip(even, odd)]


def tile_kernel(
    offset_ref, part_ref, recv_ref, high_ref, low_ref, *refs, cap, sub, parts, chunks
):
    outs, rest = refs[:parts], refs[parts:]
    meta_ref, fill_ref, n_ref, buf_v, buf_c, cos_b, sin_b, x16_ref, acc_ref, sums_ref, z_ref, tile_ref, sem = rest
    owners = recv_ref.shape[0]
    owned = offset_ref.shape[0]
    blk = recv_ref.shape[3]
    half = sub // 2
    shape = (8, blk)
    lane = iota(shape, 1)
    copy = pltpu.make_async_copy(recv_ref.at[:, cap], meta_ref, sem)
    copy.start()

    step = field_width / sub
    for g in range(half + 1):
        a = iota((half, blk), 0).astype(F32)
        s = (a * a + float(g * g)) * (step * step)
        n_ref[g] = s / (1.0 + jnp.sqrt(1.0 - s))
    tile_ref[...] = jnp.zeros_like(tile_ref)
    s_corner = 2.0 * half * half * step * step
    n_corner = s_corner / (1.0 + math.sqrt(1.0 - s_corner))

    copy.wait()

    def clear(s, carry):
        fill_ref[s] = 0
        return carry

    lax.fori_loop(0, owned, clear, 0)

    def gather(src, carry):
        for r in range(cap):
            count = meta_ref[src, 3, 2 * r].astype(jnp.int32)
            slot = meta_ref[src, 3, 2 * r + 1].astype(jnp.int32)

            @pl.when(count > 0)
            def _():
                p = fill_ref[slot]
                fill_ref[slot] = p + count
                at = slot * chunks + p // blk
                shift = p % blk
                rows = (r % 2) * 4
                v = pltpu.roll(recv_ref[src, r], shift, 1)
                c = pltpu.roll(recv_ref[src, cap + r // 2], shift, 1)[rows : rows + 4]
                keep = lane < shift
                buf_v[at] = jnp.where(keep, buf_v[at], v)
                buf_c[at] = jnp.where(keep[0:4], buf_c[at], c)
                buf_v[at + 1] = v
                buf_c[at + 1] = c

        return carry

    lax.fori_loop(0, owners, gather, 0)

    unit = iota((half, blk), 0).astype(F32) * step
    first = iota((half, blk), 0) == 0
    dims = (((1,), (1,)), ((), ()))

    def chunk(slot, k):
        live = lane < fill_ref[slot] - k * blk
        at = slot * chunks + k
        vis = jnp.where(live, buf_v[at], 0.0)
        coords = jnp.where(live[0:4], buf_c[at], 0.0)
        u, v, w = coords[0:1], coords[1:2], coords[2:3]
        cos_a, sin_a = cos_sin_turns(u * unit)
        cb, sb = cos_sin_turns(v * unit)
        cos_b[...] = cb
        sin_b[...] = sb
        edge = jnp.where(iota(shape, 0) == 0, u * (half * step), jnp.where(iota(shape, 0) == 1, v * (half * step), w * n_corner))
        cos_e, sin_e = cos_sin_turns(edge)
        ca16, sa16 = cos_e[0:1], sin_e[0:1]
        cb16, sb16 = cos_e[1:2], sin_e[1:2]
        cw16, sw16 = cos_sin_turns(w * n_ref[half])
        x16_ref[0, 0:half] = cw16 * ca16 + sw16 * sa16
        x16_ref[1, 0:half] = sw16 * ca16 - cw16 * sa16
        x16_ref[0, half : half + 1] = cos_e[2:3] * ca16 + sin_e[2:3] * sa16
        x16_ref[1, half : half + 1] = sin_e[2:3] * ca16 - cos_e[2:3] * sa16
        turned = jnp.where(iota(shape, 0) < 4, 1.0, -1.0) * pltpu.roll(vis, 4, 0)
        for g in range(half + 1):
            if g < half:
                cw, sw = cos_sin_turns(w * n_ref[g])
                cbg, sbg = cos_b[g : g + 1], sin_b[g : g + 1]
            else:
                cw, sw = cw16, sw16
                cbg, sbg = cb16, sb16
            q3 = jnp.where(first, x16_ref[1, g : g + 1], cw * sin_a)
            q4 = jnp.where(first, x16_ref[0, g : g + 1], sw * sin_a)
            weights = jnp.concatenate([cw * cos_a, sw * cos_a, q3, q4], 0)
            high, low = split(weights)
            straight, across = vis * cbg, turned * sbg
            left = jnp.concatenate([straight + across, straight - across], 0)
            left_high, left_low = split(left)
            left_all = jnp.concatenate(
                [
                    jnp.concatenate([left_high, left_high], 1),
                    jnp.concatenate([left_low, left_low], 1),
                ],
                0,
            )
            out = lax.dot_general(
                left_all, jnp.concatenate([high, low], 1), dims, preferred_element_type=F32
            )
            acc_ref[g] = acc_ref[g] + out

    def one_slot(slot, carry):
        acc_ref[...] = jnp.zeros_like(acc_ref)
        used = (fill_ref[slot] + (blk - 1)) // blk

        def step_chunk(k, c):
            chunk(slot, k)
            return c

        lax.fori_loop(0, used, step_chunk, 0)
        at = pl.ds(pl.multiple_of(slot * 8, 8), 8)
        for g in range(half + 1):
            both = acc_ref[g, 0:16] + acc_ref[g, 16:32]
            if g < half:
                sums_ref[half + g, at] = both[0:8]
            if g > 0:
                sums_ref[half - g, at] = both[8:16]
        return carry

    lax.fori_loop(0, owned, one_slot, 0)

    def along_x(y, carry):
        left_high, left_low = split(sums_ref[y])
        right = high_ref[y]
        z_ref[y] = (
            jnp.dot(left_high, right, preferred_element_type=F32)
            + jnp.dot(left_low, right, preferred_element_type=F32)
            + jnp.dot(left_high, low_ref[y], preferred_element_type=F32)
        )
        return carry

    lax.fori_loop(0, sub, along_x, 0)

    wide = iota((8, LANES), 1)

    def place(slot, carry):
        at = pl.ds(pl.multiple_of(slot * 8, 8), 8)
        lines = []
        for y in range(sub):
            pair = z_ref[y, at]
            lines.append(pair + turn_by_i(pltpu.roll(pair, LANES - sub, 1)))
        lines = fourier(lines)
        corner_row, corner_col = offset_ref[slot, 0], offset_ref[slot, 1]
        for ky in range(sub):
            line = pltpu.roll(jnp.where(wide < sub, lines[ky], 0.0), corner_col, 1)
            tile_ref[corner_row + ky] = tile_ref[corner_row + ky] + line
        return carry

    lax.fori_loop(0, owned, place, 0)

    rows = TILE // parts
    for p in range(parts):
        which = lax.rem(part_ref[0] + p, parts)
        outs[p][...] = tile_ref[pl.ds(which * rows, rows)]


def tile_parts(offsets, part, recv, high, low, cap, parts):
    owners, _, _, blk = recv.shape
    owned = offsets.shape[0]
    sub = high.shape[0]
    half = sub // 2
    chunks = owners * cap + 1
    smem = pl.BlockSpec(memory_space=pltpu.SMEM)
    vmem = pl.BlockSpec(memory_space=pltpu.VMEM)
    rows = TILE // parts
    return pl.pallas_call(
        functools.partial(tile_kernel, cap=cap, sub=sub, parts=parts, chunks=chunks),
        out_shape=[jax.ShapeDtypeStruct((rows, COMPS, TILE), F32)] * parts,
        in_specs=[smem, smem, vmem, vmem, vmem],
        out_specs=[vmem] * parts,
        scratch_shapes=[
            pltpu.SMEM((owners, 8, blk), F32),
            pltpu.SMEM((owned,), jnp.int32),
            pltpu.VMEM((half + 1, half, blk), F32),
            pltpu.VMEM((owned * chunks + 1, 8, blk), F32),
            pltpu.VMEM((owned * chunks + 1, 4, blk), F32),
            pltpu.VMEM((half, blk), F32),
            pltpu.VMEM((half, blk), F32),
            pltpu.VMEM((2, half + 8, blk), F32),
            pltpu.VMEM((half + 1, 32, 4 * half), F32),
            pltpu.VMEM((sub, owned * 8, 4 * half), F32),
            pltpu.VMEM((sub, owned * 8, LANES), F32),
            pltpu.VMEM((TILE, COMPS, TILE), F32),
            pltpu.SemaphoreType.DMA,
        ],
        name="tile",
    )(offsets, part, recv, high, low)


def shards(
    visibility, uv_offset, w_offset, taper, row_count, block_owner, block_slot, subgrid_offset
):
    blocks_here, blk = visibility.shape[1], visibility.shape[3]
    owners = lax.axis_size("uv")
    parts = lax.axis_size("freq")
    cap = 2 * blocks_here // owners
    sent = pack(
        row_count[0],
        block_owner[0, :, 0],
        block_slot[0],
        visibility[0],
        uv_offset[0],
        w_offset[0],
        owners,
        cap,
    )
    recv = lax.all_to_all(sent, "uv", split_axis=0, concat_axis=0, tiled=True)
    high, low = tables(taper, blk)
    part = lax.axis_index("freq").astype(jnp.int32).reshape(1)
    pieces = tile_parts(subgrid_offset, part, recv, high, low, cap, parts)
    total = pieces[0]
    for s in range(1, parts):
        total = total + lax.ppermute(pieces[s], "freq", [(i, (i + s) % parts) for i in range(parts)])
    return total


def solution(mesh):
    placed = (
        P("freq", "uv", None, None),
        P("freq", "uv", None, None),
        P("freq", "uv", None),
        P(),
        P("freq", "uv"),
        P("freq", "uv", None),
        P("freq", "uv"),
        P("uv", None),
    )
    return jax.shard_map(
        shards, mesh=mesh, in_specs=placed, out_specs=P(("uv", "freq"), None, None), check_vma=False
    )
```

```python
import functools
import math

import jax
import jax.numpy as jnp
import numpy as np
from jax import lax
from jax.experimental import pallas as pl
from jax.experimental.pallas import tpu as pltpu
from jax.sharding import PartitionSpec as P

TILE = 128
LANES = 128
COMPS = 8
field_width = 0.5

F32 = jnp.float32
BF16 = jnp.bfloat16


def fit_even(function, degree):
    points = np.cos(np.pi * (np.arange(400) + 0.5) / 400) * 0.125 + 0.125
    fit = np.polynomial.chebyshev.Chebyshev.fit(points, function(np.sqrt(points)), degree, domain=[0, 0.25])
    return [float(c) for c in fit.convert(kind=np.polynomial.Polynomial).coef]


SIN_COEF = fit_even(lambda f: math.sqrt(2) * np.sin(np.pi * f) / f, 3)
COS_COEF = fit_even(lambda f: math.sqrt(2) * np.cos(np.pi * f), 4)


def cos_sin_turns(turns):
    frac = turns - jnp.round(turns)
    square = frac * frac
    cos_half = COS_COEF[-1] * square + COS_COEF[-2]
    sin_half = SIN_COEF[-1] * square + SIN_COEF[-2]
    for c in COS_COEF[-3::-1]:
        cos_half = cos_half * square + c
    for c in SIN_COEF[-3::-1]:
        sin_half = sin_half * square + c
    sin_half = sin_half * frac
    return 1.0 - sin_half * sin_half, sin_half * cos_half


def split(x):
    high = x.astype(BF16)
    return high, (x - high.astype(F32)).astype(BF16)


def iota(shape, axis):
    return lax.broadcasted_iota(jnp.int32, shape, axis)


def pack_kernel(count_ref, owner_ref, slot_ref, vis_ref, uv_ref, w_ref, out_ref, used_ref, *, cap):
    owners = out_ref.shape[0]
    blk = vis_ref.shape[2]
    blocks = vis_ref.shape[0]
    extra = out_ref.shape[1] - cap
    shape = (8, blk)
    row, lane = iota(shape, 0), iota(shape, 1)

    def clear(o, carry):
        used_ref[o] = 0
        for t in range(extra):
            out_ref[o, cap + t] = jnp.zeros(shape, F32)
        return carry

    lax.fori_loop(0, owners, clear, 0)

    def place(j, carry):
        o = owner_ref[j]
        r = used_ref[o]
        used_ref[o] = r + 1
        count = count_ref[j]
        out_ref[o, r] = vis_ref[j]
        u, v, w = uv_ref[j, 0:1, :], uv_ref[j, 1:2, :], w_ref[pl.ds(j, 1), :]
        part = row % 4
        coords = jnp.where(part == 0, u, jnp.where(part == 1, v, w))
        t = cap + r // 2
        mine = (row // 4 == r % 2) & (part < 3)
        out_ref[o, t] = jnp.where(mine, coords, out_ref[o, t])
        meta = jnp.where(lane == 2 * r, count.astype(F32), slot_ref[j].astype(F32))
        here = (row == 3) & (lane // 2 == r)
        out_ref[o, cap] = jnp.where(here, meta, out_ref[o, cap])
        return carry

    lax.fori_loop(0, blocks, place, 0)


def pack(counts, owner, slot, vis, uv, w, owners, cap):
    extra = (cap + 1) // 2
    blk = vis.shape[2]
    smem = pl.BlockSpec(memory_space=pltpu.SMEM)
    vmem = pl.BlockSpec(memory_space=pltpu.VMEM)
    return pl.pallas_call(
        functools.partial(pack_kernel, cap=cap),
        out_shape=jax.ShapeDtypeStruct((owners, cap + extra, 8, blk), F32),
        in_specs=[smem] * 3 + [vmem] * 3,
        out_specs=vmem,
        scratch_shapes=[pltpu.SMEM((owners,), jnp.int32)],
        name="pack",
    )(counts, owner, slot, vis, uv, w)


def transform_constants(sub, blk):
    half = sub // 2
    scale = 1.0 / math.sqrt(blk) / sub
    k = np.arange(sub)
    plus = np.zeros((4, half, sub), np.complex128)
    minus = np.zeros((4, half, sub), np.complex128)
    for a in range(half):
        up = np.exp(-2j * np.pi * k * (half + a) / sub) * scale
        down = np.exp(-2j * np.pi * k * (half - a) / sub) * scale
        if a == 0:
            plus[0, 0], plus[1, 0] = up, -1j * up
            minus[2, 0], minus[3, 0] = -1j * scale, scale
        else:
            plus[:, a] = [up, -1j * up, -1j * up, -up]
            minus[:, a] = [down, -1j * down, 1j * down, down]
    both = np.stack([plus, minus]).reshape(2, 4 * half, sub)
    blank = np.zeros((2, 4 * half, LANES - sub))
    coef = np.concatenate([both.real, blank, both.imag, blank], 2).astype(np.float32)
    pick = np.zeros((2, 4, half, sub), np.float32)
    for a in range(half):
        pick[0, :, a, half + a] = 1
        pick[1, :, a, half - a if a else 0] = 1
    return coef, pick.reshape(2, 4 * half, sub)


def tables_kernel(taper_ref, coef_ref, pick_ref, high_ref, low_ref):
    sub = taper_ref.shape[0]
    dims = (((1,), (1,)), ((), ()))
    plus, minus = [
        lax.dot_general(pick_ref[i], taper_ref[...], dims, precision=lax.Precision.HIGHEST)
        for i in range(2)
    ]
    for y in range(sub):
        m = plus[:, y : y + 1] * coef_ref[0] + minus[:, y : y + 1] * coef_ref[1]
        high_ref[y], low_ref[y] = split(m)


def tables(taper, blk):
    sub = taper.shape[0]
    coef, pick = transform_constants(sub, blk)
    vmem = pl.BlockSpec(memory_space=pltpu.VMEM)
    shape = jax.ShapeDtypeStruct((sub, 2 * sub, 2 * LANES), BF16)
    return pl.pallas_call(
        tables_kernel,
        out_shape=[shape, shape],
        in_specs=[vmem] * 3,
        out_specs=[vmem] * 2,
        name="tables",
    )(taper, jnp.asarray(coef), jnp.asarray(pick))


def twiddle_sines(sub):
    return [math.sin(2 * math.pi * k / sub) for k in range(1, sub // 4 + 1)]


def fourier(values, times):
    count = len(values)
    if count == 1:
        return values
    even, odd = fourier(values[0::2], times), fourier(values[1::2], times)
    odd = [times(x, k, count) for k, x in enumerate(odd)]
    return [e + o for e, o in zip(even, odd)] + [e - o for e, o in zip(even, odd)]


def tile_kernel(
    offset_ref, part_ref, recv_hbm, high_ref, low_ref, *refs, cap, sub, parts, chunks
):
    outs, rest = refs[:parts], refs[parts:]
    (
        meta_ref, fill_ref, recv_ref, n_ref, buf_v, buf_c, b_ref, w_ref, x16_ref, sums_ref, z_ref,
        tile_ref, twiddle_ref, sems,
    ) = rest
    owners = recv_ref.shape[0]
    owned = offset_ref.shape[0]
    blk = recv_ref.shape[3]
    half = sub // 2
    shape = (8, blk)
    row, lane = iota(shape, 0), iota(shape, 1)
    assert half == 16
    meta_copy = pltpu.make_async_copy(recv_hbm.at[:, cap], meta_ref, sems.at[0])
    recv_copy = pltpu.make_async_copy(recv_hbm, recv_ref, sems.at[1])
    meta_copy.start()
    recv_copy.start()

    step = field_width / sub
    rowf = row.astype(F32)

    def n_of(y, x):
        s = (x * x + y * y) * (step * step)
        return s / (1.0 + jnp.sqrt(1.0 - s))

    for j in range(8):
        n_ref[j] = n_of(float(j), rowf + 8.0)
        shifted = jnp.where(row >= j, 0.0, 8.0)
        n_ref[8 + j] = n_of(float(j) + shifted, rowf + shifted)
    n_ref[16] = n_of(rowf + 8.0, rowf + 8.0)
    n_ref[17] = n_of(float(half), rowf)
    n_ref[18] = n_of(float(half), rowf + 8.0)
    s_corner = 2.0 * half * half * step * step
    n_corner = s_corner / (1.0 + math.sqrt(1.0 - s_corner))
    tile_ref[...] = jnp.zeros_like(tile_ref)
    sums_ref[...] = jnp.zeros_like(sums_ref)
    sign = jnp.where(row < 4, -1.0, 1.0)
    for i, value in enumerate(twiddle_sines(sub)):
        twiddle_ref[i] = value * sign

    def clear(s, carry):
        fill_ref[s] = 0
        return carry

    lax.fori_loop(0, owned, clear, 0)
    meta_copy.wait()
    recv_copy.wait()

    def gather(src, carry):
        moved = []
        for r in range(cap):
            count = meta_ref[src, 3, 2 * r].astype(jnp.int32)
            slot = meta_ref[src, 3, 2 * r + 1].astype(jnp.int32)
            p = fill_ref[slot]
            fill_ref[slot] = p + count
            shift = p % blk
            rows = (r % 2) * 4
            v = pltpu.roll(recv_ref[src, r], shift, 1)
            c = pltpu.roll(recv_ref[src, cap + r // 2], shift, 1)[rows : rows + 4]
            moved.append((slot * chunks + p // blk, lane < shift, v, c))
        for at, keep, v, c in moved:
            buf_v[at] = jnp.where(keep, buf_v[at], v)
            buf_c[at] = jnp.where(keep[0:4], buf_c[at], c)
            buf_v[at + 1] = v
            buf_c[at + 1] = c
        return carry

    lax.fori_loop(0, owners, gather, 0)

    unit = rowf * step
    first = row == 0
    dims = (((1,), (1,)), ((), ()))

    def chunk(slot, k):
        live = lane < fill_ref[slot] - k * blk
        at = slot * chunks + k
        vis = jnp.where(live, buf_v[at], 0.0)
        coords = jnp.where(live[0:4], buf_c[at], 0.0)
        u, v, w = coords[0:1], coords[1:2], coords[2:3]
        far = jnp.where(
            row < 2,
            u * jnp.where(row == 0, 8 * step, half * step),
            jnp.where(row < 4, v * jnp.where(row == 2, 8 * step, half * step), w * n_corner),
        )
        cos_f, sin_f = cos_sin_turns(far)
        cos_f, sin_f = [[x[i : i + 1] for i in range(5)] for x in (cos_f, sin_f)]

        def line(t, c8, s8):
            c, s = cos_sin_turns(t * unit)
            return [c, c * c8 - s * s8], [s, s * c8 + c * s8]

        cos_a, sin_a = line(u, cos_f[0], sin_f[0])
        cos_b, sin_b = line(v, cos_f[2], sin_f[2])
        for i in range(2):
            b_ref[0, 8 * i : 8 * i + 8] = cos_b[i]
            b_ref[1, 8 * i : 8 * i + 8] = sin_b[i]
        b_ref[0, half : half + 1] = cos_f[3]
        b_ref[1, half : half + 1] = sin_f[3]
        ca16, sa16 = cos_f[1], sin_f[1]

        for j in range(8):
            w_ref[0, 0, 8 * j : 8 * j + 8], w_ref[1, 0, 8 * j : 8 * j + 8] = cos_sin_turns(w * n_ref[j])
            both = cos_sin_turns(w * n_ref[8 + j])
            for i in range(2):
                w_ref[i, 1, 8 * j : 8 * j + 8] = both[i]
                w_ref[i, 2, 8 * j : 8 * j + 8] = both[i]
        diagonal = cos_sin_turns(w * n_ref[16])
        for j in range(8):
            for i in range(2):
                w_ref[i, 2, 9 * j : 9 * j + 1] = diagonal[i][j : j + 1]
        edge = [cos_sin_turns(w * n_ref[17 + i]) for i in range(2)]
        for i in range(2):
            cw, sw = edge[i]
            x16_ref[0, 8 * i : 8 * i + 8] = cw * ca16 + sw * sa16
            x16_ref[1, 8 * i : 8 * i + 8] = sw * ca16 - cw * sa16
        x16_ref[0, half : half + 1] = cos_f[4] * ca16 + sin_f[4] * sa16
        x16_ref[1, half : half + 1] = sin_f[4] * ca16 - cos_f[4] * sa16

        def plane(i, g):
            if g == half:
                return edge[0][i], edge[1][i]
            j = g % 8
            own, across = pl.ds(8 * j, 8), pl.ds(j, 8, stride=8)
            if g < 8:
                return jnp.where(row >= j, w_ref[i, 1, own], w_ref[i, 1, across]), w_ref[i, 0, own]
            return w_ref[i, 0, across], jnp.where(row <= j, w_ref[i, 2, own], w_ref[i, 2, across])

        turned = -sign * pltpu.roll(vis, 4, 0)
        at = pl.ds(pl.multiple_of(slot * 8, 8), 8)
        for g in range(half + 1):
            cw, sw = plane(0, g), plane(1, g)
            q1 = [cw[i] * cos_a[i] for i in range(2)]
            q2 = [sw[i] * cos_a[i] for i in range(2)]
            q3 = [cw[i] * sin_a[i] for i in range(2)]
            q4 = [sw[i] * sin_a[i] for i in range(2)]
            q3[0] = jnp.where(first, x16_ref[1, g : g + 1], q3[0])
            q4[0] = jnp.where(first, x16_ref[0, g : g + 1], q4[0])
            high, low = split(jnp.concatenate(q1 + q2 + q3 + q4, 0))
            straight, across = vis * b_ref[0, g : g + 1], turned * b_ref[1, g : g + 1]
            left_high, left_low = split(jnp.concatenate([straight + across, straight - across], 0))
            left = jnp.concatenate(
                [
                    jnp.concatenate([left_high, left_high], 1),
                    jnp.concatenate([left_low, left_low], 1),
                ],
                0,
            )
            out = lax.dot_general(
                left, jnp.concatenate([high, low], 1), dims, preferred_element_type=F32
            )
            if g < half:
                sums_ref[half + g, at] += out[0:8] + out[16:24]
            if g > 0:
                sums_ref[half - g, at] += out[8:16] + out[24:32]

    def one_slot(slot, carry):
        used = (fill_ref[slot] + (blk - 1)) // blk

        def step_chunk(k, c):
            chunk(slot, k)
            return c

        return lax.fori_loop(0, used, step_chunk, carry)

    lax.fori_loop(0, owned, one_slot, 0)

    def along_x(y, carry):
        left = jnp.concatenate(split(sums_ref[y]), 1)
        high, low = high_ref[y], low_ref[y]
        right = jnp.concatenate([high, high, low, jnp.zeros_like(low)], 0)
        z_ref[y] = jnp.dot(jnp.concatenate([left, left], 1), right, preferred_element_type=F32)
        return carry

    lax.fori_loop(0, sub, along_x, 0, unroll=2)

    together = math.gcd(owned, LANES // sub)

    def times(x, k, count):
        if k == 0:
            return x
        k = k * (sub // count)
        cosine = math.cos(2 * math.pi * k / sub)
        sine = twiddle_ref[min(k, sub // 2 - k) - 1]
        turned = sine * pltpu.roll(x, 4, 0)
        return -turned if k == sub // 4 else cosine * x - turned

    def place(group, carry):
        lines = []
        for y in range(sub):
            real, imag = None, None
            for i in range(together):
                at = pl.ds(pl.multiple_of((group * together + i) * 8, 8), 8)
                re, im = z_ref[y, at, 0:LANES], z_ref[y, at, LANES : 2 * LANES]
                if i == 0:
                    real, imag = re, im
                else:
                    real = real + pltpu.roll(re, i * sub, 1)
                    imag = imag + pltpu.roll(im, i * sub, 1)
            lines.append(real + sign * pltpu.roll(imag, 4, 0))
        lines = fourier(lines, times)
        for i in range(together):
            slot = group * together + i
            corner_row, corner_col = offset_ref[slot, 0], offset_ref[slot, 1]
            here = (lane >= corner_col) & (lane < corner_col + sub)
            turn = (corner_col + (LANES - i * sub)) % LANES
            for ky in range(sub):
                moved = jnp.where(here, pltpu.roll(lines[ky], turn, 1), 0.0)
                tile_ref[corner_row + ky] += moved
        return carry

    lax.fori_loop(0, owned // together, place, 0)

    rows = TILE // parts
    for p in range(parts):
        which = lax.rem(part_ref[0] + p, parts)
        outs[p][...] = tile_ref[pl.ds(which * rows, rows)]


def tile_parts(offsets, part, recv, high, low, cap, parts):
    owners, tiles, _, blk = recv.shape
    owned = offsets.shape[0]
    sub = high.shape[0]
    half = sub // 2
    chunks = owners * cap + 1
    smem = pl.BlockSpec(memory_space=pltpu.SMEM)
    vmem = pl.BlockSpec(memory_space=pltpu.VMEM)
    rows = TILE // parts
    return pl.pallas_call(
        functools.partial(tile_kernel, cap=cap, sub=sub, parts=parts, chunks=chunks),
        out_shape=[jax.ShapeDtypeStruct((rows, COMPS, TILE), F32)] * parts,
        in_specs=[smem, smem, pl.BlockSpec(memory_space=pl.ANY), vmem, vmem],
        out_specs=[vmem] * parts,
        scratch_shapes=[
            pltpu.SMEM((owners, 8, blk), F32),
            pltpu.SMEM((owned,), jnp.int32),
            pltpu.VMEM((owners, tiles, 8, blk), F32),
            pltpu.VMEM((half + 3, 8, blk), F32),
            pltpu.VMEM((owned * chunks + 1, 8, blk), F32),
            pltpu.VMEM((owned * chunks + 1, 4, blk), F32),
            pltpu.VMEM((2, half + 8, blk), F32),
            pltpu.VMEM((2, 3, 64, blk), F32),
            pltpu.VMEM((2, half + 8, blk), F32),
            pltpu.VMEM((sub, owned * 8, 4 * half), F32),
            pltpu.VMEM((sub, owned * 8, 2 * LANES), F32),
            pltpu.VMEM((TILE, COMPS, TILE), F32),
            pltpu.VMEM((sub // 4, 8, LANES), F32),
            pltpu.SemaphoreType.DMA((2,)),
        ],
        name="tile",
    )(offsets, part, recv, high, low)


def shards(
    visibility, uv_offset, w_offset, taper, row_count, block_owner, block_slot, subgrid_offset
):
    blocks_here, blk = visibility.shape[1], visibility.shape[3]
    owners = lax.axis_size("uv")
    parts = lax.axis_size("freq")
    cap = 2 * blocks_here // owners
    sent = pack(
        row_count[0],
        block_owner[0, :, 0],
        block_slot[0],
        visibility[0],
        uv_offset[0],
        w_offset[0],
        owners,
        cap,
    )
    recv = lax.all_to_all(sent, "uv", split_axis=0, concat_axis=0, tiled=True)
    high, low = tables(taper, blk)
    part = lax.axis_index("freq").astype(jnp.int32).reshape(1)
    pieces = tile_parts(subgrid_offset, part, recv, high, low, cap, parts)
    total = pieces[0]
    for s in range(1, parts):
        total = total + lax.ppermute(pieces[s], "freq", [(i, (i + s) % parts) for i in range(parts)])
    return total


def solution(mesh):
    placed = (
        P("freq", "uv", None, None),
        P("freq", "uv", None, None),
        P("freq", "uv", None),
        P(),
        P("freq", "uv"),
        P("freq", "uv", None),
        P("freq", "uv"),
        P("uv", None),
    )
    return jax.shard_map(
        shards, mesh=mesh, in_specs=placed, out_specs=P(("uv", "freq"), None, None), check_vma=False
    )
```

```python
import functools
import math

import jax
import jax.numpy as jnp
import numpy as np
from jax import lax
from jax.experimental import pallas as pl
from jax.experimental.pallas import tpu as pltpu
from jax.sharding import PartitionSpec as P

TILE = 128
LANES = 128
COMPS = 8
SIDES = 2
field_width = 0.5

F32 = jnp.float32
BF16 = jnp.bfloat16


def fit_even(function, degree):
    points = np.cos(np.pi * (np.arange(400) + 0.5) / 400) * 0.125 + 0.125
    fit = np.polynomial.chebyshev.Chebyshev.fit(points, function(np.sqrt(points)), degree, domain=[0, 0.25])
    return [float(c) for c in fit.convert(kind=np.polynomial.Polynomial).coef]


SIN_COEF = fit_even(lambda f: math.sqrt(2) * np.sin(np.pi * f) / f, 3)
COS_COEF = fit_even(lambda f: math.sqrt(2) * np.cos(np.pi * f), 4)


def cos_sin_turns(turns):
    frac = turns - jnp.round(turns)
    square = frac * frac
    cos_half = COS_COEF[-1] * square + COS_COEF[-2]
    sin_half = SIN_COEF[-1] * square + SIN_COEF[-2]
    for c in COS_COEF[-3::-1]:
        cos_half = cos_half * square + c
    for c in SIN_COEF[-3::-1]:
        sin_half = sin_half * square + c
    sin_half = sin_half * frac
    return 1.0 - sin_half * sin_half, sin_half * cos_half


def split(x):
    high = x.astype(BF16)
    return high, (x - high.astype(F32)).astype(BF16)


def iota(shape, axis):
    return lax.broadcasted_iota(jnp.int32, shape, axis)


def pack_kernel(count_ref, owner_ref, slot_ref, vis_ref, uv_ref, w_ref, out_ref, used_ref, *, cap):
    owners = out_ref.shape[0]
    blk = vis_ref.shape[2]
    blocks = vis_ref.shape[0]
    extra = out_ref.shape[1] - cap
    shape = (8, blk)
    row, lane = iota(shape, 0), iota(shape, 1)

    def clear(o, carry):
        used_ref[o] = 0
        for t in range(extra):
            out_ref[o, cap + t] = jnp.zeros(shape, F32)
        return carry

    lax.fori_loop(0, owners, clear, 0)

    def place(j, carry):
        o = owner_ref[j]
        r = used_ref[o]
        used_ref[o] = r + 1
        count = count_ref[j]
        out_ref[o, r] = vis_ref[j]
        u, v, w = uv_ref[j, 0:1, :], uv_ref[j, 1:2, :], w_ref[pl.ds(j, 1), :]
        part = row % 4
        coords = jnp.where(part == 0, u, jnp.where(part == 1, v, w))
        t = cap + r // 2
        mine = (row // 4 == r % 2) & (part < 3)
        out_ref[o, t] = jnp.where(mine, coords, out_ref[o, t])
        meta = jnp.where(lane == 2 * r, count.astype(F32), slot_ref[j].astype(F32))
        here = (row == 3) & (lane // 2 == r)
        out_ref[o, cap] = jnp.where(here, meta, out_ref[o, cap])
        return carry

    lax.fori_loop(0, blocks, place, 0)


def pack(counts, owner, slot, vis, uv, w, owners, cap):
    extra = (cap + 1) // 2
    blk = vis.shape[2]
    smem = pl.BlockSpec(memory_space=pltpu.SMEM)
    vmem = pl.BlockSpec(memory_space=pltpu.VMEM)
    return pl.pallas_call(
        functools.partial(pack_kernel, cap=cap),
        out_shape=jax.ShapeDtypeStruct((owners, cap + extra, 8, blk), F32),
        in_specs=[smem] * 3 + [vmem] * 3,
        out_specs=vmem,
        scratch_shapes=[pltpu.SMEM((owners,), jnp.int32)],
        name="pack",
    )(counts, owner, slot, vis, uv, w)


def transform_constants(sub, blk, pack):
    half = sub // 2
    scale = 1.0 / math.sqrt(blk) / sub
    k = np.arange(sub)
    both = np.zeros((2, 4, half, sub), np.complex128)
    pick = np.zeros((2, 4, half, sub), np.float32)
    for a in range(half):
        up = np.exp(-2j * np.pi * k * (half + a) / sub) * scale
        down = np.exp(-2j * np.pi * k * (half - a) / sub) * scale
        pick[0, :, a, half + a] = 1
        pick[1, :, a, half - a if a else 0] = 1
        if a == 0:
            both[0, 0, 0], both[0, 1, 0] = up, -1j * up
            both[1, 2, 0], both[1, 3, 0] = -1j * scale, scale
        else:
            both[0, :, a] = [up, -1j * up, -1j * up, -up]
            both[1, :, a] = [down, -1j * down, 1j * down, down]
    both = both.reshape(2, 4 * half, sub)
    coef = np.zeros((2, pack, 2, 4 * half, LANES), np.float32)
    for i in range(pack):
        coef[:, i, 0, :, i * sub : (i + 1) * sub] = both.real
        coef[:, i, 1, :, i * sub : (i + 1) * sub] = both.imag
    return coef, pick.reshape(2, 4 * half, sub)


def tables_kernel(taper_ref, coef_ref, pick_ref, high_ref, low_ref):
    sub = taper_ref.shape[0]
    pack, rows = coef_ref.shape[1], coef_ref.shape[3]
    dims = (((1,), (1,)), ((), ()))
    plus, minus = [
        lax.dot_general(pick_ref[i], taper_ref[...], dims, precision=lax.Precision.HIGHEST)
        for i in range(2)
    ]
    for y in range(sub):
        up = jnp.broadcast_to(plus[:, y : y + 1], (rows, LANES))
        down = jnp.broadcast_to(minus[:, y : y + 1], (rows, LANES))
        for i in range(pack):
            for part in range(2):
                at = (y, pl.ds(i * rows, rows), pl.ds(part * LANES, LANES))
                m = up * coef_ref[0, i, part] + down * coef_ref[1, i, part]
                high_ref[at], low_ref[at] = split(m)


def tables(taper, blk):
    sub = taper.shape[0]
    pack = LANES // (2 * sub)
    coef, pick = transform_constants(sub, blk, pack)
    vmem = pl.BlockSpec(memory_space=pltpu.VMEM)
    shape = jax.ShapeDtypeStruct((sub, LANES, 2 * LANES), BF16)
    return pl.pallas_call(
        tables_kernel,
        out_shape=[shape, shape],
        in_specs=[vmem] * 3,
        out_specs=[vmem] * 2,
        name="tables",
    )(taper, jnp.asarray(coef), jnp.asarray(pick))


def twiddle_sines(sub):
    return [math.sin(2 * math.pi * k / sub) for k in range(1, sub // 4 + 1)]


def fourier(values, times):
    count = len(values)
    if count == 1:
        return values
    even, odd = fourier(values[0::2], times), fourier(values[1::2], times)
    odd = [times(x, k, count) for k, x in enumerate(odd)]
    return [e + o for e, o in zip(even, odd)] + [e - o for e, o in zip(even, odd)]


def lane_sums_row(place, pack, stride):
    return lax.rem(place, pack) * stride + lax.div(place, pack) * 8


def tile_kernel(*refs, inside, cap, sub, parts, chunks):
    if inside:
        offset_ref, part_ref, kept_ref, kept_v, kept_c, high_hbm, low_hbm, base_ref, out_ref, *rest = refs
    else:
        offset_ref, part_ref, recv_hbm, high_hbm, low_hbm = refs[:5]
        outs = refs[5 : 5 + parts]
        kept_ref, kept_v, kept_c, *rest = refs[5 + parts :]
        meta_ref, order_ref, place_ref, fill_ref, at_ref, live_ref, to_ref, recv_ref, buf_v, buf_c, *rest = rest
        owners = recv_ref.shape[0]
    (
        n_ref, b_ref, w_ref, x16_ref, sums_ref, z_ref, lines_ref, tile_ref, twiddle_ref, high_ref, low_ref, sems,
    ) = rest
    owned = offset_ref.shape[0]
    blk = kept_v.shape[2]
    half = sub // 2
    pack = LANES // (2 * sub)
    stride = owned // pack * 8
    keep_rows = TILE // parts
    head = owned + 3
    shape = (8, blk)
    row, lane = iota(shape, 0), iota(shape, 1)
    blk_log = blk.bit_length() - 1
    assert half == 16 and blk == 1 << blk_log
    table_copies = [
        pltpu.make_async_copy(high_hbm, high_ref, sems.at[2]),
        pltpu.make_async_copy(low_hbm, low_ref, sems.at[3]),
    ]
    if not inside:
        meta_copy = pltpu.make_async_copy(recv_hbm.at[:, cap, 3], meta_ref, sems.at[0])
        recv_copy = pltpu.make_async_copy(recv_hbm, recv_ref, sems.at[1])
        meta_copy.start()
        recv_copy.start()
    for copy in table_copies:
        copy.start()

    first_row = part_ref[0] * keep_rows
    if inside:
        listed, count_all = kept_ref[0], kept_ref[1]
    else:

        def clear(s, carry):
            fill_ref[s] = 0
            order_ref[s] = 0
            kept_ref[2 + s] = 0
            return carry

        lax.fori_loop(0, owned + 1, clear, 0)

        def choose(s, n):
            corner = offset_ref[s, 0]
            within = (corner >= first_row) & (corner + sub <= first_row + keep_rows)
            place_ref[s] = jnp.where(within, owned - 1 - (s - n), n)
            order_ref[n] = s
            kept_ref[2 + s - n] = s
            return n + jnp.where(within, 0, 1)

        count_all = lax.fori_loop(0, owned, choose, 0)
    groups = lax.div(count_all + (pack - 1), pack)

    step = field_width / sub
    rowf = row.astype(F32)

    def n_of(y, x):
        s = (x * x + y * y) * (step * step)
        return s / (1.0 + jnp.sqrt(1.0 - s))

    for j in range(8):
        n_ref[j] = n_of(float(j), rowf + 8.0)
        shifted = jnp.where(row >= j, 0.0, 8.0)
        n_ref[8 + j] = n_of(float(j) + shifted, rowf + shifted)
    n_ref[16] = n_of(rowf + 8.0, rowf + 8.0)
    n_ref[17] = n_of(float(half), rowf)
    n_ref[18] = n_of(float(half), rowf + 8.0)
    s_corner = 2.0 * half * half * step * step
    n_corner = s_corner / (1.0 + math.sqrt(1.0 - s_corner))
    sign = jnp.where(row < 4, -1.0, 1.0)
    for i, value in enumerate(twiddle_sines(sub)):
        twiddle_ref[i] = value * sign
    if inside:
        tile_ref[0:keep_rows] = base_ref[...]
        tile_ref[keep_rows:] = jnp.zeros((sub, COMPS, TILE), F32)
    else:
        tile_ref[...] = jnp.zeros_like(tile_ref)

    def clear_sums(group, carry):
        for i in range(pack):
            at = pl.ds(pl.multiple_of(i * stride + group * 8, 8), 8)
            for y in range(sub):
                sums_ref[y, at] = jnp.zeros((8, 4 * half), F32)
        return carry

    lax.fori_loop(0, groups, clear_sums, 0)
    if not inside:
        meta_copy.wait()
        recv_copy.wait()

        def gather(src, carry):
            moved = []
            for r in range(cap):
                count = meta_ref[src, 2 * r].astype(jnp.int32)
                place = place_ref[meta_ref[src, 2 * r + 1].astype(jnp.int32)]
                p = fill_ref[place]
                fill_ref[place] = p + count
                shift = p & (blk - 1)
                rows = (r % 2) * 4
                v = pltpu.roll(recv_ref[src, r], shift, 1)
                c = pltpu.roll(recv_ref[src, cap + r // 2], shift, 1)[rows : rows + 4]
                moved.append((place * chunks + lax.shift_right_logical(p, blk_log), lane < shift, v, c))
            for at, keep, v, c in moved:
                buf_v[at] = jnp.where(keep, buf_v[at], v)
                buf_c[at] = jnp.where(keep[0:4], buf_c[at], c)
                buf_v[at + 1] = v
                buf_c[at + 1] = c
            return carry

        lax.fori_loop(0, owners, gather, 0, unroll=2)

        def list_chunks(place, n):
            fill = fill_ref[place]
            to = lane_sums_row(place, pack, stride)

            def one(k, n):
                at_ref[n] = place * chunks + k
                live_ref[n] = fill - k * blk
                to_ref[n] = to
                return n + 1

            return lax.fori_loop(0, lax.shift_right_logical(fill + (blk - 1), blk_log), one, n)

        listed = lax.fori_loop(0, count_all, list_chunks, 0)
        for i in range(SIDES - 1):
            for ref in (at_ref, live_ref, to_ref):
                ref[listed + i] = 0

        def keep_chunks(i, n):
            place = owned - 1 - i
            fill = fill_ref[place]
            to = lane_sums_row(i, pack, stride)

            def one(k, n):
                live = lane < fill - k * blk
                kept_v[n] = jnp.where(live, buf_v[place * chunks + k], 0.0)
                kept_c[n] = jnp.where(live[0:4], buf_c[place * chunks + k], 0.0)
                kept_ref[head + n] = to
                return n + 1

            return lax.fori_loop(0, lax.shift_right_logical(fill + (blk - 1), blk_log), one, n)

        kept = lax.fori_loop(0, owned - count_all, keep_chunks, 0)
        for i in range(SIDES - 1):
            kept_v[kept + i] = jnp.zeros(shape, F32)
            kept_c[kept + i] = jnp.zeros((4, blk), F32)
            kept_ref[head + kept + i] = 0
        kept_ref[0] = kept
        kept_ref[1] = owned - count_all

    unit = rowf * step
    first = row == 0
    dims = (((1,), (1,)), ((), ()))

    def chunk(number, side):
        if inside:
            vis, coords, to = kept_v[number], kept_c[number], kept_ref[head + number]
        else:
            at, to = at_ref[number], to_ref[number]
            live = lane < live_ref[number]
            vis = jnp.where(live, buf_v[at], 0.0)
            coords = jnp.where(live[0:4], buf_c[at], 0.0)
        u, v, w = coords[0:1], coords[1:2], coords[2:3]
        far = jnp.where(
            row < 2,
            u * jnp.where(row == 0, 8 * step, half * step),
            jnp.where(row < 4, v * jnp.where(row == 2, 8 * step, half * step), w * n_corner),
        )
        cos_f, sin_f = cos_sin_turns(far)
        cos_f, sin_f = [[x[i : i + 1] for i in range(5)] for x in (cos_f, sin_f)]

        def line(t, c8, s8):
            c, s = cos_sin_turns(t * unit)
            return [c, c * c8 - s * s8], [s, s * c8 + c * s8]

        cos_a, sin_a = line(u, cos_f[0], sin_f[0])
        cos_b, sin_b = line(v, cos_f[2], sin_f[2])
        for i in range(2):
            b_ref[side, 0, 8 * i : 8 * i + 8] = cos_b[i]
            b_ref[side, 1, 8 * i : 8 * i + 8] = sin_b[i]
        b_ref[side, 0, half : half + 1] = cos_f[3]
        b_ref[side, 1, half : half + 1] = sin_f[3]
        ca16, sa16 = cos_f[1], sin_f[1]

        for j in range(8):
            both = cos_sin_turns(w * n_ref[8 + j])
            for i in range(2):
                w_ref[side, i, 1, 8 * j : 8 * j + 8] = both[i]
                w_ref[side, i, 2, 8 * j : 8 * j + 8] = both[i]
        diagonal = cos_sin_turns(w * n_ref[16])
        for j in range(8):
            for i in range(2):
                w_ref[side, i, 2, 9 * j : 9 * j + 1] = diagonal[i][j : j + 1]
        edge = [cos_sin_turns(w * n_ref[17 + i]) for i in range(2)]
        for i in range(2):
            cw, sw = edge[i]
            x16_ref[side, 0, 8 * i : 8 * i + 8] = cw * ca16 + sw * sa16
            x16_ref[side, 1, 8 * i : 8 * i + 8] = sw * ca16 - cw * sa16
        x16_ref[side, 0, half : half + 1] = cos_f[4] * ca16 + sin_f[4] * sa16
        x16_ref[side, 1, half : half + 1] = sin_f[4] * ca16 - cos_f[4] * sa16
        turned = -sign * pltpu.roll(vis, 4, 0)
        to = pl.ds(pl.multiple_of(to, 8), 8)

        def add(g, cw, sw):
            q1 = [cw[i] * cos_a[i] for i in range(2)]
            q2 = [sw[i] * cos_a[i] for i in range(2)]
            q3 = [cw[i] * sin_a[i] for i in range(2)]
            q4 = [sw[i] * sin_a[i] for i in range(2)]
            q3[0] = jnp.where(first, x16_ref[side, 1, g : g + 1], q3[0])
            q4[0] = jnp.where(first, x16_ref[side, 0, g : g + 1], q4[0])
            right = jnp.concatenate(split(jnp.concatenate(q1 + q2 + q3 + q4, 0)), 1)
            straight, across = vis * b_ref[side, 0, g : g + 1], turned * b_ref[side, 1, g : g + 1]
            left = jnp.concatenate(split(jnp.concatenate([straight + across, straight - across], 0)), 0)
            out = lax.dot_general(
                jnp.concatenate([left, left], 1), right, dims, preferred_element_type=F32
            )
            if g < half:
                sums_ref[half + g, to] += out[0:8] + out[16:24]
            if g > 0:
                sums_ref[half - g, to] += out[8:16] + out[24:32]

        add(half, [edge[i][0] for i in range(2)], [edge[i][1] for i in range(2)])
        for j in range(8):
            own, across = pl.ds(8 * j, 8), pl.ds(j, 8, stride=8)
            far_pair = cos_sin_turns(w * n_ref[j])
            pairs = []
            for i in range(2):
                w_ref[side, i, 0, 8 * j : 8 * j + 8] = far_pair[i]
                near = jnp.where(row >= j, w_ref[side, i, 1, own], w_ref[side, i, 1, across])
                pairs.append([near, far_pair[i]])
            add(j, *pairs)
        for j in range(8):
            own, across = pl.ds(8 * j, 8), pl.ds(j, 8, stride=8)
            pairs = []
            for i in range(2):
                far_one = jnp.where(row <= j, w_ref[side, i, 2, own], w_ref[side, i, 2, across])
                pairs.append([w_ref[side, i, 0, across], far_one])
            add(8 + j, *pairs)

    def some_chunks(i, carry):
        for side in range(SIDES):
            chunk(SIDES * i + side, side)
        return carry

    lax.fori_loop(0, lax.div(listed + (SIDES - 1), SIDES), some_chunks, 0)

    for copy in table_copies:
        copy.wait()

    def transform_x(used):
        def along_x(y, carry):
            sums = [sums_ref[y, i * stride : i * stride + used] for i in range(pack)]
            high, low = split(jnp.concatenate(sums, 1))
            right = jnp.concatenate([high_ref[y], high_ref[y]], 0)
            z_ref[y, 0:used] = jnp.dot(
                jnp.concatenate([high, low], 1), right, preferred_element_type=F32
            ) + jnp.dot(high, low_ref[y], preferred_element_type=F32)
            return carry

        lax.fori_loop(0, sub, along_x, 0, unroll=8)

    if inside:
        few = stride // 2

        @pl.when(groups * 8 <= few)
        def _():
            transform_x(few)

        @pl.when(groups * 8 > few)
        def _():
            transform_x(stride)
    else:
        transform_x(stride)

    def times(x, k, count):
        if k == 0:
            return x
        k = k * (sub // count)
        cosine = math.cos(2 * math.pi * k / sub)
        sine = twiddle_ref[min(k, sub // 2 - k) - 1]
        turned = sine * pltpu.roll(x, 4, 0)
        return -turned if k == sub // 4 else cosine * x - turned

    top_row = tile_ref.shape[0] - sub

    def put(group):
        def one(i, ky, turn, here, corner_row):
            moved = jnp.where(here, pltpu.roll(lines_ref[ky], turn, 1), 0.0)
            tile_ref[corner_row + ky] += moved

        steps = []
        for i in range(pack):
            slot = (kept_ref if inside else order_ref)[group * pack + i + (2 if inside else 0)]
            corner_row, corner_col = offset_ref[slot, 0], offset_ref[slot, 1]
            if inside:
                corner_row = jnp.clip(corner_row - first_row, 0, top_row)
            here = (lane >= corner_col) & (lane < corner_col + sub)
            turn = (corner_col + (LANES - i * sub)) & (LANES - 1)
            steps += [functools.partial(one, i, ky, turn, here, corner_row) for ky in range(sub)]
        return steps

    def place(group, carry):
        steps = put(jnp.maximum(group - 1, 0))
        at = pl.ds(pl.multiple_of(group * 8, 8), 8)
        lines = []
        for y in range(sub):
            for step_of in steps[y * pack : (y + 1) * pack]:
                step_of()
            real, imag = z_ref[y, at, 0:LANES], z_ref[y, at, LANES : 2 * LANES]
            lines.append(real + sign * pltpu.roll(imag, 4, 0))
        lines = fourier(lines, times)
        for ky in range(sub):
            lines_ref[ky] = lines[ky]
        return carry

    lines_ref[...] = jnp.zeros_like(lines_ref)
    lax.fori_loop(0, groups, place, 0)
    for step_of in put(jnp.maximum(groups - 1, 0)):
        step_of()

    if inside:
        out_ref[...] = tile_ref[0:keep_rows]
    else:
        for p in range(parts):
            which = lax.rem(part_ref[0] + p, parts)
            outs[p][...] = tile_ref[pl.ds(which * keep_rows, keep_rows)]


def tile_rows(offsets, part, given, high, low, cap, parts, base=None):
    inside = base is not None
    owned = offsets.shape[0]
    sub = high.shape[0]
    half = sub // 2
    blk = LANES
    smem = pl.BlockSpec(memory_space=pltpu.SMEM)
    vmem = pl.BlockSpec(memory_space=pltpu.VMEM)
    anywhere = pl.BlockSpec(memory_space=pl.ANY)
    rows = TILE // parts
    shape = jax.ShapeDtypeStruct((rows, COMPS, TILE), F32)
    scratch, chunks = [], None
    if inside:
        operands = [*given, high, low, base]
        in_specs = [smem, vmem, vmem, anywhere, anywhere, vmem]
        out_shape, out_specs = shape, vmem
    else:
        owners, tiles, _, blk = given.shape
        chunks = owners * cap + 1
        most = owners * cap + SIDES
        index = pltpu.SMEM((owned + 1,), jnp.int32)
        listing = pltpu.SMEM((most,), jnp.int32)
        operands = [given, high, low]
        in_specs = [anywhere] * 3
        out_shape = [shape] * parts + [
            jax.ShapeDtypeStruct((owned + 3 + most,), jnp.int32),
            jax.ShapeDtypeStruct((most, 8, blk), F32),
            jax.ShapeDtypeStruct((most, 4, blk), F32),
        ]
        out_specs = [vmem] * parts + [smem, vmem, vmem]
        scratch = [
            pltpu.SMEM((owners, blk), F32),
            index,
            index,
            index,
            listing,
            listing,
            listing,
            pltpu.VMEM((owners, tiles, 8, blk), F32),
            pltpu.VMEM((owned * chunks + 1, 8, blk), F32),
            pltpu.VMEM((owned * chunks + 1, 4, blk), F32),
        ]
    return pl.pallas_call(
        functools.partial(tile_kernel, inside=inside, cap=cap, sub=sub, parts=parts, chunks=chunks),
        out_shape=out_shape,
        in_specs=[smem, smem, *in_specs],
        out_specs=out_specs,
        scratch_shapes=scratch
        + [
            pltpu.VMEM((half + 3, 8, blk), F32),
            pltpu.VMEM((SIDES, 2, half + 8, blk), F32),
            pltpu.VMEM((SIDES, 2, 3, 64, blk), F32),
            pltpu.VMEM((SIDES, 2, half + 8, blk), F32),
            pltpu.VMEM((sub, owned * 8, 4 * half), F32),
            pltpu.VMEM((sub, owned * 2 * sub * 8 // LANES, 2 * LANES), F32),
            pltpu.VMEM((sub, 8, LANES), F32),
            pltpu.VMEM((rows + sub if inside else TILE, COMPS, TILE), F32),
            pltpu.VMEM((sub // 4, 8, LANES), F32),
            pltpu.VMEM(high.shape, BF16),
            pltpu.VMEM(low.shape, BF16),
            pltpu.SemaphoreType.DMA((4,)),
        ],
        name="inner" if inside else "tile",
    )(offsets, part, *operands)


def shards(
    visibility, uv_offset, w_offset, taper, row_count, block_owner, block_slot, subgrid_offset
):
    blocks_here, blk = visibility.shape[1], visibility.shape[3]
    owners = lax.axis_size("uv")
    parts = lax.axis_size("freq")
    cap = 2 * blocks_here // owners
    sent = pack(
        row_count[0],
        block_owner[0, :, 0],
        block_slot[0],
        visibility[0],
        uv_offset[0],
        w_offset[0],
        owners,
        cap,
    )
    recv = lax.all_to_all(sent, "uv", split_axis=0, concat_axis=0, tiled=True)
    high, low = tables(taper, blk)
    part = lax.axis_index("freq").astype(jnp.int32).reshape(1)
    *pieces, kept, kept_v, kept_c = tile_rows(subgrid_offset, part, recv, high, low, cap, parts)
    moved = [
        lax.ppermute(pieces[s], "freq", [(i, (i + s) % parts) for i in range(parts)])
        for s in range(1, parts)
    ]
    total = tile_rows(
        subgrid_offset, part, (kept, kept_v, kept_c), high, low, cap, parts, pieces[0]
    )
    for piece in moved:
        total = total + piece
    return total


def solution(mesh):
    placed = (
        P("freq", "uv", None, None),
        P("freq", "uv", None, None),
        P("freq", "uv", None),
        P(),
        P("freq", "uv"),
        P("freq", "uv", None),
        P("freq", "uv"),
        P("uv", None),
    )
    return jax.shard_map(
        shards, mesh=mesh, in_specs=placed, out_specs=P(("uv", "freq"), None, None), check_vma=False
    )
```

```python
import functools
import math

import jax
import jax.numpy as jnp
import numpy as np
from jax import lax
from jax.experimental import pallas as pl
from jax.experimental.pallas import tpu as pltpu
from jax.sharding import PartitionSpec as P

TILE = 128
LANES = 128
COMPS = 8
SIDES = 2
field_width = 0.5

F32 = jnp.float32
BF16 = jnp.bfloat16


def fit_even(function, degree):
    points = np.cos(np.pi * (np.arange(400) + 0.5) / 400) * 0.125 + 0.125
    fit = np.polynomial.chebyshev.Chebyshev.fit(points, function(np.sqrt(points)), degree, domain=[0, 0.25])
    return [float(c) for c in fit.convert(kind=np.polynomial.Polynomial).coef]


SIN_COEF = fit_even(lambda f: math.sqrt(2) * np.sin(np.pi * f) / f, 3)
COS_COEF = fit_even(lambda f: math.sqrt(2) * np.cos(np.pi * f), 4)


def cos_sin_turns(turns):
    frac = turns - jnp.round(turns)
    square = frac * frac
    cos_half = COS_COEF[-1] * square + COS_COEF[-2]
    sin_half = SIN_COEF[-1] * square + SIN_COEF[-2]
    for c in COS_COEF[-3::-1]:
        cos_half = cos_half * square + c
    for c in SIN_COEF[-3::-1]:
        sin_half = sin_half * square + c
    sin_half = sin_half * frac
    return 1.0 - sin_half * sin_half, sin_half * cos_half


def split(x):
    high = x.astype(BF16)
    return high, (x - high.astype(F32)).astype(BF16)


def in_vmem(x):
    return pltpu.with_memory_space_constraint(x, pltpu.VMEM)


def iota(shape, axis):
    return lax.broadcasted_iota(jnp.int32, shape, axis)


def pack_kernel(count_ref, owner_ref, slot_ref, vis_ref, uv_ref, w_ref, out_ref, used_ref, *, cap):
    owners = out_ref.shape[0]
    blk = vis_ref.shape[2]
    blocks = vis_ref.shape[0]
    extra = out_ref.shape[1] - cap
    shape = (8, blk)
    row, lane = iota(shape, 0), iota(shape, 1)

    def clear(o, carry):
        used_ref[o] = 0
        for t in range(extra):
            out_ref[o, cap + t] = jnp.zeros(shape, F32)
        return carry

    lax.fori_loop(0, owners, clear, 0)

    def place(j, carry):
        o = owner_ref[j]
        r = used_ref[o]
        used_ref[o] = r + 1
        count = count_ref[j]
        out_ref[o, r] = vis_ref[j]
        u, v, w = uv_ref[j, 0:1, :], uv_ref[j, 1:2, :], w_ref[pl.ds(j, 1), :]
        part = row % 4
        coords = jnp.where(part == 0, u, jnp.where(part == 1, v, w))
        t = cap + r // 2
        mine = (row // 4 == r % 2) & (part < 3)
        out_ref[o, t] = jnp.where(mine, coords, out_ref[o, t])
        meta = jnp.where(lane == 2 * r, count.astype(F32), slot_ref[j].astype(F32))
        here = (row == 3) & (lane // 2 == r)
        out_ref[o, cap] = jnp.where(here, meta, out_ref[o, cap])
        return carry

    lax.fori_loop(0, blocks, place, 0)


def pack(counts, owner, slot, vis, uv, w, owners, cap):
    extra = (cap + 1) // 2
    blk = vis.shape[2]
    smem = pl.BlockSpec(memory_space=pltpu.SMEM)
    vmem = pl.BlockSpec(memory_space=pltpu.VMEM)
    return pl.pallas_call(
        functools.partial(pack_kernel, cap=cap),
        out_shape=jax.ShapeDtypeStruct((owners, cap + extra, 8, blk), F32),
        in_specs=[smem] * 3 + [vmem] * 3,
        out_specs=vmem,
        scratch_shapes=[pltpu.SMEM((owners,), jnp.int32)],
        name="pack",
    )(counts, owner, slot, vis, uv, w)


def transform_constants(sub, blk, pack):
    half = sub // 2
    scale = 1.0 / math.sqrt(blk) / sub
    k = np.arange(sub)
    both = np.zeros((2, 4, half, sub), np.complex128)
    pick = np.zeros((2, 4, half, sub), np.float32)
    for a in range(half):
        up = np.exp(-2j * np.pi * k * (half + a) / sub) * scale
        down = np.exp(-2j * np.pi * k * (half - a) / sub) * scale
        pick[0, :, a, half + a] = 1
        pick[1, :, a, half - a if a else 0] = 1
        if a == 0:
            both[0, 0, 0], both[0, 1, 0] = up, -1j * up
            both[1, 2, 0], both[1, 3, 0] = -1j * scale, scale
        else:
            both[0, :, a] = [up, -1j * up, -1j * up, -up]
            both[1, :, a] = [down, -1j * down, 1j * down, down]
    both = both.reshape(2, 4 * half, sub)
    coef = np.zeros((2, pack, 4 * half, LANES), np.float32)
    for i in range(pack):
        for part, values in enumerate((both.real, both.imag)):
            at = (part * pack + i) * sub
            coef[:, i, :, at : at + sub] = values
    return coef, pick.reshape(2, 4 * half, sub)


def tables_kernel(taper_ref, coef_ref, pick_ref, table_ref):
    sub = taper_ref.shape[0]
    pack, rows = coef_ref.shape[1], coef_ref.shape[2]
    dims = (((1,), (1,)), ((), ()))
    plus, minus = [
        lax.dot_general(pick_ref[i], taper_ref[...], dims, precision=lax.Precision.HIGHEST)
        for i in range(2)
    ]
    for y in range(sub):
        up = jnp.broadcast_to(plus[:, y : y + 1], (rows, LANES))
        down = jnp.broadcast_to(minus[:, y : y + 1], (rows, LANES))
        for i in range(pack):
            at = pl.ds(i * rows, rows)
            table_ref[0, y, at], table_ref[1, y, at] = split(up * coef_ref[0, i] + down * coef_ref[1, i])


def tables(taper, blk):
    sub = taper.shape[0]
    pack = LANES // (2 * sub)
    coef, pick = transform_constants(sub, blk, pack)
    vmem = pl.BlockSpec(memory_space=pltpu.VMEM)
    return pl.pallas_call(
        tables_kernel,
        out_shape=jax.ShapeDtypeStruct((2, sub, LANES, LANES), BF16),
        in_specs=[vmem] * 3,
        out_specs=vmem,
        name="tables",
        compiler_params=pltpu.CompilerParams(vmem_limit_bytes=16 << 20),
    )(taper, jnp.asarray(coef), jnp.asarray(pick))


def twiddle_sines(sub):
    return [math.sin(2 * math.pi * k / sub) for k in range(1, sub // 4 + 1)]


def fourier(values, times):
    count = len(values)
    if count == 1:
        return values
    even, odd = fourier(values[0::2], times), fourier(values[1::2], times)
    odd = [times(x, k, count) for k, x in enumerate(odd)]
    return [e + o for e, o in zip(even, odd)] + [e - o for e, o in zip(even, odd)]


def lane_sums_row(place, pack, stride):
    return lax.rem(place, pack) * stride + lax.div(place, pack) * 8


def tile_kernel(*refs, inside, cap, sub, parts, chunks):
    if inside:
        offset_ref, part_ref, kept_ref, kept_v, kept_c, table_ref, base_ref, out_ref, *rest = refs
    else:
        offset_ref, part_ref, recv_ref, table_ref = refs[:4]
        outs = refs[4 : 4 + parts]
        kept_ref, kept_v, kept_c, *rest = refs[4 + parts :]
        meta_ref, order_ref, place_ref, fill_ref, at_ref, live_ref, to_ref, buf_v, buf_c, sem, *rest = rest
        owners = recv_ref.shape[0]
    (
        n_ref, b_ref, w_ref, x16_ref, sums_ref, z_ref, lines_ref, tile_ref, twiddle_ref,
    ) = rest
    owned = offset_ref.shape[0]
    blk = kept_v.shape[2]
    half = sub // 2
    pack = LANES // (2 * sub)
    stride = owned // pack * 8
    keep_rows = TILE // parts
    head = owned + 3
    shape = (8, blk)
    row, lane = iota(shape, 0), iota(shape, 1)
    blk_log = blk.bit_length() - 1
    assert half == 16 and blk == 1 << blk_log
    if not inside:
        meta_copy = pltpu.make_async_copy(recv_ref.at[:, cap, 3], meta_ref, sem)
        meta_copy.start()

    first_row = part_ref[0] * keep_rows
    if inside:
        listed, count_all = kept_ref[0], kept_ref[1]
    else:

        def clear(s, carry):
            fill_ref[s] = 0
            order_ref[s] = 0
            kept_ref[2 + s] = 0
            return carry

        lax.fori_loop(0, owned + 1, clear, 0)

        def choose(s, n):
            corner = offset_ref[s, 0]
            within = (corner >= first_row) & (corner + sub <= first_row + keep_rows)
            place_ref[s] = jnp.where(within, owned - 1 - (s - n), n)
            order_ref[n] = s
            kept_ref[2 + s - n] = s
            return n + jnp.where(within, 0, 1)

        count_all = lax.fori_loop(0, owned, choose, 0)
    groups = lax.div(count_all + (pack - 1), pack)

    step = field_width / sub
    rowf = row.astype(F32)

    def n_of(y, x):
        s = (x * x + y * y) * (step * step)
        return s / (1.0 + jnp.sqrt(1.0 - s))

    for j in range(8):
        n_ref[j] = n_of(float(j), rowf + 8.0)
        shifted = jnp.where(row >= j, 0.0, 8.0)
        n_ref[8 + j] = n_of(float(j) + shifted, rowf + shifted)
    n_ref[16] = n_of(rowf + 8.0, rowf + 8.0)
    n_ref[17] = n_of(float(half), rowf)
    n_ref[18] = n_of(float(half), rowf + 8.0)
    s_corner = 2.0 * half * half * step * step
    n_corner = s_corner / (1.0 + math.sqrt(1.0 - s_corner))
    sign = jnp.where(row < 4, -1.0, 1.0)
    for i, value in enumerate(twiddle_sines(sub)):
        twiddle_ref[i] = value * sign
    if inside:
        tile_ref[0:keep_rows] = base_ref[...]
        tile_ref[keep_rows:] = jnp.zeros((sub, COMPS, TILE), F32)
    else:
        tile_ref[...] = jnp.zeros_like(tile_ref)

    def clear_sums(group, carry):
        for i in range(pack):
            at = pl.ds(pl.multiple_of(i * stride + group * 8, 8), 8)
            for y in range(sub):
                sums_ref[y, at] = jnp.zeros((8, 4 * half), F32)
        return carry

    lax.fori_loop(0, groups, clear_sums, 0)
    if not inside:
        meta_copy.wait()

        def gather(src, carry):
            moved = []
            for r in range(cap):
                count = meta_ref[src, 2 * r].astype(jnp.int32)
                place = place_ref[meta_ref[src, 2 * r + 1].astype(jnp.int32)]
                p = fill_ref[place]
                fill_ref[place] = p + count
                shift = p & (blk - 1)
                rows = (r % 2) * 4
                v = pltpu.roll(recv_ref[src, r], shift, 1)
                c = pltpu.roll(recv_ref[src, cap + r // 2], shift, 1)[rows : rows + 4]
                moved.append((place * chunks + lax.shift_right_logical(p, blk_log), lane < shift, v, c))
            for at, keep, v, c in moved:
                buf_v[at] = jnp.where(keep, buf_v[at], v)
                buf_c[at] = jnp.where(keep[0:4], buf_c[at], c)
                buf_v[at + 1] = v
                buf_c[at + 1] = c
            return carry

        lax.fori_loop(0, owners, gather, 0, unroll=2)

        def list_chunks(place, n):
            fill = fill_ref[place]
            to = lane_sums_row(place, pack, stride)

            def one(k, n):
                at_ref[n] = place * chunks + k
                live_ref[n] = fill - k * blk
                to_ref[n] = to
                return n + 1

            return lax.fori_loop(0, lax.shift_right_logical(fill + (blk - 1), blk_log), one, n)

        listed = lax.fori_loop(0, count_all, list_chunks, 0)
        for i in range(SIDES - 1):
            for ref in (at_ref, live_ref, to_ref):
                ref[listed + i] = 0

        def keep_chunks(i, n):
            place = owned - 1 - i
            fill = fill_ref[place]
            to = lane_sums_row(i, pack, stride)

            def one(k, n):
                live = lane < fill - k * blk
                kept_v[n] = jnp.where(live, buf_v[place * chunks + k], 0.0)
                kept_c[n] = jnp.where(live[0:4], buf_c[place * chunks + k], 0.0)
                kept_ref[head + n] = to
                return n + 1

            return lax.fori_loop(0, lax.shift_right_logical(fill + (blk - 1), blk_log), one, n)

        kept = lax.fori_loop(0, owned - count_all, keep_chunks, 0)
        for i in range(SIDES - 1):
            kept_v[kept + i] = jnp.zeros(shape, F32)
            kept_c[kept + i] = jnp.zeros((4, blk), F32)
            kept_ref[head + kept + i] = 0
        kept_ref[0] = kept
        kept_ref[1] = owned - count_all

    unit = rowf * step
    first = row == 0
    dims = (((1,), (1,)), ((), ()))

    def chunk(number, side):
        if inside:
            vis, coords, to = kept_v[number], kept_c[number], kept_ref[head + number]
        else:
            at, to = at_ref[number], to_ref[number]
            live = lane < live_ref[number]
            vis = jnp.where(live, buf_v[at], 0.0)
            coords = jnp.where(live[0:4], buf_c[at], 0.0)
        u, v, w = coords[0:1], coords[1:2], coords[2:3]
        far = jnp.where(
            row < 2,
            u * jnp.where(row == 0, 8 * step, half * step),
            jnp.where(row < 4, v * jnp.where(row == 2, 8 * step, half * step), w * n_corner),
        )
        cos_f, sin_f = cos_sin_turns(far)
        cos_f, sin_f = [[x[i : i + 1] for i in range(5)] for x in (cos_f, sin_f)]

        def line(t, c8, s8):
            c, s = cos_sin_turns(t * unit)
            return [c, c * c8 - s * s8], [s, s * c8 + c * s8]

        cos_a, sin_a = line(u, cos_f[0], sin_f[0])
        cos_b, sin_b = line(v, cos_f[2], sin_f[2])
        for i in range(2):
            b_ref[side, 0, 8 * i : 8 * i + 8] = cos_b[i]
            b_ref[side, 1, 8 * i : 8 * i + 8] = sin_b[i]
        b_ref[side, 0, half : half + 1] = cos_f[3]
        b_ref[side, 1, half : half + 1] = sin_f[3]
        ca16, sa16 = cos_f[1], sin_f[1]

        for j in range(8):
            both = cos_sin_turns(w * n_ref[8 + j])
            for i in range(2):
                w_ref[side, i, 1, 8 * j : 8 * j + 8] = both[i]
                w_ref[side, i, 2, 8 * j : 8 * j + 8] = both[i]
        diagonal = cos_sin_turns(w * n_ref[16])
        for j in range(8):
            for i in range(2):
                w_ref[side, i, 2, 9 * j : 9 * j + 1] = diagonal[i][j : j + 1]
        edge = [cos_sin_turns(w * n_ref[17 + i]) for i in range(2)]
        for i in range(2):
            cw, sw = edge[i]
            x16_ref[side, 0, 8 * i : 8 * i + 8] = cw * ca16 + sw * sa16
            x16_ref[side, 1, 8 * i : 8 * i + 8] = sw * ca16 - cw * sa16
        x16_ref[side, 0, half : half + 1] = cos_f[4] * ca16 + sin_f[4] * sa16
        x16_ref[side, 1, half : half + 1] = sin_f[4] * ca16 - cos_f[4] * sa16
        turned = -sign * pltpu.roll(vis, 4, 0)
        to = pl.ds(pl.multiple_of(to, 8), 8)

        def add(g, cw, sw):
            q1 = [cw[i] * cos_a[i] for i in range(2)]
            q2 = [sw[i] * cos_a[i] for i in range(2)]
            q3 = [cw[i] * sin_a[i] for i in range(2)]
            q4 = [sw[i] * sin_a[i] for i in range(2)]
            q3[0] = jnp.where(first, x16_ref[side, 1, g : g + 1], q3[0])
            q4[0] = jnp.where(first, x16_ref[side, 0, g : g + 1], q4[0])
            right = jnp.concatenate(split(jnp.concatenate(q1 + q2 + q3 + q4, 0)), 1)
            straight, across = vis * b_ref[side, 0, g : g + 1], turned * b_ref[side, 1, g : g + 1]
            left = jnp.concatenate(split(jnp.concatenate([straight + across, straight - across], 0)), 0)
            out = lax.dot_general(
                jnp.concatenate([left, left], 1), right, dims, preferred_element_type=F32
            )
            if g < half:
                sums_ref[half + g, to] += out[0:8] + out[16:24]
            if g > 0:
                sums_ref[half - g, to] += out[8:16] + out[24:32]

        add(half, [edge[i][0] for i in range(2)], [edge[i][1] for i in range(2)])
        for j in range(8):
            own, across = pl.ds(8 * j, 8), pl.ds(j, 8, stride=8)
            far_pair = cos_sin_turns(w * n_ref[j])
            pairs = []
            for i in range(2):
                w_ref[side, i, 0, 8 * j : 8 * j + 8] = far_pair[i]
                near = jnp.where(row >= j, w_ref[side, i, 1, own], w_ref[side, i, 1, across])
                pairs.append([near, far_pair[i]])
            add(j, *pairs)
        for j in range(8):
            own, across = pl.ds(8 * j, 8), pl.ds(j, 8, stride=8)
            pairs = []
            for i in range(2):
                far_one = jnp.where(row <= j, w_ref[side, i, 2, own], w_ref[side, i, 2, across])
                pairs.append([w_ref[side, i, 0, across], far_one])
            add(8 + j, *pairs)

    def some_chunks(i, carry):
        for side in range(SIDES):
            chunk(SIDES * i + side, side)
        return carry

    lax.fori_loop(0, lax.div(listed + (SIDES - 1), SIDES), some_chunks, 0)

    def transform_x(used):
        def along_x(y, carry):
            sums = [sums_ref[y, i * stride : i * stride + used] for i in range(pack)]
            high, low = split(jnp.concatenate(sums, 1))
            right = jnp.concatenate([table_ref[0, y], table_ref[0, y]], 0)
            z_ref[y, 0:used] = jnp.dot(
                jnp.concatenate([high, low], 1), right, preferred_element_type=F32
            ) + jnp.dot(high, table_ref[1, y], preferred_element_type=F32)
            return carry

        lax.fori_loop(0, sub, along_x, 0, unroll=8)

    if inside:
        few = stride // 2

        @pl.when(groups * 8 <= few)
        def _():
            transform_x(few)

        @pl.when(groups * 8 > few)
        def _():
            transform_x(stride)
    else:
        transform_x(stride)

    def times(x, k, count):
        if k == 0:
            return x
        k = k * (sub // count)
        cosine = math.cos(2 * math.pi * k / sub)
        sine = twiddle_ref[min(k, sub // 2 - k) - 1]
        turned = sine * pltpu.roll(x, 4, 0)
        return -turned if k == sub // 4 else cosine * x - turned

    top_row = tile_ref.shape[0] - sub

    def put(group):
        def one(i, ky, turn, here, corner_row):
            moved = jnp.where(here, pltpu.roll(lines_ref[ky], turn, 1), 0.0)
            tile_ref[corner_row + ky] += moved

        steps = []
        for i in range(pack):
            slot = (kept_ref if inside else order_ref)[group * pack + i + (2 if inside else 0)]
            corner_row, corner_col = offset_ref[slot, 0], offset_ref[slot, 1]
            if inside:
                corner_row = jnp.clip(corner_row - first_row, 0, top_row)
            here = (lane >= corner_col) & (lane < corner_col + sub)
            turn = (corner_col + (LANES - i * sub)) & (LANES - 1)
            steps += [functools.partial(one, i, ky, turn, here, corner_row) for ky in range(sub)]
        return steps

    def place(group, carry):
        steps = put(jnp.maximum(group - 1, 0))
        at = pl.ds(pl.multiple_of(group * 8, 8), 8)
        lines = []
        for y in range(sub):
            for step_of in steps[y * pack : (y + 1) * pack]:
                step_of()
            pair = z_ref[y, at]
            imag = pltpu.roll(pair, LANES // 2, 1)
            lines.append(pair + sign * pltpu.roll(imag, 4, 0))
        lines = fourier(lines, times)
        for ky in range(sub):
            lines_ref[ky] = lines[ky]
        return carry

    lines_ref[...] = jnp.zeros_like(lines_ref)
    lax.fori_loop(0, groups, place, 0)
    for step_of in put(jnp.maximum(groups - 1, 0)):
        step_of()

    if inside:
        out_ref[...] = tile_ref[0:keep_rows]
    else:
        for p in range(parts):
            which = lax.rem(part_ref[0] + p, parts)
            outs[p][...] = tile_ref[pl.ds(which * keep_rows, keep_rows)]


def tile_rows(offsets, part, given, table, cap, parts, base=None):
    inside = base is not None
    owned = offsets.shape[0]
    sub = table.shape[1]
    half = sub // 2
    blk = LANES
    smem = pl.BlockSpec(memory_space=pltpu.SMEM)
    vmem = pl.BlockSpec(memory_space=pltpu.VMEM)
    rows = TILE // parts
    shape = jax.ShapeDtypeStruct((rows, COMPS, TILE), F32)
    scratch, chunks = [], None
    if inside:
        operands = [*given, table, base]
        in_specs = [smem] + [vmem] * 4
        out_shape, out_specs = shape, vmem
    else:
        owners, _, _, blk = given.shape
        chunks = owners * cap + 1
        most = owners * cap + SIDES
        index = pltpu.SMEM((owned + 1,), jnp.int32)
        listing = pltpu.SMEM((most,), jnp.int32)
        operands = [given, table]
        in_specs = [vmem] * 2
        out_shape = [shape] * parts + [
            jax.ShapeDtypeStruct((owned + 3 + most,), jnp.int32),
            jax.ShapeDtypeStruct((most, 8, blk), F32),
            jax.ShapeDtypeStruct((most, 4, blk), F32),
        ]
        out_specs = [vmem] * parts + [smem, vmem, vmem]
        scratch = [
            pltpu.SMEM((owners, blk), F32),
            index,
            index,
            index,
            listing,
            listing,
            listing,
            pltpu.VMEM((owned * chunks + 1, 8, blk), F32),
            pltpu.VMEM((owned * chunks + 1, 4, blk), F32),
            pltpu.SemaphoreType.DMA,
        ]
    return pl.pallas_call(
        functools.partial(tile_kernel, inside=inside, cap=cap, sub=sub, parts=parts, chunks=chunks),
        out_shape=out_shape,
        in_specs=[smem, smem, *in_specs],
        out_specs=out_specs,
        scratch_shapes=scratch
        + [
            pltpu.VMEM((half + 3, 8, blk), F32),
            pltpu.VMEM((SIDES, 2, half + 8, blk), F32),
            pltpu.VMEM((SIDES, 2, 3, 64, blk), F32),
            pltpu.VMEM((SIDES, 2, half + 8, blk), F32),
            pltpu.VMEM((sub, owned * 8, 4 * half), F32),
            pltpu.VMEM((sub, owned * 2 * sub * 8 // LANES, LANES), F32),
            pltpu.VMEM((sub, 8, LANES), F32),
            pltpu.VMEM((rows + sub if inside else TILE, COMPS, TILE), F32),
            pltpu.VMEM((sub // 4, 8, LANES), F32),
        ],
        name="inner" if inside else "tile",
        compiler_params=pltpu.CompilerParams(vmem_limit_bytes=20 << 20),
    )(offsets, part, *operands)


def shards(
    visibility, uv_offset, w_offset, taper, row_count, block_owner, block_slot, subgrid_offset
):
    blocks_here, blk = visibility.shape[1], visibility.shape[3]
    owners = lax.axis_size("uv")
    parts = lax.axis_size("freq")
    cap = 2 * blocks_here // owners
    sent = pack(
        row_count[0],
        block_owner[0, :, 0],
        block_slot[0],
        visibility[0],
        uv_offset[0],
        w_offset[0],
        owners,
        cap,
    )
    recv = lax.all_to_all(sent, "uv", split_axis=0, concat_axis=0, tiled=True)
    recv = in_vmem(recv)
    table = in_vmem(tables(taper, blk))
    part = lax.axis_index("freq").astype(jnp.int32).reshape(1)
    *pieces, kept, kept_v, kept_c = tile_rows(subgrid_offset, part, recv, table, cap, parts)
    moved = [
        lax.ppermute(pieces[s], "freq", [(i, (i + s) % parts) for i in range(parts)])
        for s in range(1, parts)
    ]
    total = tile_rows(
        subgrid_offset,
        part,
        (kept, in_vmem(kept_v), in_vmem(kept_c)),
        table,
        cap,
        parts,
        in_vmem(pieces[0]),
    )
    for piece in moved:
        total = total + piece
    return total


def solution(mesh):
    placed = (
        P("freq", "uv", None, None),
        P("freq", "uv", None, None),
        P("freq", "uv", None),
        P(),
        P("freq", "uv"),
        P("freq", "uv", None),
        P("freq", "uv"),
        P("uv", None),
    )
    return jax.shard_map(
        shards, mesh=mesh, in_specs=placed, out_specs=P(("uv", "freq"), None, None), check_vma=False
    )
```

```python
import functools
import math

import jax
import jax.numpy as jnp
import numpy as np
from jax import lax
from jax.experimental import pallas as pl
from jax.experimental.pallas import tpu as pltpu
from jax.sharding import PartitionSpec as P

TILE = 128
LANES = 128
COMPS = 8
SIDES = 2
field_width = 0.5

F32 = jnp.float32
BF16 = jnp.bfloat16


def fit_even(function, degree):
    points = np.cos(np.pi * (np.arange(400) + 0.5) / 400) * 0.125 + 0.125
    fit = np.polynomial.chebyshev.Chebyshev.fit(points, function(np.sqrt(points)), degree, domain=[0, 0.25])
    return [float(c) for c in fit.convert(kind=np.polynomial.Polynomial).coef]


SIN_COEF = fit_even(lambda f: math.sqrt(2) * np.sin(np.pi * f) / f, 3)
COS_COEF = fit_even(lambda f: math.sqrt(2) * np.cos(np.pi * f), 4)


def cos_sin_turns(turns):
    frac = turns - jnp.round(turns)
    square = frac * frac
    cos_half = COS_COEF[-1] * square + COS_COEF[-2]
    sin_half = SIN_COEF[-1] * square + SIN_COEF[-2]
    for c in COS_COEF[-3::-1]:
        cos_half = cos_half * square + c
    for c in SIN_COEF[-3::-1]:
        sin_half = sin_half * square + c
    sin_half = sin_half * frac
    return 1.0 - sin_half * sin_half, sin_half * cos_half


def split(x):
    high = x.astype(BF16)
    return high, (x - high.astype(F32)).astype(BF16)


def in_vmem(x):
    return pltpu.with_memory_space_constraint(x, pltpu.VMEM)


def iota(shape, axis):
    return lax.broadcasted_iota(jnp.int32, shape, axis)


def pack_kernel(*refs, cap):
    given, out_ref, held, used_ref, sems = refs[:6], refs[6], refs[7:13], refs[13], refs[14]
    count_ref, owner_ref, slot_ref, vis_ref, uv_ref, w_ref = held
    copies = [pltpu.make_async_copy(a, b, sems.at[i]) for i, (a, b) in enumerate(zip(given, held))]
    for copy in copies:
        copy.start()
    owners = out_ref.shape[0]
    blk = vis_ref.shape[2]
    blocks = vis_ref.shape[0]
    extra = out_ref.shape[1] - cap
    shape = (8, blk)
    row, lane = iota(shape, 0), iota(shape, 1)

    def clear(o, carry):
        used_ref[o] = 0
        for t in range(extra):
            out_ref[o, cap + t] = jnp.zeros(shape, F32)
        return carry

    lax.fori_loop(0, owners, clear, 0)
    for copy in copies:
        copy.wait()

    def place(j, carry):
        o = owner_ref[j]
        r = used_ref[o]
        used_ref[o] = r + 1
        count = count_ref[j]
        out_ref[o, r] = vis_ref[j]
        u, v, w = uv_ref[j, 0:1, :], uv_ref[j, 1:2, :], w_ref[pl.ds(j, 1), :]
        part = row % 4
        coords = jnp.where(part == 0, u, jnp.where(part == 1, v, w))
        t = cap + r // 2
        mine = (row // 4 == r % 2) & (part < 3)
        out_ref[o, t] = jnp.where(mine, coords, out_ref[o, t])
        meta = jnp.where(lane == 2 * r, count.astype(F32), slot_ref[j].astype(F32))
        here = (row == 3) & (lane // 2 == r)
        out_ref[o, cap] = jnp.where(here, meta, out_ref[o, cap])
        return carry

    lax.fori_loop(0, blocks, place, 0, unroll=4)


def pack(counts, owner, slot, vis, uv, w, owners, cap):
    extra = (cap + 1) // 2
    blk = vis.shape[2]
    operands = (counts, owner, slot, vis, uv, w)
    return pl.pallas_call(
        functools.partial(pack_kernel, cap=cap),
        out_shape=jax.ShapeDtypeStruct((owners, cap + extra, 8, blk), F32),
        in_specs=[pl.BlockSpec(memory_space=pltpu.HBM)] * 6,
        out_specs=pl.BlockSpec(memory_space=pltpu.VMEM),
        scratch_shapes=[pltpu.SMEM(x.shape, x.dtype) for x in operands[:3]]
        + [pltpu.VMEM(x.shape, x.dtype) for x in operands[3:]]
        + [pltpu.SMEM((owners,), jnp.int32), pltpu.SemaphoreType.DMA((6,))],
        name="pack",
    )(*operands)


def transform_constants(sub, blk, pack):
    half = sub // 2
    scale = 1.0 / math.sqrt(blk) / sub
    k = np.arange(sub)
    both = np.zeros((2, 4, half, sub), np.complex128)
    pick = np.zeros((2, 4, half, sub), np.float32)
    for a in range(half):
        up = np.exp(-2j * np.pi * k * (half + a) / sub) * scale
        down = np.exp(-2j * np.pi * k * (half - a) / sub) * scale
        pick[0, :, a, half + a] = 1
        pick[1, :, a, half - a if a else 0] = 1
        if a == 0:
            both[0, 0, 0], both[0, 1, 0] = up, -1j * up
            both[1, 2, 0], both[1, 3, 0] = -1j * scale, scale
        else:
            both[0, :, a] = [up, -1j * up, -1j * up, -up]
            both[1, :, a] = [down, -1j * down, 1j * down, down]
    both = both.reshape(2, 4 * half, sub)
    coef = np.zeros((2, pack, 4 * half, LANES), np.float32)
    for i in range(pack):
        for part, values in enumerate((both.real, both.imag)):
            at = (part * pack + i) * sub
            coef[:, i, :, at : at + sub] = values
    return coef, pick.reshape(2, 4 * half, sub)


def tables_kernel(taper_ref, coef_ref, pick_ref, table_ref):
    sub = taper_ref.shape[0]
    pack, rows = coef_ref.shape[1], coef_ref.shape[2]
    dims = (((1,), (1,)), ((), ()))
    plus, minus = [
        lax.dot_general(pick_ref[i], taper_ref[...], dims, precision=lax.Precision.HIGHEST)
        for i in range(2)
    ]
    for y in range(sub):
        up = jnp.broadcast_to(plus[:, y : y + 1], (rows, LANES))
        down = jnp.broadcast_to(minus[:, y : y + 1], (rows, LANES))
        for i in range(pack):
            at = pl.ds(i * rows, rows)
            table_ref[0, y, at], table_ref[1, y, at] = split(up * coef_ref[0, i] + down * coef_ref[1, i])


def tables(taper, blk):
    sub = taper.shape[0]
    pack = LANES // (2 * sub)
    coef, pick = transform_constants(sub, blk, pack)
    vmem = pl.BlockSpec(memory_space=pltpu.VMEM)
    return pl.pallas_call(
        tables_kernel,
        out_shape=jax.ShapeDtypeStruct((2, sub, LANES, LANES), BF16),
        in_specs=[vmem] * 3,
        out_specs=vmem,
        name="tables",
        compiler_params=pltpu.CompilerParams(vmem_limit_bytes=16 << 20),
    )(taper, jnp.asarray(coef), jnp.asarray(pick))


def twiddle_sines(sub):
    return [math.sin(2 * math.pi * k / sub) for k in range(1, sub // 4 + 1)]


def fourier(values, times):
    count = len(values)
    if count == 1:
        return values
    even, odd = fourier(values[0::2], times), fourier(values[1::2], times)
    odd = [times(x, k, count) for k, x in enumerate(odd)]
    return [e + o for e, o in zip(even, odd)] + [e - o for e, o in zip(even, odd)]


def lane_sums_row(place, pack, stride):
    return lax.rem(place, pack) * stride + lax.div(place, pack) * 8


def tile_kernel(*refs, inside, cap, sub, parts, chunks):
    if inside:
        offset_ref, part_ref, kept_ref, kept_v, kept_c, table_ref, base_ref, out_ref, *rest = refs
    else:
        offset_ref, part_ref, recv_ref, table_ref = refs[:4]
        outs = refs[4 : 4 + parts]
        kept_ref, kept_v, kept_c, *rest = refs[4 + parts :]
        meta_ref, order_ref, place_ref, fill_ref, at_ref, live_ref, to_ref, buf_v, buf_c, sem, *rest = rest
        owners = recv_ref.shape[0]
    (
        n_ref, b_ref, w_ref, x16_ref, sums_ref, z_ref, lines_ref, tile_ref, twiddle_ref,
    ) = rest
    owned = offset_ref.shape[0]
    blk = kept_v.shape[2]
    half = sub // 2
    pack = LANES // (2 * sub)
    stride = owned // pack * 8
    keep_rows = TILE // parts
    head = owned + 3
    shape = (8, blk)
    row, lane = iota(shape, 0), iota(shape, 1)
    blk_log = blk.bit_length() - 1
    assert half == 16 and blk == 1 << blk_log
    if not inside:
        meta_copy = pltpu.make_async_copy(recv_ref.at[:, cap, 3], meta_ref, sem)
        meta_copy.start()

    first_row = part_ref[0] * keep_rows
    if inside:
        listed, count_all = kept_ref[0], kept_ref[1]
    else:

        def clear(s, carry):
            fill_ref[s] = 0
            order_ref[s] = 0
            kept_ref[2 + s] = 0
            return carry

        lax.fori_loop(0, owned + 1, clear, 0)

        def choose(s, n):
            corner = offset_ref[s, 0]
            within = (corner >= first_row) & (corner + sub <= first_row + keep_rows)
            place_ref[s] = jnp.where(within, owned - 1 - (s - n), n)
            order_ref[n] = s
            kept_ref[2 + s - n] = s
            return n + jnp.where(within, 0, 1)

        count_all = lax.fori_loop(0, owned, choose, 0)
    groups = lax.div(count_all + (pack - 1), pack)

    step = field_width / sub
    rowf = row.astype(F32)

    def n_of(y, x):
        s = (x * x + y * y) * (step * step)
        return s / (1.0 + jnp.sqrt(1.0 - s))

    for j in range(8):
        n_ref[j] = n_of(float(j), rowf + 8.0)
        shifted = jnp.where(row >= j, 0.0, 8.0)
        n_ref[8 + j] = n_of(float(j) + shifted, rowf + shifted)
    n_ref[16] = n_of(rowf + 8.0, rowf + 8.0)
    n_ref[17] = n_of(float(half), rowf)
    n_ref[18] = n_of(float(half), rowf + 8.0)
    s_corner = 2.0 * half * half * step * step
    n_corner = s_corner / (1.0 + math.sqrt(1.0 - s_corner))
    sign = jnp.where(row < 4, -1.0, 1.0)
    for i, value in enumerate(twiddle_sines(sub)):
        twiddle_ref[i] = value * sign
    if inside:
        tile_ref[0:keep_rows] = base_ref[...]
        tile_ref[keep_rows:] = jnp.zeros((sub, COMPS, TILE), F32)
    else:
        tile_ref[...] = jnp.zeros_like(tile_ref)

    def clear_sums(group, carry):
        for i in range(pack):
            at = pl.ds(pl.multiple_of(i * stride + group * 8, 8), 8)
            for y in range(sub):
                sums_ref[y, at] = jnp.zeros((8, 4 * half), F32)
        return carry

    lax.fori_loop(0, groups, clear_sums, 0)
    if not inside:
        meta_copy.wait()

        def gather(src, carry):
            moved = []
            for r in range(cap):
                count = meta_ref[src, 2 * r].astype(jnp.int32)
                place = place_ref[meta_ref[src, 2 * r + 1].astype(jnp.int32)]
                p = fill_ref[place]
                fill_ref[place] = p + count
                shift = p & (blk - 1)
                rows = (r % 2) * 4
                v = pltpu.roll(recv_ref[src, r], shift, 1)
                c = pltpu.roll(recv_ref[src, cap + r // 2], shift, 1)[rows : rows + 4]
                moved.append((place * chunks + lax.shift_right_logical(p, blk_log), lane < shift, v, c))
            for at, keep, v, c in moved:
                buf_v[at] = jnp.where(keep, buf_v[at], v)
                buf_c[at] = jnp.where(keep[0:4], buf_c[at], c)
                buf_v[at + 1] = v
                buf_c[at + 1] = c
            return carry

        lax.fori_loop(0, owners, gather, 0, unroll=4)

        def list_chunks(place, n):
            fill = fill_ref[place]
            to = lane_sums_row(place, pack, stride)

            def one(k, n):
                at_ref[n] = place * chunks + k
                live_ref[n] = fill - k * blk
                to_ref[n] = to
                return n + 1

            return lax.fori_loop(0, lax.shift_right_logical(fill + (blk - 1), blk_log), one, n)

        listed = lax.fori_loop(0, count_all, list_chunks, 0)
        for i in range(SIDES - 1):
            for ref in (at_ref, live_ref, to_ref):
                ref[listed + i] = 0

        def keep_chunks(i, n):
            place = owned - 1 - i
            fill = fill_ref[place]
            to = lane_sums_row(i, pack, stride)

            def one(k, n):
                live = lane < fill - k * blk
                kept_v[n] = jnp.where(live, buf_v[place * chunks + k], 0.0)
                kept_c[n] = jnp.where(live[0:4], buf_c[place * chunks + k], 0.0)
                kept_ref[head + n] = to
                return n + 1

            return lax.fori_loop(0, lax.shift_right_logical(fill + (blk - 1), blk_log), one, n)

        kept = lax.fori_loop(0, owned - count_all, keep_chunks, 0)
        for i in range(SIDES - 1):
            kept_v[kept + i] = jnp.zeros(shape, F32)
            kept_c[kept + i] = jnp.zeros((4, blk), F32)
            kept_ref[head + kept + i] = 0
        kept_ref[0] = kept
        kept_ref[1] = owned - count_all

    unit = rowf * step
    first = row == 0
    dims = (((1,), (1,)), ((), ()))

    def chunk(number, side):
        if inside:
            vis, coords, to = kept_v[number], kept_c[number], kept_ref[head + number]
        else:
            at, to = at_ref[number], to_ref[number]
            live = lane < live_ref[number]
            vis = jnp.where(live, buf_v[at], 0.0)
            coords = jnp.where(live[0:4], buf_c[at], 0.0)
        u, v, w = coords[0:1], coords[1:2], coords[2:3]
        far = jnp.where(
            row < 2,
            u * jnp.where(row == 0, 8 * step, half * step),
            jnp.where(row < 4, v * jnp.where(row == 2, 8 * step, half * step), w * n_corner),
        )
        cos_f, sin_f = cos_sin_turns(far)
        cos_f, sin_f = [[x[i : i + 1] for i in range(5)] for x in (cos_f, sin_f)]

        def line(t, c8, s8):
            c, s = cos_sin_turns(t * unit)
            return [c, c * c8 - s * s8], [s, s * c8 + c * s8]

        cos_a, sin_a = line(u, cos_f[0], sin_f[0])
        cos_b, sin_b = line(v, cos_f[2], sin_f[2])
        for i in range(2):
            b_ref[side, 0, 8 * i : 8 * i + 8] = cos_b[i]
            b_ref[side, 1, 8 * i : 8 * i + 8] = sin_b[i]
        b_ref[side, 0, half : half + 1] = cos_f[3]
        b_ref[side, 1, half : half + 1] = sin_f[3]
        ca16, sa16 = cos_f[1], sin_f[1]

        for j in range(8):
            both = cos_sin_turns(w * n_ref[8 + j])
            for i in range(2):
                w_ref[side, i, 1, 8 * j : 8 * j + 8] = both[i]
                w_ref[side, i, 2, 8 * j : 8 * j + 8] = both[i]
        diagonal = cos_sin_turns(w * n_ref[16])
        for j in range(8):
            for i in range(2):
                w_ref[side, i, 2, 9 * j : 9 * j + 1] = diagonal[i][j : j + 1]
        edge = [cos_sin_turns(w * n_ref[17 + i]) for i in range(2)]
        for i in range(2):
            cw, sw = edge[i]
            x16_ref[side, 0, 8 * i : 8 * i + 8] = cw * ca16 + sw * sa16
            x16_ref[side, 1, 8 * i : 8 * i + 8] = sw * ca16 - cw * sa16
        x16_ref[side, 0, half : half + 1] = cos_f[4] * ca16 + sin_f[4] * sa16
        x16_ref[side, 1, half : half + 1] = sin_f[4] * ca16 - cos_f[4] * sa16
        turned = -sign * pltpu.roll(vis, 4, 0)
        to = pl.ds(pl.multiple_of(to, 8), 8)

        def add(g, cw, sw):
            q1 = [cw[i] * cos_a[i] for i in range(2)]
            q2 = [sw[i] * cos_a[i] for i in range(2)]
            q3 = [cw[i] * sin_a[i] for i in range(2)]
            q4 = [sw[i] * sin_a[i] for i in range(2)]
            q3[0] = jnp.where(first, x16_ref[side, 1, g : g + 1], q3[0])
            q4[0] = jnp.where(first, x16_ref[side, 0, g : g + 1], q4[0])
            right = jnp.concatenate(split(jnp.concatenate(q1 + q2 + q3 + q4, 0)), 1)
            straight, across = vis * b_ref[side, 0, g : g + 1], turned * b_ref[side, 1, g : g + 1]
            left = jnp.concatenate(split(jnp.concatenate([straight + across, straight - across], 0)), 0)
            out = lax.dot_general(
                jnp.concatenate([left, left], 1), right, dims, preferred_element_type=F32
            )
            if g < half:
                sums_ref[half + g, to] += out[0:8] + out[16:24]
            if g > 0:
                sums_ref[half - g, to] += out[8:16] + out[24:32]

        add(half, [edge[i][0] for i in range(2)], [edge[i][1] for i in range(2)])
        for j in range(8):
            own, across = pl.ds(8 * j, 8), pl.ds(j, 8, stride=8)
            far_pair = cos_sin_turns(w * n_ref[j])
            pairs = []
            for i in range(2):
                w_ref[side, i, 0, 8 * j : 8 * j + 8] = far_pair[i]
                near = jnp.where(row >= j, w_ref[side, i, 1, own], w_ref[side, i, 1, across])
                pairs.append([near, far_pair[i]])
            add(j, *pairs)
        for j in range(8):
            own, across = pl.ds(8 * j, 8), pl.ds(j, 8, stride=8)
            pairs = []
            for i in range(2):
                far_one = jnp.where(row <= j, w_ref[side, i, 2, own], w_ref[side, i, 2, across])
                pairs.append([w_ref[side, i, 0, across], far_one])
            add(8 + j, *pairs)

    def some_chunks(i, carry):
        for side in range(SIDES):
            chunk(SIDES * i + side, side)
        return carry

    lax.fori_loop(0, lax.div(listed + (SIDES - 1), SIDES), some_chunks, 0)

    def transform_x(used):
        def along_x(y, carry):
            sums = [sums_ref[y, i * stride : i * stride + used] for i in range(pack)]
            high, low = split(jnp.concatenate(sums, 1))
            right = jnp.concatenate([table_ref[0, y], table_ref[0, y]], 0)
            z_ref[y, 0:used] = jnp.dot(
                jnp.concatenate([high, low], 1), right, preferred_element_type=F32
            ) + jnp.dot(high, table_ref[1, y], preferred_element_type=F32)
            return carry

        lax.fori_loop(0, sub, along_x, 0, unroll=16)

    if inside:
        few = stride // 2

        @pl.when(groups * 8 <= few)
        def _():
            transform_x(few)

        @pl.when(groups * 8 > few)
        def _():
            transform_x(stride)
    else:
        transform_x(stride)

    def times(x, k, count):
        if k == 0:
            return x
        k = k * (sub // count)
        cosine = math.cos(2 * math.pi * k / sub)
        sine = twiddle_ref[min(k, sub // 2 - k) - 1]
        turned = sine * pltpu.roll(x, 4, 0)
        return -turned if k == sub // 4 else cosine * x - turned

    top_row = tile_ref.shape[0] - sub

    def put(group):
        def one(i, ky, turn, here, corner_row):
            moved = jnp.where(here, pltpu.roll(lines_ref[ky], turn, 1), 0.0)
            tile_ref[corner_row + ky] += moved

        steps = []
        for i in range(pack):
            slot = (kept_ref if inside else order_ref)[group * pack + i + (2 if inside else 0)]
            corner_row, corner_col = offset_ref[slot, 0], offset_ref[slot, 1]
            if inside:
                corner_row = jnp.clip(corner_row - first_row, 0, top_row)
            here = (lane >= corner_col) & (lane < corner_col + sub)
            turn = (corner_col + (LANES - i * sub)) & (LANES - 1)
            steps += [functools.partial(one, i, ky, turn, here, corner_row) for ky in range(sub)]
        return steps

    def place(group, carry):
        steps = put(jnp.maximum(group - 1, 0))
        at = pl.ds(pl.multiple_of(group * 8, 8), 8)
        lines = []
        for y in range(sub):
            for step_of in steps[y * pack : (y + 1) * pack]:
                step_of()
            pair = z_ref[y, at]
            imag = pltpu.roll(pair, LANES // 2, 1)
            lines.append(pair + sign * pltpu.roll(imag, 4, 0))
        lines = fourier(lines, times)
        for ky in range(sub):
            lines_ref[ky] = lines[ky]
        return carry

    lines_ref[...] = jnp.zeros_like(lines_ref)
    lax.fori_loop(0, groups, place, 0)
    for step_of in put(jnp.maximum(groups - 1, 0)):
        step_of()

    if inside:
        out_ref[...] = tile_ref[0:keep_rows]
    else:
        for p in range(parts):
            which = lax.rem(part_ref[0] + p, parts)
            outs[p][...] = tile_ref[pl.ds(which * keep_rows, keep_rows)]


def tile_rows(offsets, part, given, table, cap, parts, base=None):
    inside = base is not None
    owned = offsets.shape[0]
    sub = table.shape[1]
    half = sub // 2
    blk = LANES
    smem = pl.BlockSpec(memory_space=pltpu.SMEM)
    vmem = pl.BlockSpec(memory_space=pltpu.VMEM)
    rows = TILE // parts
    shape = jax.ShapeDtypeStruct((rows, COMPS, TILE), F32)
    scratch, chunks = [], None
    if inside:
        operands = [*given, table, base]
        in_specs = [smem] + [vmem] * 4
        out_shape, out_specs = shape, vmem
    else:
        owners, _, _, blk = given.shape
        chunks = owners * cap + 1
        most = owners * cap + SIDES
        index = pltpu.SMEM((owned + 1,), jnp.int32)
        listing = pltpu.SMEM((most,), jnp.int32)
        operands = [given, table]
        in_specs = [vmem] * 2
        out_shape = [shape] * parts + [
            jax.ShapeDtypeStruct((owned + 3 + most,), jnp.int32),
            jax.ShapeDtypeStruct((most, 8, blk), F32),
            jax.ShapeDtypeStruct((most, 4, blk), F32),
        ]
        out_specs = [vmem] * parts + [smem, vmem, vmem]
        scratch = [
            pltpu.SMEM((owners, blk), F32),
            index,
            index,
            index,
            listing,
            listing,
            listing,
            pltpu.VMEM((owned * chunks + 1, 8, blk), F32),
            pltpu.VMEM((owned * chunks + 1, 4, blk), F32),
            pltpu.SemaphoreType.DMA,
        ]
    return pl.pallas_call(
        functools.partial(tile_kernel, inside=inside, cap=cap, sub=sub, parts=parts, chunks=chunks),
        out_shape=out_shape,
        in_specs=[smem, smem, *in_specs],
        out_specs=out_specs,
        scratch_shapes=scratch
        + [
            pltpu.VMEM((half + 3, 8, blk), F32),
            pltpu.VMEM((SIDES, 2, half + 8, blk), F32),
            pltpu.VMEM((SIDES, 2, 3, 64, blk), F32),
            pltpu.VMEM((SIDES, 2, half + 8, blk), F32),
            pltpu.VMEM((sub, owned * 8, 4 * half), F32),
            pltpu.VMEM((sub, owned * 2 * sub * 8 // LANES, LANES), F32),
            pltpu.VMEM((sub, 8, LANES), F32),
            pltpu.VMEM((rows + sub if inside else TILE, COMPS, TILE), F32),
            pltpu.VMEM((sub // 4, 8, LANES), F32),
        ],
        name="inner" if inside else "tile",
        compiler_params=pltpu.CompilerParams(vmem_limit_bytes=20 << 20),
    )(offsets, part, *operands)


def shards(
    visibility, uv_offset, w_offset, taper, row_count, block_owner, block_slot, subgrid_offset
):
    blocks_here, blk = visibility.shape[1], visibility.shape[3]
    owners = lax.axis_size("uv")
    parts = lax.axis_size("freq")
    cap = 2 * blocks_here // owners
    sent = pack(
        row_count[0],
        block_owner[0, :, 0],
        block_slot[0],
        visibility[0],
        uv_offset[0],
        w_offset[0],
        owners,
        cap,
    )
    recv = lax.all_to_all(in_vmem(sent), "uv", split_axis=0, concat_axis=0, tiled=True)
    recv = in_vmem(recv)
    table = in_vmem(tables(taper, blk))
    part = lax.axis_index("freq").astype(jnp.int32).reshape(1)
    *pieces, kept, kept_v, kept_c = tile_rows(subgrid_offset, part, recv, table, cap, parts)
    moved = [
        lax.ppermute(pieces[s], "freq", [(i, (i + s) % parts) for i in range(parts)])
        for s in range(1, parts)
    ]
    total = tile_rows(
        subgrid_offset,
        part,
        (kept, in_vmem(kept_v), in_vmem(kept_c)),
        table,
        cap,
        parts,
        in_vmem(pieces[0]),
    )
    for piece in moved:
        total = total + piece
    return total


def solution(mesh):
    placed = (
        P("freq", "uv", None, None),
        P("freq", "uv", None, None),
        P("freq", "uv", None),
        P(),
        P("freq", "uv"),
        P("freq", "uv", None),
        P("freq", "uv"),
        P("uv", None),
    )
    return jax.shard_map(
        shards, mesh=mesh, in_specs=placed, out_specs=P(("uv", "freq"), None, None), check_vma=False
    )
```

```python
import functools
import math

import jax
import jax.numpy as jnp
import numpy as np
from jax import lax
from jax.experimental import pallas as pl
from jax.experimental.pallas import tpu as pltpu
from jax.sharding import PartitionSpec as P

TILE = 128
LANES = 128
COMPS = 8
SIDES = 2
BESIDE = 10
field_width = 0.5

F32 = jnp.float32
BF16 = jnp.bfloat16


def fit_even(function, degree):
    points = np.cos(np.pi * (np.arange(400) + 0.5) / 400) * 0.125 + 0.125
    fit = np.polynomial.chebyshev.Chebyshev.fit(points, function(np.sqrt(points)), degree, domain=[0, 0.25])
    return [float(c) for c in fit.convert(kind=np.polynomial.Polynomial).coef]


SIN_COEF = fit_even(lambda f: math.sqrt(2) * np.sin(np.pi * f) / f, 3)
COS_COEF = fit_even(lambda f: math.sqrt(2) * np.cos(np.pi * f), 4)


def cos_sin_turns(turns):
    frac = turns - jnp.round(turns)
    square = frac * frac
    cos_half = COS_COEF[-1] * square + COS_COEF[-2]
    sin_half = SIN_COEF[-1] * square + SIN_COEF[-2]
    for c in COS_COEF[-3::-1]:
        cos_half = cos_half * square + c
    for c in SIN_COEF[-3::-1]:
        sin_half = sin_half * square + c
    sin_half = sin_half * frac
    return 1.0 - sin_half * sin_half, sin_half * cos_half


def split(x):
    high = x.astype(BF16)
    return high, (x - high.astype(F32)).astype(BF16)


def in_vmem(x):
    return pltpu.with_memory_space_constraint(x, pltpu.VMEM)


def iota(shape, axis):
    return lax.broadcasted_iota(jnp.int32, shape, axis)


def pack_kernel(*refs, cap):
    given, out_ref, held, used_ref, sems = refs[:6], refs[6], refs[7:13], refs[13], refs[14]
    count_ref, owner_ref, slot_ref, vis_ref, uv_ref, w_ref = held
    copies = [pltpu.make_async_copy(a, b, sems.at[i]) for i, (a, b) in enumerate(zip(given, held))]
    for copy in copies:
        copy.start()
    owners = out_ref.shape[0]
    blk = vis_ref.shape[2]
    blocks = vis_ref.shape[0]
    extra = out_ref.shape[1] - cap
    shape = (8, blk)
    row, lane = iota(shape, 0), iota(shape, 1)

    def clear(o, carry):
        used_ref[o] = 0
        for t in range(extra):
            out_ref[o, cap + t] = jnp.zeros(shape, F32)
        return carry

    lax.fori_loop(0, owners, clear, 0)
    for copy in copies:
        copy.wait()

    def place(j, carry):
        o = owner_ref[j]
        r = used_ref[o]
        used_ref[o] = r + 1
        count = count_ref[j]
        out_ref[o, r] = vis_ref[j]
        u, v, w = uv_ref[j, 0:1, :], uv_ref[j, 1:2, :], w_ref[pl.ds(j, 1), :]
        part = row % 4
        coords = jnp.where(part == 0, u, jnp.where(part == 1, v, w))
        t = cap + r // 2
        mine = (row // 4 == r % 2) & (part < 3)
        out_ref[o, t] = jnp.where(mine, coords, out_ref[o, t])
        meta = jnp.where(lane == 2 * r, count.astype(F32), slot_ref[j].astype(F32))
        here = (row == 3) & (lane // 2 == r)
        out_ref[o, cap] = jnp.where(here, meta, out_ref[o, cap])
        return carry

    lax.fori_loop(0, blocks, place, 0, unroll=4)


def pack(counts, owner, slot, vis, uv, w, owners, cap):
    extra = (cap + 1) // 2
    blk = vis.shape[2]
    operands = (counts, owner, slot, vis, uv, w)
    return pl.pallas_call(
        functools.partial(pack_kernel, cap=cap),
        out_shape=jax.ShapeDtypeStruct((owners, cap + extra, 8, blk), F32),
        in_specs=[pl.BlockSpec(memory_space=pltpu.HBM)] * 6,
        out_specs=pl.BlockSpec(memory_space=pltpu.VMEM),
        scratch_shapes=[pltpu.SMEM(x.shape, x.dtype) for x in operands[:3]]
        + [pltpu.VMEM(x.shape, x.dtype) for x in operands[3:]]
        + [pltpu.SMEM((owners,), jnp.int32), pltpu.SemaphoreType.DMA((6,))],
        name="pack",
    )(*operands)


def transform_constants(sub, blk, pack):
    half = sub // 2
    scale = 1.0 / math.sqrt(blk) / sub
    k = np.arange(sub)
    both = np.zeros((2, 4, half, sub), np.complex128)
    pick = np.zeros((2, 4, half, sub), np.float32)
    for a in range(half):
        up = np.exp(-2j * np.pi * k * (half + a) / sub) * scale
        down = np.exp(-2j * np.pi * k * (half - a) / sub) * scale
        pick[0, :, a, half + a] = 1
        pick[1, :, a, half - a if a else 0] = 1
        if a == 0:
            both[0, 0, 0], both[0, 1, 0] = up, -1j * up
            both[1, 2, 0], both[1, 3, 0] = -1j * scale, scale
        else:
            both[0, :, a] = [up, -1j * up, -1j * up, -up]
            both[1, :, a] = [down, -1j * down, 1j * down, down]
    both = both.reshape(2, 4 * half, sub)
    coef = np.zeros((2, pack, 4 * half, LANES), np.float32)
    for i in range(pack):
        for part, values in enumerate((both.real, both.imag)):
            at = (part * pack + i) * sub
            coef[:, i, :, at : at + sub] = values
    return coef, pick.reshape(2, 4 * half, sub)


def tables_kernel(taper_ref, coef_ref, pick_ref, table_ref):
    sub = taper_ref.shape[0]
    pack, rows = coef_ref.shape[1], coef_ref.shape[2]
    dims = (((1,), (1,)), ((), ()))
    plus, minus = [
        lax.dot_general(pick_ref[i], taper_ref[...], dims, precision=lax.Precision.HIGHEST)
        for i in range(2)
    ]
    for y in range(sub):
        up = jnp.broadcast_to(plus[:, y : y + 1], (rows, LANES))
        down = jnp.broadcast_to(minus[:, y : y + 1], (rows, LANES))
        for i in range(pack):
            at = pl.ds(i * rows, rows)
            table_ref[0, y, at], table_ref[1, y, at] = split(up * coef_ref[0, i] + down * coef_ref[1, i])


def tables(taper, blk):
    sub = taper.shape[0]
    pack = LANES // (2 * sub)
    coef, pick = transform_constants(sub, blk, pack)
    vmem = pl.BlockSpec(memory_space=pltpu.VMEM)
    return pl.pallas_call(
        tables_kernel,
        out_shape=jax.ShapeDtypeStruct((2, sub, LANES, LANES), BF16),
        in_specs=[vmem] * 3,
        out_specs=vmem,
        name="tables",
        compiler_params=pltpu.CompilerParams(vmem_limit_bytes=16 << 20),
    )(taper, jnp.asarray(coef), jnp.asarray(pick))


def twiddle_sines(sub):
    return [math.sin(2 * math.pi * k / sub) for k in range(1, sub // 4 + 1)]


def fourier(values, times):
    count = len(values)
    if count == 1:
        return values
    even, odd = fourier(values[0::2], times), fourier(values[1::2], times)
    odd = [times(x, k, count) for k, x in enumerate(odd)]
    return [e + o for e, o in zip(even, odd)] + [e - o for e, o in zip(even, odd)]


def lane_sums_row(place, pack, stride):
    return lax.rem(place, pack) * stride + lax.div(place, pack) * 8


def tile_kernel(*refs, inside, cap, sub, parts, chunks):
    if inside:
        offset_ref, part_ref, kept_ref, kept_v, kept_c, table_ref, base_ref, out_ref, *rest = refs
    else:
        offset_ref, part_ref, recv_ref, table_ref = refs[:4]
        outs = refs[4 : 4 + parts]
        kept_ref, kept_v, kept_c, *rest = refs[4 + parts :]
        meta_ref, order_ref, place_ref, fill_ref, at_ref, live_ref, to_ref, buf_v, buf_c, sem, *rest = rest
        owners = recv_ref.shape[0]
    (
        n_ref, b_ref, w_ref, x16_ref, sums_ref, z_ref, lines_ref, tile_ref, twiddle_ref,
    ) = rest
    owned = offset_ref.shape[0]
    blk = kept_v.shape[2]
    half = sub // 2
    pack = LANES // (2 * sub)
    stride = owned // pack * 8
    keep_rows = TILE // parts
    head = owned + 3
    shape = (8, blk)
    row, lane = iota(shape, 0), iota(shape, 1)
    blk_log = blk.bit_length() - 1
    assert half == 16 and blk == 1 << blk_log
    if not inside:
        meta_copy = pltpu.make_async_copy(recv_ref.at[:, cap, 3], meta_ref, sem)
        meta_copy.start()

    first_row = part_ref[0] * keep_rows
    if inside:
        listed, count_all = kept_ref[0], kept_ref[1]
    else:

        def clear(s, carry):
            fill_ref[s] = 0
            order_ref[s] = 0
            kept_ref[2 + s] = 0
            return carry

        lax.fori_loop(0, owned + 1, clear, 0)

        def choose(s, n):
            corner = offset_ref[s, 0]
            within = (corner >= first_row) & (corner + sub <= first_row + keep_rows)
            place_ref[s] = jnp.where(within, owned - 1 - (s - n), n)
            order_ref[n] = s
            kept_ref[2 + s - n] = s
            return n + jnp.where(within, 0, 1)

        others = lax.fori_loop(0, owned, choose, 0)

    step = field_width / sub
    rowf = row.astype(F32)

    def n_of(y, x):
        s = (x * x + y * y) * (step * step)
        return s / (1.0 + jnp.sqrt(1.0 - s))

    for j in range(8):
        n_ref[j] = n_of(float(j), rowf + 8.0)
        shifted = jnp.where(row >= j, 0.0, 8.0)
        n_ref[8 + j] = n_of(float(j) + shifted, rowf + shifted)
    n_ref[16] = n_of(rowf + 8.0, rowf + 8.0)
    n_ref[17] = n_of(float(half), rowf)
    n_ref[18] = n_of(float(half), rowf + 8.0)
    s_corner = 2.0 * half * half * step * step
    n_corner = s_corner / (1.0 + math.sqrt(1.0 - s_corner))
    sign = jnp.where(row < 4, -1.0, 1.0)
    for i, value in enumerate(twiddle_sines(sub)):
        twiddle_ref[i] = value * sign
    if inside:
        tile_ref[0:keep_rows] = base_ref[...]
        tile_ref[keep_rows:] = jnp.zeros((sub, COMPS, TILE), F32)
    else:
        tile_ref[...] = jnp.zeros_like(tile_ref)

    def clear_sums(group, carry):
        for i in range(pack):
            at = pl.ds(pl.multiple_of(i * stride + group * 8, 8), 8)
            for y in range(sub):
                sums_ref[y, at] = jnp.zeros((8, 4 * half), F32)
        return carry

    lax.fori_loop(0, lax.div(count_all + (pack - 1), pack) if inside else owned // pack, clear_sums, 0)
    if not inside:
        meta_copy.wait()

        def gather(src, carry):
            moved = []
            for r in range(cap):
                count = meta_ref[src, 2 * r].astype(jnp.int32)
                place = place_ref[meta_ref[src, 2 * r + 1].astype(jnp.int32)]
                p = fill_ref[place]
                fill_ref[place] = p + count
                shift = p & (blk - 1)
                rows = (r % 2) * 4
                v = pltpu.roll(recv_ref[src, r], shift, 1)
                c = pltpu.roll(recv_ref[src, cap + r // 2], shift, 1)[rows : rows + 4]
                moved.append((place * chunks + lax.shift_right_logical(p, blk_log), lane < shift, v, c))
            for at, keep, v, c in moved:
                buf_v[at] = jnp.where(keep, buf_v[at], v)
                buf_c[at] = jnp.where(keep[0:4], buf_c[at], c)
                buf_v[at + 1] = v
                buf_c[at + 1] = c
            return carry

        lax.fori_loop(0, owners, gather, 0, unroll=4)

        def leave(i, carry):
            left, load = carry
            used = lax.shift_right_logical(fill_ref[owned - 1 - i] + (blk - 1), blk_log)
            stays = (load < BESIDE) & (i < owned - others)
            order_ref[owned - 1 - i] = jnp.where(stays | (i >= owned - others), order_ref[owned - 1 - i], kept_ref[2 + i])
            return jnp.where(stays, i + 1, left), load + used

        left, _ = lax.fori_loop(0, owned, leave, (0, 0))
        count_all = owned - left

        def list_chunks(place, n):
            fill = fill_ref[place]
            to = lane_sums_row(place, pack, stride)

            def one(k, n):
                at_ref[n] = place * chunks + k
                live_ref[n] = fill - k * blk
                to_ref[n] = to
                return n + 1

            return lax.fori_loop(0, lax.shift_right_logical(fill + (blk - 1), blk_log), one, n)

        listed = lax.fori_loop(0, count_all, list_chunks, 0)
        for i in range(SIDES - 1):
            for ref in (at_ref, live_ref, to_ref):
                ref[listed + i] = 0

        def keep_chunks(i, n):
            place = owned - 1 - i
            fill = fill_ref[place]
            to = lane_sums_row(i, pack, stride)

            def one(k, n):
                live = lane < fill - k * blk
                kept_v[n] = jnp.where(live, buf_v[place * chunks + k], 0.0)
                kept_c[n] = jnp.where(live[0:4], buf_c[place * chunks + k], 0.0)
                kept_ref[head + n] = to
                return n + 1

            return lax.fori_loop(0, lax.shift_right_logical(fill + (blk - 1), blk_log), one, n)

        kept = lax.fori_loop(0, owned - count_all, keep_chunks, 0)
        for i in range(SIDES - 1):
            kept_v[kept + i] = jnp.zeros(shape, F32)
            kept_c[kept + i] = jnp.zeros((4, blk), F32)
            kept_ref[head + kept + i] = 0
        kept_ref[0] = kept
        kept_ref[1] = owned - count_all

    unit = rowf * step
    first = row == 0
    dims = (((1,), (1,)), ((), ()))

    def chunk(number, side):
        if inside:
            vis, coords, to = kept_v[number], kept_c[number], kept_ref[head + number]
        else:
            at, to = at_ref[number], to_ref[number]
            live = lane < live_ref[number]
            vis = jnp.where(live, buf_v[at], 0.0)
            coords = jnp.where(live[0:4], buf_c[at], 0.0)
        u, v, w = coords[0:1], coords[1:2], coords[2:3]
        far = jnp.where(
            row < 2,
            u * jnp.where(row == 0, 8 * step, half * step),
            jnp.where(row < 4, v * jnp.where(row == 2, 8 * step, half * step), w * n_corner),
        )
        cos_f, sin_f = cos_sin_turns(far)
        cos_f, sin_f = [[x[i : i + 1] for i in range(5)] for x in (cos_f, sin_f)]

        def line(t, c8, s8):
            c, s = cos_sin_turns(t * unit)
            return [c, c * c8 - s * s8], [s, s * c8 + c * s8]

        cos_a, sin_a = line(u, cos_f[0], sin_f[0])
        cos_b, sin_b = line(v, cos_f[2], sin_f[2])
        for i in range(2):
            b_ref[side, 0, 8 * i : 8 * i + 8] = cos_b[i]
            b_ref[side, 1, 8 * i : 8 * i + 8] = sin_b[i]
        b_ref[side, 0, half : half + 1] = cos_f[3]
        b_ref[side, 1, half : half + 1] = sin_f[3]
        ca16, sa16 = cos_f[1], sin_f[1]

        for j in range(8):
            both = cos_sin_turns(w * n_ref[8 + j])
            for i in range(2):
                w_ref[side, i, 1, 8 * j : 8 * j + 8] = both[i]
                w_ref[side, i, 2, 8 * j : 8 * j + 8] = both[i]
        diagonal = cos_sin_turns(w * n_ref[16])
        for j in range(8):
            for i in range(2):
                w_ref[side, i, 2, 9 * j : 9 * j + 1] = diagonal[i][j : j + 1]
        edge = [cos_sin_turns(w * n_ref[17 + i]) for i in range(2)]
        for i in range(2):
            cw, sw = edge[i]
            x16_ref[side, 0, 8 * i : 8 * i + 8] = cw * ca16 + sw * sa16
            x16_ref[side, 1, 8 * i : 8 * i + 8] = sw * ca16 - cw * sa16
        x16_ref[side, 0, half : half + 1] = cos_f[4] * ca16 + sin_f[4] * sa16
        x16_ref[side, 1, half : half + 1] = sin_f[4] * ca16 - cos_f[4] * sa16
        turned = -sign * pltpu.roll(vis, 4, 0)
        to = pl.ds(pl.multiple_of(to, 8), 8)

        def add(g, cw, sw):
            q1 = [cw[i] * cos_a[i] for i in range(2)]
            q2 = [sw[i] * cos_a[i] for i in range(2)]
            q3 = [cw[i] * sin_a[i] for i in range(2)]
            q4 = [sw[i] * sin_a[i] for i in range(2)]
            q3[0] = jnp.where(first, x16_ref[side, 1, g : g + 1], q3[0])
            q4[0] = jnp.where(first, x16_ref[side, 0, g : g + 1], q4[0])
            right = jnp.concatenate(split(jnp.concatenate(q1 + q2 + q3 + q4, 0)), 1)
            straight, across = vis * b_ref[side, 0, g : g + 1], turned * b_ref[side, 1, g : g + 1]
            left = jnp.concatenate(split(jnp.concatenate([straight + across, straight - across], 0)), 0)
            out = lax.dot_general(
                jnp.concatenate([left, left], 1), right, dims, preferred_element_type=F32
            )
            if g < half:
                sums_ref[half + g, to] += out[0:8] + out[16:24]
            if g > 0:
                sums_ref[half - g, to] += out[8:16] + out[24:32]

        add(half, [edge[i][0] for i in range(2)], [edge[i][1] for i in range(2)])
        for j in range(8):
            own, across = pl.ds(8 * j, 8), pl.ds(j, 8, stride=8)
            far_pair = cos_sin_turns(w * n_ref[j])
            pairs = []
            for i in range(2):
                w_ref[side, i, 0, 8 * j : 8 * j + 8] = far_pair[i]
                near = jnp.where(row >= j, w_ref[side, i, 1, own], w_ref[side, i, 1, across])
                pairs.append([near, far_pair[i]])
            add(j, *pairs)
        for j in range(8):
            own, across = pl.ds(8 * j, 8), pl.ds(j, 8, stride=8)
            pairs = []
            for i in range(2):
                far_one = jnp.where(row <= j, w_ref[side, i, 2, own], w_ref[side, i, 2, across])
                pairs.append([w_ref[side, i, 0, across], far_one])
            add(8 + j, *pairs)

    def some_chunks(i, carry):
        for side in range(SIDES):
            chunk(SIDES * i + side, side)
        return carry

    lax.fori_loop(0, lax.div(listed + (SIDES - 1), SIDES), some_chunks, 0)

    def transform_x(used):
        def along_x(y, carry):
            sums = [sums_ref[y, i * stride : i * stride + used] for i in range(pack)]
            high, low = split(jnp.concatenate(sums, 1))
            right = jnp.concatenate([table_ref[0, y], table_ref[0, y]], 0)
            z_ref[y, 0:used] = jnp.dot(
                jnp.concatenate([high, low], 1), right, preferred_element_type=F32
            ) + jnp.dot(high, table_ref[1, y], preferred_element_type=F32)
            return carry

        lax.fori_loop(0, sub, along_x, 0, unroll=16)

    groups = lax.div(count_all + (pack - 1), pack)
    if inside:
        few = stride // 2

        @pl.when(groups * 8 <= few)
        def _():
            transform_x(few)

        @pl.when(groups * 8 > few)
        def _():
            transform_x(stride)
    else:
        transform_x(stride)

    def times(x, k, count):
        if k == 0:
            return x
        k = k * (sub // count)
        cosine = math.cos(2 * math.pi * k / sub)
        sine = twiddle_ref[min(k, sub // 2 - k) - 1]
        turned = sine * pltpu.roll(x, 4, 0)
        return -turned if k == sub // 4 else cosine * x - turned

    top_row = tile_ref.shape[0] - sub

    def put(group):
        def one(i, ky, turn, here, corner_row):
            moved = jnp.where(here, pltpu.roll(lines_ref[ky], turn, 1), 0.0)
            tile_ref[corner_row + ky] += moved

        steps = []
        for i in range(pack):
            slot = (kept_ref if inside else order_ref)[group * pack + i + (2 if inside else 0)]
            corner_row, corner_col = offset_ref[slot, 0], offset_ref[slot, 1]
            if inside:
                corner_row = jnp.clip(corner_row - first_row, 0, top_row)
            here = (lane >= corner_col) & (lane < corner_col + sub)
            turn = (corner_col + (LANES - i * sub)) & (LANES - 1)
            steps += [functools.partial(one, i, ky, turn, here, corner_row) for ky in range(sub)]
        return steps

    def place(group, carry):
        steps = put(jnp.maximum(group - 1, 0))
        at = pl.ds(pl.multiple_of(group * 8, 8), 8)
        lines = []
        for y in range(sub):
            for step_of in steps[y * pack : (y + 1) * pack]:
                step_of()
            pair = z_ref[y, at]
            imag = pltpu.roll(pair, LANES // 2, 1)
            lines.append(pair + sign * pltpu.roll(imag, 4, 0))
        lines = fourier(lines, times)
        for ky in range(sub):
            lines_ref[ky] = lines[ky]
        return carry

    lines_ref[...] = jnp.zeros_like(lines_ref)
    lax.fori_loop(0, groups, place, 0)
    for step_of in put(jnp.maximum(groups - 1, 0)):
        step_of()

    if inside:
        out_ref[...] = tile_ref[0:keep_rows]
    else:
        for p in range(parts):
            which = lax.rem(part_ref[0] + p, parts)
            outs[p][...] = tile_ref[pl.ds(which * keep_rows, keep_rows)]


def tile_rows(offsets, part, given, table, cap, parts, base=None):
    inside = base is not None
    owned = offsets.shape[0]
    sub = table.shape[1]
    half = sub // 2
    blk = LANES
    smem = pl.BlockSpec(memory_space=pltpu.SMEM)
    vmem = pl.BlockSpec(memory_space=pltpu.VMEM)
    rows = TILE // parts
    shape = jax.ShapeDtypeStruct((rows, COMPS, TILE), F32)
    scratch, chunks = [], None
    if inside:
        operands = [*given, table, base]
        in_specs = [smem] + [vmem] * 4
        out_shape, out_specs = shape, vmem
    else:
        owners, _, _, blk = given.shape
        chunks = owners * cap + 1
        most = owners * cap + SIDES
        index = pltpu.SMEM((owned + 1,), jnp.int32)
        listing = pltpu.SMEM((most,), jnp.int32)
        operands = [given, table]
        in_specs = [vmem] * 2
        out_shape = [shape] * parts + [
            jax.ShapeDtypeStruct((owned + 3 + most,), jnp.int32),
            jax.ShapeDtypeStruct((most, 8, blk), F32),
            jax.ShapeDtypeStruct((most, 4, blk), F32),
        ]
        out_specs = [vmem] * parts + [smem, vmem, vmem]
        scratch = [
            pltpu.SMEM((owners, blk), F32),
            index,
            index,
            index,
            listing,
            listing,
            listing,
            pltpu.VMEM((owned * chunks + 1, 8, blk), F32),
            pltpu.VMEM((owned * chunks + 1, 4, blk), F32),
            pltpu.SemaphoreType.DMA,
        ]
    return pl.pallas_call(
        functools.partial(tile_kernel, inside=inside, cap=cap, sub=sub, parts=parts, chunks=chunks),
        out_shape=out_shape,
        in_specs=[smem, smem, *in_specs],
        out_specs=out_specs,
        scratch_shapes=scratch
        + [
            pltpu.VMEM((half + 3, 8, blk), F32),
            pltpu.VMEM((SIDES, 2, half + 8, blk), F32),
            pltpu.VMEM((SIDES, 2, 3, 64, blk), F32),
            pltpu.VMEM((SIDES, 2, half + 8, blk), F32),
            pltpu.VMEM((sub, owned * 8, 4 * half), F32),
            pltpu.VMEM((sub, owned * 2 * sub * 8 // LANES, LANES), F32),
            pltpu.VMEM((sub, 8, LANES), F32),
            pltpu.VMEM((rows + sub if inside else TILE, COMPS, TILE), F32),
            pltpu.VMEM((sub // 4, 8, LANES), F32),
        ],
        name="inner" if inside else "tile",
        compiler_params=pltpu.CompilerParams(vmem_limit_bytes=20 << 20),
    )(offsets, part, *operands)


def shards(
    visibility, uv_offset, w_offset, taper, row_count, block_owner, block_slot, subgrid_offset
):
    blocks_here, blk = visibility.shape[1], visibility.shape[3]
    owners = lax.axis_size("uv")
    parts = lax.axis_size("freq")
    cap = 2 * blocks_here // owners
    sent = pack(
        row_count[0],
        block_owner[0, :, 0],
        block_slot[0],
        visibility[0],
        uv_offset[0],
        w_offset[0],
        owners,
        cap,
    )
    recv = lax.all_to_all(in_vmem(sent), "uv", split_axis=0, concat_axis=0, tiled=True)
    recv = in_vmem(recv)
    table = in_vmem(tables(taper, blk))
    part = lax.axis_index("freq").astype(jnp.int32).reshape(1)
    *pieces, kept, kept_v, kept_c = tile_rows(subgrid_offset, part, recv, table, cap, parts)
    moved = [
        lax.ppermute(pieces[s], "freq", [(i, (i + s) % parts) for i in range(parts)])
        for s in range(1, parts)
    ]
    total = tile_rows(
        subgrid_offset,
        part,
        (kept, in_vmem(kept_v), in_vmem(kept_c)),
        table,
        cap,
        parts,
        in_vmem(pieces[0]),
    )
    for piece in moved:
        total = total + piece
    return total


def solution(mesh):
    placed = (
        P("freq", "uv", None, None),
        P("freq", "uv", None, None),
        P("freq", "uv", None),
        P(),
        P("freq", "uv"),
        P("freq", "uv", None),
        P("freq", "uv"),
        P("uv", None),
    )
    return jax.shard_map(
        shards, mesh=mesh, in_specs=placed, out_specs=P(("uv", "freq"), None, None), check_vma=False
    )
```

```python
import functools
import math

import jax
import jax.numpy as jnp
import numpy as np
from jax import lax
from jax.experimental import pallas as pl
from jax.experimental.pallas import tpu as pltpu
from jax.sharding import PartitionSpec as P

TILE = 128
LANES = 128
COMPS = 8
SIDES = 2
BESIDE = 10
field_width = 0.5

F32 = jnp.float32
BF16 = jnp.bfloat16


def fit_even(function, degree):
    points = np.cos(np.pi * (np.arange(400) + 0.5) / 400) * 0.125 + 0.125
    fit = np.polynomial.chebyshev.Chebyshev.fit(points, function(np.sqrt(points)), degree, domain=[0, 0.25])
    return [float(c) for c in fit.convert(kind=np.polynomial.Polynomial).coef]


SIN_COEF = fit_even(lambda f: math.sqrt(2) * np.sin(np.pi * f) / f, 3)
COS_COEF = fit_even(lambda f: math.sqrt(2) * np.cos(np.pi * f), 4)


def cos_sin_turns(turns):
    frac = turns - jnp.round(turns)
    square = frac * frac
    cos_half = COS_COEF[-1] * square + COS_COEF[-2]
    sin_half = SIN_COEF[-1] * square + SIN_COEF[-2]
    for c in COS_COEF[-3::-1]:
        cos_half = cos_half * square + c
    for c in SIN_COEF[-3::-1]:
        sin_half = sin_half * square + c
    sin_half = sin_half * frac
    return 1.0 - sin_half * sin_half, sin_half * cos_half


def split(x):
    high = x.astype(BF16)
    return high, (x - high.astype(F32)).astype(BF16)


def in_vmem(x):
    return pltpu.with_memory_space_constraint(x, pltpu.VMEM)


def iota(shape, axis):
    return lax.broadcasted_iota(jnp.int32, shape, axis)


def pack_kernel(*refs, cap):
    given, out_ref, held, used_ref, sems = refs[:6], refs[6], refs[7:13], refs[13], refs[14]
    count_ref, owner_ref, slot_ref, vis_ref, uv_ref, w_ref = held
    copies = [pltpu.make_async_copy(a, b, sems.at[i]) for i, (a, b) in enumerate(zip(given, held))]
    for copy in copies:
        copy.start()
    owners = out_ref.shape[0]
    blk = vis_ref.shape[2]
    blocks = vis_ref.shape[0]
    extra = out_ref.shape[1] - cap
    shape = (8, blk)
    row, lane = iota(shape, 0), iota(shape, 1)

    def clear(o, carry):
        used_ref[o] = 0
        for t in range(extra):
            out_ref[o, cap + t] = jnp.zeros(shape, F32)
        return carry

    lax.fori_loop(0, owners, clear, 0)
    for copy in copies:
        copy.wait()

    def place(j, carry):
        o = owner_ref[j]
        r = used_ref[o]
        used_ref[o] = r + 1
        count = count_ref[j]
        out_ref[o, r] = vis_ref[j]
        u, v, w = uv_ref[j, 0:1, :], uv_ref[j, 1:2, :], w_ref[pl.ds(j, 1), :]
        part = row % 4
        coords = jnp.where(part == 0, u, jnp.where(part == 1, v, w))
        t = cap + r // 2
        mine = (row // 4 == r % 2) & (part < 3)
        out_ref[o, t] = jnp.where(mine, coords, out_ref[o, t])
        meta = jnp.where(lane == 2 * r, count.astype(F32), slot_ref[j].astype(F32))
        here = (row == 3) & (lane // 2 == r)
        out_ref[o, cap] = jnp.where(here, meta, out_ref[o, cap])
        return carry

    lax.fori_loop(0, blocks, place, 0, unroll=4)


def pack(counts, owner, slot, vis, uv, w, owners, cap):
    extra = (cap + 1) // 2
    blk = vis.shape[2]
    operands = (counts, owner, slot, vis, uv, w)
    return pl.pallas_call(
        functools.partial(pack_kernel, cap=cap),
        out_shape=jax.ShapeDtypeStruct((owners, cap + extra, 8, blk), F32),
        in_specs=[pl.BlockSpec(memory_space=pltpu.HBM)] * 6,
        out_specs=pl.BlockSpec(memory_space=pltpu.VMEM),
        scratch_shapes=[pltpu.SMEM(x.shape, x.dtype) for x in operands[:3]]
        + [pltpu.VMEM(x.shape, x.dtype) for x in operands[3:]]
        + [pltpu.SMEM((owners,), jnp.int32), pltpu.SemaphoreType.DMA((6,))],
        name="pack",
    )(*operands)


def transform_constants(sub, blk, pack):
    half = sub // 2
    scale = 1.0 / math.sqrt(blk) / sub
    k = np.arange(sub)
    both = np.zeros((2, 4, half, sub), np.complex128)
    pick = np.zeros((2, 4, half, sub), np.float32)
    for a in range(half):
        up = np.exp(-2j * np.pi * k * (half + a) / sub) * scale
        down = np.exp(-2j * np.pi * k * (half - a) / sub) * scale
        pick[0, :, a, half + a] = 1
        pick[1, :, a, half - a if a else 0] = 1
        if a == 0:
            both[0, 0, 0], both[0, 1, 0] = up, -1j * up
            both[1, 2, 0], both[1, 3, 0] = -1j * scale, scale
        else:
            both[0, :, a] = [up, -1j * up, -1j * up, -up]
            both[1, :, a] = [down, -1j * down, 1j * down, down]
    both = both.reshape(2, 4 * half, sub)
    coef = np.zeros((2, pack, 4 * half, LANES), np.float32)
    for i in range(pack):
        for part, values in enumerate((both.real, both.imag)):
            at = (part * pack + i) * sub
            coef[:, i, :, at : at + sub] = values
    return coef, pick.reshape(2, 4 * half, sub)


def tables_kernel(taper_ref, coef_ref, pick_ref, table_ref):
    sub = taper_ref.shape[0]
    pack, rows = coef_ref.shape[1], coef_ref.shape[2]
    dims = (((1,), (1,)), ((), ()))
    plus, minus = [
        lax.dot_general(pick_ref[i], taper_ref[...], dims, precision=lax.Precision.HIGHEST)
        for i in range(2)
    ]
    for y in range(sub):
        up = jnp.broadcast_to(plus[:, y : y + 1], (rows, LANES))
        down = jnp.broadcast_to(minus[:, y : y + 1], (rows, LANES))
        for i in range(pack):
            at = pl.ds(i * rows, rows)
            table_ref[0, y, at], table_ref[1, y, at] = split(up * coef_ref[0, i] + down * coef_ref[1, i])


def tables(taper, blk):
    sub = taper.shape[0]
    pack = LANES // (2 * sub)
    coef, pick = transform_constants(sub, blk, pack)
    vmem = pl.BlockSpec(memory_space=pltpu.VMEM)
    return pl.pallas_call(
        tables_kernel,
        out_shape=jax.ShapeDtypeStruct((2, sub, LANES, LANES), BF16),
        in_specs=[vmem] * 3,
        out_specs=vmem,
        name="tables",
        compiler_params=pltpu.CompilerParams(vmem_limit_bytes=16 << 20),
    )(taper, jnp.asarray(coef), jnp.asarray(pick))


def twiddle_sines(sub):
    return [math.sin(2 * math.pi * k / sub) for k in range(1, sub // 4 + 1)]


def fourier(values, times):
    count = len(values)
    if count == 1:
        return values
    even, odd = fourier(values[0::2], times), fourier(values[1::2], times)
    odd = [times(x, k, count) for k, x in enumerate(odd)]
    return [e + o for e, o in zip(even, odd)] + [e - o for e, o in zip(even, odd)]


def lane_sums_row(place, pack, stride):
    return lax.rem(place, pack) * stride + lax.div(place, pack) * 8


def tile_kernel(*refs, inside, cap, sub, parts, chunks):
    if inside:
        offset_ref, part_ref, kept_ref, kept_v, kept_c, table_ref, base_ref, out_ref, *rest = refs
    else:
        offset_ref, part_ref, recv_ref, table_ref = refs[:4]
        outs = refs[4 : 4 + parts]
        kept_ref, kept_v, kept_c, *rest = refs[4 + parts :]
        meta_ref, order_ref, place_ref, fill_ref, at_ref, live_ref, to_ref, buf_v, buf_c, sem, *rest = rest
        owners = recv_ref.shape[0]
    (
        n_ref, b_ref, w_ref, x16_ref, sums_ref, z_ref, lines_ref, tile_ref, twiddle_ref,
    ) = rest
    owned = offset_ref.shape[0]
    blk = kept_v.shape[2]
    half = sub // 2
    pack = LANES // (2 * sub)
    stride = owned // pack * 8
    keep_rows = TILE // parts
    head = owned + 3
    shape = (8, blk)
    row, lane = iota(shape, 0), iota(shape, 1)
    blk_log = blk.bit_length() - 1
    assert half == 16 and blk == 1 << blk_log
    if not inside:
        meta_copy = pltpu.make_async_copy(recv_ref.at[:, cap, 3], meta_ref, sem)
        meta_copy.start()

    first_row = part_ref[0] * keep_rows
    if inside:
        listed, count_all = kept_ref[0], kept_ref[1]
    else:

        def clear(s, carry):
            fill_ref[s] = 0
            order_ref[s] = 0
            kept_ref[2 + s] = 0
            return carry

        lax.fori_loop(0, owned + 1, clear, 0, unroll=True)

        def choose(s, n):
            corner = offset_ref[s, 0]
            within = (corner >= first_row) & (corner + sub <= first_row + keep_rows)
            place_ref[s] = jnp.where(within, owned - 1 - (s - n), n)
            order_ref[n] = s
            kept_ref[2 + s - n] = s
            return n + jnp.where(within, 0, 1)

        others = lax.fori_loop(0, owned, choose, 0, unroll=True)

    step = field_width / sub
    rowf = row.astype(F32)

    def n_of(y, x):
        s = (x * x + y * y) * (step * step)
        return s / (1.0 + jnp.sqrt(1.0 - s))

    for j in range(8):
        n_ref[j] = n_of(float(j), rowf + 8.0)
        shifted = jnp.where(row >= j, 0.0, 8.0)
        n_ref[8 + j] = n_of(float(j) + shifted, rowf + shifted)
    n_ref[16] = n_of(rowf + 8.0, rowf + 8.0)
    n_ref[17] = n_of(float(half), rowf)
    n_ref[18] = n_of(float(half), rowf + 8.0)
    s_corner = 2.0 * half * half * step * step
    n_corner = s_corner / (1.0 + math.sqrt(1.0 - s_corner))
    sign = jnp.where(row < 4, -1.0, 1.0)
    for i, value in enumerate(twiddle_sines(sub)):
        twiddle_ref[i] = value * sign
    if inside:
        tile_ref[0:keep_rows] = base_ref[...]
        tile_ref[keep_rows:] = jnp.zeros((sub, COMPS, TILE), F32)
    else:
        tile_ref[...] = jnp.zeros_like(tile_ref)

    def clear_sums(group, carry):
        for i in range(pack):
            at = pl.ds(pl.multiple_of(i * stride + group * 8, 8), 8)
            for y in range(sub):
                sums_ref[y, at] = jnp.zeros((8, 4 * half), F32)
        return carry

    lax.fori_loop(0, lax.div(count_all + (pack - 1), pack) if inside else owned // pack, clear_sums, 0)
    if not inside:
        meta_copy.wait()

        def gather(src, carry):
            moved = []
            for r in range(cap):
                count = meta_ref[src, 2 * r].astype(jnp.int32)
                place = place_ref[meta_ref[src, 2 * r + 1].astype(jnp.int32)]
                p = fill_ref[place]
                fill_ref[place] = p + count
                shift = p & (blk - 1)
                rows = (r % 2) * 4
                v = pltpu.roll(recv_ref[src, r], shift, 1)
                c = pltpu.roll(recv_ref[src, cap + r // 2], shift, 1)[rows : rows + 4]
                moved.append((place * chunks + lax.shift_right_logical(p, blk_log), lane < shift, v, c))
            for at, keep, v, c in moved:
                buf_v[at] = jnp.where(keep, buf_v[at], v)
                buf_c[at] = jnp.where(keep[0:4], buf_c[at], c)
                buf_v[at + 1] = v
                buf_c[at + 1] = c
            return carry

        lax.fori_loop(0, owners, gather, 0, unroll=8)

        def leave(i, carry):
            left, load = carry
            used = lax.shift_right_logical(fill_ref[owned - 1 - i] + (blk - 1), blk_log)
            stays = (load < BESIDE) & (i < owned - others)
            order_ref[owned - 1 - i] = jnp.where(stays | (i >= owned - others), order_ref[owned - 1 - i], kept_ref[2 + i])
            return jnp.where(stays, i + 1, left), load + used

        left, _ = lax.fori_loop(0, owned, leave, (0, 0), unroll=True)
        count_all = owned - left

        def list_chunks(place, n):
            fill = fill_ref[place]
            to = lane_sums_row(place, pack, stride)

            def one(k, n):
                at_ref[n] = place * chunks + k
                live_ref[n] = fill - k * blk
                to_ref[n] = to
                return n + 1

            return lax.fori_loop(0, lax.shift_right_logical(fill + (blk - 1), blk_log), one, n)

        listed = lax.fori_loop(0, count_all, list_chunks, 0)
        for i in range(SIDES - 1):
            for ref in (at_ref, live_ref, to_ref):
                ref[listed + i] = 0

        def keep_chunks(i, n):
            place = owned - 1 - i
            fill = fill_ref[place]
            to = lane_sums_row(i, pack, stride)

            def one(k, n):
                live = lane < fill - k * blk
                kept_v[n] = jnp.where(live, buf_v[place * chunks + k], 0.0)
                kept_c[n] = jnp.where(live[0:4], buf_c[place * chunks + k], 0.0)
                kept_ref[head + n] = to
                return n + 1

            return lax.fori_loop(0, lax.shift_right_logical(fill + (blk - 1), blk_log), one, n)

        kept = lax.fori_loop(0, owned - count_all, keep_chunks, 0)
        for i in range(SIDES - 1):
            kept_v[kept + i] = jnp.zeros(shape, F32)
            kept_c[kept + i] = jnp.zeros((4, blk), F32)
            kept_ref[head + kept + i] = 0
        kept_ref[0] = kept
        kept_ref[1] = owned - count_all

    unit = rowf * step
    first = row == 0
    dims = (((1,), (1,)), ((), ()))

    def chunk(number, side):
        if inside:
            vis, coords, to = kept_v[number], kept_c[number], kept_ref[head + number]
        else:
            at, to = at_ref[number], to_ref[number]
            live = lane < live_ref[number]
            vis = jnp.where(live, buf_v[at], 0.0)
            coords = jnp.where(live[0:4], buf_c[at], 0.0)
        u, v, w = coords[0:1], coords[1:2], coords[2:3]
        far = jnp.where(
            row < 2,
            u * jnp.where(row == 0, 8 * step, half * step),
            jnp.where(row < 4, v * jnp.where(row == 2, 8 * step, half * step), w * n_corner),
        )
        cos_f, sin_f = cos_sin_turns(far)
        cos_f, sin_f = [[x[i : i + 1] for i in range(5)] for x in (cos_f, sin_f)]

        def line(t, c8, s8):
            c, s = cos_sin_turns(t * unit)
            return [c, c * c8 - s * s8], [s, s * c8 + c * s8]

        cos_a, sin_a = line(u, cos_f[0], sin_f[0])
        cos_b, sin_b = line(v, cos_f[2], sin_f[2])
        for i in range(2):
            b_ref[side, 0, 8 * i : 8 * i + 8] = cos_b[i]
            b_ref[side, 1, 8 * i : 8 * i + 8] = sin_b[i]
        b_ref[side, 0, half : half + 1] = cos_f[3]
        b_ref[side, 1, half : half + 1] = sin_f[3]
        ca16, sa16 = cos_f[1], sin_f[1]

        for j in range(8):
            both = cos_sin_turns(w * n_ref[8 + j])
            for i in range(2):
                w_ref[side, i, 1, 8 * j : 8 * j + 8] = both[i]
                w_ref[side, i, 2, 8 * j : 8 * j + 8] = both[i]
        diagonal = cos_sin_turns(w * n_ref[16])
        for j in range(8):
            for i in range(2):
                w_ref[side, i, 2, 9 * j : 9 * j + 1] = diagonal[i][j : j + 1]
        edge = [cos_sin_turns(w * n_ref[17 + i]) for i in range(2)]
        for i in range(2):
            cw, sw = edge[i]
            x16_ref[side, 0, 8 * i : 8 * i + 8] = cw * ca16 + sw * sa16
            x16_ref[side, 1, 8 * i : 8 * i + 8] = sw * ca16 - cw * sa16
        x16_ref[side, 0, half : half + 1] = cos_f[4] * ca16 + sin_f[4] * sa16
        x16_ref[side, 1, half : half + 1] = sin_f[4] * ca16 - cos_f[4] * sa16
        turned = -sign * pltpu.roll(vis, 4, 0)
        to = pl.ds(pl.multiple_of(to, 8), 8)

        def add(g, cw, sw):
            q1 = [cw[i] * cos_a[i] for i in range(2)]
            q2 = [sw[i] * cos_a[i] for i in range(2)]
            q3 = [cw[i] * sin_a[i] for i in range(2)]
            q4 = [sw[i] * sin_a[i] for i in range(2)]
            q3[0] = jnp.where(first, x16_ref[side, 1, g : g + 1], q3[0])
            q4[0] = jnp.where(first, x16_ref[side, 0, g : g + 1], q4[0])
            right = jnp.concatenate(split(jnp.concatenate(q1 + q2 + q3 + q4, 0)), 1)
            straight, across = vis * b_ref[side, 0, g : g + 1], turned * b_ref[side, 1, g : g + 1]
            left = jnp.concatenate(split(jnp.concatenate([straight + across, straight - across], 0)), 0)
            out = lax.dot_general(
                jnp.concatenate([left, left], 1), right, dims, preferred_element_type=F32
            )
            if g < half:
                sums_ref[half + g, to] += out[0:8] + out[16:24]
            if g > 0:
                sums_ref[half - g, to] += out[8:16] + out[24:32]

        add(half, [edge[i][0] for i in range(2)], [edge[i][1] for i in range(2)])
        for j in range(8):
            own, across = pl.ds(8 * j, 8), pl.ds(j, 8, stride=8)
            far_pair = cos_sin_turns(w * n_ref[j])
            pairs = []
            for i in range(2):
                w_ref[side, i, 0, 8 * j : 8 * j + 8] = far_pair[i]
                near = jnp.where(row >= j, w_ref[side, i, 1, own], w_ref[side, i, 1, across])
                pairs.append([near, far_pair[i]])
            add(j, *pairs)
        for j in range(8):
            own, across = pl.ds(8 * j, 8), pl.ds(j, 8, stride=8)
            pairs = []
            for i in range(2):
                far_one = jnp.where(row <= j, w_ref[side, i, 2, own], w_ref[side, i, 2, across])
                pairs.append([w_ref[side, i, 0, across], far_one])
            add(8 + j, *pairs)

    def some_chunks(i, carry):
        for side in range(SIDES):
            chunk(SIDES * i + side, side)
        return carry

    lax.fori_loop(0, lax.div(listed + (SIDES - 1), SIDES), some_chunks, 0)

    def transform_x(used):
        def along_x(y, carry):
            sums = [sums_ref[y, i * stride : i * stride + used] for i in range(pack)]
            high, low = split(jnp.concatenate(sums, 1))
            right = jnp.concatenate([table_ref[0, y], table_ref[0, y]], 0)
            z_ref[y, 0:used] = jnp.dot(
                jnp.concatenate([high, low], 1), right, preferred_element_type=F32
            ) + jnp.dot(high, table_ref[1, y], preferred_element_type=F32)
            return carry

        lax.fori_loop(0, sub, along_x, 0, unroll=True)

    groups = lax.div(count_all + (pack - 1), pack)
    if inside:
        few = stride // 2

        @pl.when(groups * 8 <= few)
        def _():
            transform_x(few)

        @pl.when(groups * 8 > few)
        def _():
            transform_x(stride)
    else:
        transform_x(stride)

    def times(x, k, count):
        if k == 0:
            return x
        k = k * (sub // count)
        cosine = math.cos(2 * math.pi * k / sub)
        sine = twiddle_ref[min(k, sub // 2 - k) - 1]
        turned = sine * pltpu.roll(x, 4, 0)
        return -turned if k == sub // 4 else cosine * x - turned

    top_row = tile_ref.shape[0] - sub

    def put(group):
        def one(i, ky, turn, here, corner_row):
            moved = jnp.where(here, pltpu.roll(lines_ref[ky], turn, 1), 0.0)
            tile_ref[corner_row + ky] += moved

        steps = []
        for i in range(pack):
            slot = (kept_ref if inside else order_ref)[group * pack + i + (2 if inside else 0)]
            corner_row, corner_col = offset_ref[slot, 0], offset_ref[slot, 1]
            if inside:
                corner_row = jnp.clip(corner_row - first_row, 0, top_row)
            here = (lane >= corner_col) & (lane < corner_col + sub)
            turn = (corner_col + (LANES - i * sub)) & (LANES - 1)
            steps += [functools.partial(one, i, ky, turn, here, corner_row) for ky in range(sub)]
        return steps

    def place(group, carry):
        steps = put(jnp.maximum(group - 1, 0))
        at = pl.ds(pl.multiple_of(group * 8, 8), 8)
        lines = []
        for y in range(sub):
            for step_of in steps[y * pack : (y + 1) * pack]:
                step_of()
            pair = z_ref[y, at]
            imag = pltpu.roll(pair, LANES // 2, 1)
            lines.append(pair + sign * pltpu.roll(imag, 4, 0))
        lines = fourier(lines, times)
        for ky in range(sub):
            lines_ref[ky] = lines[ky]
        return carry

    lines_ref[...] = jnp.zeros_like(lines_ref)
    lax.fori_loop(0, groups, place, 0)
    for step_of in put(jnp.maximum(groups - 1, 0)):
        step_of()

    if inside:
        out_ref[...] = tile_ref[0:keep_rows]
    else:
        for p in range(parts):
            which = lax.rem(part_ref[0] + p, parts)
            outs[p][...] = tile_ref[pl.ds(which * keep_rows, keep_rows)]


def tile_rows(offsets, part, given, table, cap, parts, base=None):
    inside = base is not None
    owned = offsets.shape[0]
    sub = table.shape[1]
    half = sub // 2
    blk = LANES
    smem = pl.BlockSpec(memory_space=pltpu.SMEM)
    vmem = pl.BlockSpec(memory_space=pltpu.VMEM)
    rows = TILE // parts
    shape = jax.ShapeDtypeStruct((rows, COMPS, TILE), F32)
    scratch, chunks = [], None
    if inside:
        operands = [*given, table, base]
        in_specs = [smem] + [vmem] * 4
        out_shape, out_specs = shape, vmem
    else:
        owners, _, _, blk = given.shape
        chunks = owners * cap + 1
        most = owners * cap + SIDES
        index = pltpu.SMEM((owned + 1,), jnp.int32)
        listing = pltpu.SMEM((most,), jnp.int32)
        operands = [given, table]
        in_specs = [vmem] * 2
        out_shape = [shape] * parts + [
            jax.ShapeDtypeStruct((owned + 3 + most,), jnp.int32),
            jax.ShapeDtypeStruct((most, 8, blk), F32),
            jax.ShapeDtypeStruct((most, 4, blk), F32),
        ]
        out_specs = [vmem] * parts + [smem, vmem, vmem]
        scratch = [
            pltpu.SMEM((owners, blk), F32),
            index,
            index,
            index,
            listing,
            listing,
            listing,
            pltpu.VMEM((owned * chunks + 1, 8, blk), F32),
            pltpu.VMEM((owned * chunks + 1, 4, blk), F32),
            pltpu.SemaphoreType.DMA,
        ]
    return pl.pallas_call(
        functools.partial(tile_kernel, inside=inside, cap=cap, sub=sub, parts=parts, chunks=chunks),
        out_shape=out_shape,
        in_specs=[smem, smem, *in_specs],
        out_specs=out_specs,
        scratch_shapes=scratch
        + [
            pltpu.VMEM((half + 3, 8, blk), F32),
            pltpu.VMEM((SIDES, 2, half + 8, blk), F32),
            pltpu.VMEM((SIDES, 2, 3, 64, blk), F32),
            pltpu.VMEM((SIDES, 2, half + 8, blk), F32),
            pltpu.VMEM((sub, owned * 8, 4 * half), F32),
            pltpu.VMEM((sub, owned * 2 * sub * 8 // LANES, LANES), F32),
            pltpu.VMEM((sub, 8, LANES), F32),
            pltpu.VMEM((rows + sub if inside else TILE, COMPS, TILE), F32),
            pltpu.VMEM((sub // 4, 8, LANES), F32),
        ],
        name="inner" if inside else "tile",
        compiler_params=pltpu.CompilerParams(vmem_limit_bytes=20 << 20),
    )(offsets, part, *operands)


def shards(
    visibility, uv_offset, w_offset, taper, row_count, block_owner, block_slot, subgrid_offset
):
    blocks_here, blk = visibility.shape[1], visibility.shape[3]
    owners = lax.axis_size("uv")
    parts = lax.axis_size("freq")
    cap = 2 * blocks_here // owners
    sent = pack(
        row_count[0],
        block_owner[0, :, 0],
        block_slot[0],
        visibility[0],
        uv_offset[0],
        w_offset[0],
        owners,
        cap,
    )
    recv = lax.all_to_all(in_vmem(sent), "uv", split_axis=0, concat_axis=0, tiled=True)
    recv = in_vmem(recv)
    table = in_vmem(tables(taper, blk))
    part = lax.axis_index("freq").astype(jnp.int32).reshape(1)
    *pieces, kept, kept_v, kept_c = tile_rows(subgrid_offset, part, recv, table, cap, parts)
    moved = [
        lax.ppermute(pieces[s], "freq", [(i, (i + s) % parts) for i in range(parts)])
        for s in range(1, parts)
    ]
    total = tile_rows(
        subgrid_offset,
        part,
        (kept, in_vmem(kept_v), in_vmem(kept_c)),
        table,
        cap,
        parts,
        in_vmem(pieces[0]),
    )
    for piece in moved:
        total = total + piece
    return total


def solution(mesh):
    placed = (
        P("freq", "uv", None, None),
        P("freq", "uv", None, None),
        P("freq", "uv", None),
        P(),
        P("freq", "uv"),
        P("freq", "uv", None),
        P("freq", "uv"),
        P("uv", None),
    )
    return jax.shard_map(
        shards, mesh=mesh, in_specs=placed, out_specs=P(("uv", "freq"), None, None), check_vma=False
    )
```

```python
import functools
import math

import jax
import jax.numpy as jnp
import numpy as np
from jax import lax
from jax.experimental import pallas as pl
from jax.experimental.pallas import tpu as pltpu
from jax.sharding import PartitionSpec as P

TILE = 128
LANES = 128
COMPS = 8
SIDES = 3
BESIDE = 10
field_width = 0.5

F32 = jnp.float32
BF16 = jnp.bfloat16


def fit_even(function, degree):
    points = np.cos(np.pi * (np.arange(400) + 0.5) / 400) * 0.125 + 0.125
    fit = np.polynomial.chebyshev.Chebyshev.fit(points, function(np.sqrt(points)), degree, domain=[0, 0.25])
    return [float(c) for c in fit.convert(kind=np.polynomial.Polynomial).coef]


SIN_COEF = fit_even(lambda f: math.sqrt(2) * np.sin(np.pi * f) / f, 3)
COS_COEF = fit_even(lambda f: math.sqrt(2) * np.cos(np.pi * f), 4)


def cos_sin_turns(turns):
    frac = turns - jnp.round(turns)
    square = frac * frac
    cos_half = COS_COEF[-1] * square + COS_COEF[-2]
    sin_half = SIN_COEF[-1] * square + SIN_COEF[-2]
    for c in COS_COEF[-3::-1]:
        cos_half = cos_half * square + c
    for c in SIN_COEF[-3::-1]:
        sin_half = sin_half * square + c
    sin_half = sin_half * frac
    return 1.0 - sin_half * sin_half, sin_half * cos_half


def split(x):
    high = x.astype(BF16)
    return high, (x - high.astype(F32)).astype(BF16)


def in_vmem(x):
    return pltpu.with_memory_space_constraint(x, pltpu.VMEM)


def iota(shape, axis):
    return lax.broadcasted_iota(jnp.int32, shape, axis)


def pack_kernel(*refs, cap):
    given, out_ref, held, used_ref, sems = refs[:6], refs[6], refs[7:13], refs[13], refs[14]
    count_ref, owner_ref, slot_ref, vis_ref, uv_ref, w_ref = held
    copies = [pltpu.make_async_copy(a, b, sems.at[i]) for i, (a, b) in enumerate(zip(given, held))]
    for copy in copies:
        copy.start()
    owners = out_ref.shape[0]
    blk = vis_ref.shape[2]
    blocks = vis_ref.shape[0]
    extra = out_ref.shape[1] - cap
    shape = (8, blk)
    row, lane = iota(shape, 0), iota(shape, 1)

    def clear(o, carry):
        used_ref[o] = 0
        for t in range(extra):
            out_ref[o, cap + t] = jnp.zeros(shape, F32)
        return carry

    lax.fori_loop(0, owners, clear, 0)
    for copy in copies:
        copy.wait()

    def place(j, carry):
        o = owner_ref[j]
        r = used_ref[o]
        used_ref[o] = r + 1
        count = count_ref[j]
        out_ref[o, r] = vis_ref[j]
        u, v, w = uv_ref[j, 0:1, :], uv_ref[j, 1:2, :], w_ref[pl.ds(j, 1), :]
        part = row % 4
        coords = jnp.where(part == 0, u, jnp.where(part == 1, v, w))
        t = cap + r // 2
        mine = (row // 4 == r % 2) & (part < 3)
        out_ref[o, t] = jnp.where(mine, coords, out_ref[o, t])
        meta = jnp.where(lane == 2 * r, count.astype(F32), slot_ref[j].astype(F32))
        here = (row == 3) & (lane // 2 == r)
        out_ref[o, cap] = jnp.where(here, meta, out_ref[o, cap])
        return carry

    lax.fori_loop(0, blocks, place, 0, unroll=4)


def pack(counts, owner, slot, vis, uv, w, owners, cap):
    extra = (cap + 1) // 2
    blk = vis.shape[2]
    operands = (counts, owner, slot, vis, uv, w)
    return pl.pallas_call(
        functools.partial(pack_kernel, cap=cap),
        out_shape=jax.ShapeDtypeStruct((owners, cap + extra, 8, blk), F32),
        in_specs=[pl.BlockSpec(memory_space=pltpu.HBM)] * 6,
        out_specs=pl.BlockSpec(memory_space=pltpu.VMEM),
        scratch_shapes=[pltpu.SMEM(x.shape, x.dtype) for x in operands[:3]]
        + [pltpu.VMEM(x.shape, x.dtype) for x in operands[3:]]
        + [pltpu.SMEM((owners,), jnp.int32), pltpu.SemaphoreType.DMA((6,))],
        name="pack",
    )(*operands)


def transform_constants(sub, blk, pack):
    half = sub // 2
    scale = 1.0 / math.sqrt(blk) / sub
    k = np.arange(sub)
    both = np.zeros((2, 4, half, sub), np.complex128)
    pick = np.zeros((2, 4, half, sub), np.float32)
    for a in range(half):
        up = np.exp(-2j * np.pi * k * (half + a) / sub) * scale
        down = np.exp(-2j * np.pi * k * (half - a) / sub) * scale
        pick[0, :, a, half + a] = 1
        pick[1, :, a, half - a if a else 0] = 1
        if a == 0:
            both[0, 0, 0], both[0, 1, 0] = up, -1j * up
            both[1, 2, 0], both[1, 3, 0] = -1j * scale, scale
        else:
            both[0, :, a] = [up, -1j * up, -1j * up, -up]
            both[1, :, a] = [down, -1j * down, 1j * down, down]
    both = both.reshape(2, 4 * half, sub)
    coef = np.zeros((2, pack, 4 * half, LANES), np.float32)
    for i in range(pack):
        for part, values in enumerate((both.real, both.imag)):
            at = (part * pack + i) * sub
            coef[:, i, :, at : at + sub] = values
    return coef, pick.reshape(2, 4 * half, sub)


def twiddle_sines(sub):
    return [math.sin(2 * math.pi * k / sub) for k in range(1, sub // 4 + 1)]


def tables_kernel(taper_ref, coef_ref, pick_ref, table_ref, n_ref):
    sub = taper_ref.shape[0]
    half = sub // 2
    row = iota((8, LANES), 0)
    step = field_width / sub
    rowf = row.astype(F32)

    def n_of(y, x):
        s = (x * x + y * y) * (step * step)
        return s / (1.0 + jnp.sqrt(1.0 - s))

    for j in range(8):
        n_ref[j] = n_of(float(j), rowf + 8.0)
        shifted = jnp.where(row >= j, 0.0, 8.0)
        n_ref[8 + j] = n_of(float(j) + shifted, rowf + shifted)
    n_ref[16] = n_of(rowf + 8.0, rowf + 8.0)
    n_ref[17] = n_of(float(half), rowf)
    n_ref[18] = n_of(float(half), rowf + 8.0)
    for i, value in enumerate(twiddle_sines(sub)):
        n_ref[half + 3 + i] = value * jnp.where(row < 4, -1.0, 1.0)
    pack, rows = coef_ref.shape[1], coef_ref.shape[2]
    dims = (((1,), (1,)), ((), ()))
    plus, minus = [
        lax.dot_general(pick_ref[i], taper_ref[...], dims, precision=lax.Precision.HIGHEST)
        for i in range(2)
    ]
    for y in range(sub):
        up = jnp.broadcast_to(plus[:, y : y + 1], (rows, LANES))
        down = jnp.broadcast_to(minus[:, y : y + 1], (rows, LANES))
        for i in range(pack):
            at = pl.ds(i * rows, rows)
            table_ref[0, y, at], table_ref[1, y, at] = split(up * coef_ref[0, i] + down * coef_ref[1, i])


def tables(taper, blk):
    sub = taper.shape[0]
    pack = LANES // (2 * sub)
    coef, pick = transform_constants(sub, blk, pack)
    vmem = pl.BlockSpec(memory_space=pltpu.VMEM)
    return pl.pallas_call(
        tables_kernel,
        out_shape=[
            jax.ShapeDtypeStruct((2, sub, LANES, LANES), BF16),
            jax.ShapeDtypeStruct((sub // 2 + 3 + sub // 4, 8, LANES), F32),
        ],
        in_specs=[vmem] * 3,
        out_specs=[vmem] * 2,
        name="tables",
        compiler_params=pltpu.CompilerParams(vmem_limit_bytes=16 << 20),
    )(taper, jnp.asarray(coef), jnp.asarray(pick))


def fourier(values, times):
    count = len(values)
    if count == 1:
        return values
    even, odd = fourier(values[0::2], times), fourier(values[1::2], times)
    odd = [times(x, k, count) for k, x in enumerate(odd)]
    return [e + o for e, o in zip(even, odd)] + [e - o for e, o in zip(even, odd)]


def lane_sums_row(place, pack, stride):
    return lax.rem(place, pack) * stride + lax.div(place, pack) * 8


def tile_kernel(*refs, inside, cap, sub, parts, chunks):
    if inside:
        offset_ref, part_ref, kept_ref, kept_v, kept_c, table_ref, n_ref, base_ref, out_ref, *rest = refs
    else:
        offset_ref, part_ref, recv_ref, table_ref, n_ref = refs[:5]
        outs = refs[5 : 5 + parts]
        kept_ref, kept_v, kept_c, *rest = refs[5 + parts :]
        meta_ref, order_ref, place_ref, fill_ref, at_ref, live_ref, to_ref, buf_v, buf_c, sem, *rest = rest
        owners = recv_ref.shape[0]
    (
        b_ref, w_ref, x16_ref, sums_ref, z_ref, lines_ref, tile_ref,
    ) = rest
    owned = offset_ref.shape[0]
    blk = kept_v.shape[2]
    half = sub // 2
    pack = LANES // (2 * sub)
    stride = owned // pack * 8
    keep_rows = TILE // parts
    head = owned + 3
    shape = (8, blk)
    row, lane = iota(shape, 0), iota(shape, 1)
    blk_log = blk.bit_length() - 1
    assert half == 16 and blk == 1 << blk_log
    if not inside:
        meta_copy = pltpu.make_async_copy(recv_ref.at[:, cap, 3], meta_ref, sem)
        meta_copy.start()

    first_row = part_ref[0] * keep_rows
    if inside:
        listed, count_all = kept_ref[0], kept_ref[1]
    else:

        def clear(s, carry):
            fill_ref[s] = 0
            order_ref[s] = 0
            kept_ref[2 + s] = 0
            return carry

        lax.fori_loop(0, owned + 1, clear, 0, unroll=True)

        def choose(s, n):
            corner = offset_ref[s, 0]
            within = (corner >= first_row) & (corner + sub <= first_row + keep_rows)
            place_ref[s] = jnp.where(within, owned - 1 - (s - n), n)
            order_ref[n] = s
            kept_ref[2 + s - n] = s
            return n + jnp.where(within, 0, 1)

        others = lax.fori_loop(0, owned, choose, 0, unroll=True)

    step = field_width / sub
    rowf = row.astype(F32)
    s_corner = 2.0 * half * half * step * step
    n_corner = s_corner / (1.0 + math.sqrt(1.0 - s_corner))
    sign = jnp.where(row < 4, -1.0, 1.0)
    if inside:
        tile_ref[0:keep_rows] = base_ref[...]
        tile_ref[keep_rows:] = jnp.zeros((sub, COMPS, TILE), F32)
    else:
        tile_ref[...] = jnp.zeros_like(tile_ref)

    def clear_sums(group, carry):
        for i in range(pack):
            at = pl.ds(pl.multiple_of(i * stride + group * 8, 8), 8)
            for part in range(2):
                for g in range(half + 1):
                    sums_ref[part, g, at] = jnp.zeros((8, 4 * half), F32)
        return carry

    lax.fori_loop(0, lax.div(count_all + (pack - 1), pack) if inside else owned // pack, clear_sums, 0)
    if not inside:
        meta_copy.wait()

        def gather(src, carry):
            moved = []
            for r in range(cap):
                count = meta_ref[src, 2 * r].astype(jnp.int32)
                place = place_ref[meta_ref[src, 2 * r + 1].astype(jnp.int32)]
                p = fill_ref[place]
                fill_ref[place] = p + count
                shift = p & (blk - 1)
                rows = (r % 2) * 4
                v = pltpu.roll(recv_ref[src, r], shift, 1)
                c = pltpu.roll(recv_ref[src, cap + r // 2], shift, 1)[rows : rows + 4]
                moved.append((place * chunks + lax.shift_right_logical(p, blk_log), lane < shift, v, c))
            for at, keep, v, c in moved:
                buf_v[at] = jnp.where(keep, buf_v[at], v)
                buf_c[at] = jnp.where(keep[0:4], buf_c[at], c)
                buf_v[at + 1] = v
                buf_c[at + 1] = c
            return carry

        lax.fori_loop(0, owners, gather, 0, unroll=8)

        def leave(i, carry):
            left, load = carry
            used = lax.shift_right_logical(fill_ref[owned - 1 - i] + (blk - 1), blk_log)
            stays = (load < BESIDE) & (i < owned - others)
            order_ref[owned - 1 - i] = jnp.where(stays | (i >= owned - others), order_ref[owned - 1 - i], kept_ref[2 + i])
            return jnp.where(stays, i + 1, left), load + used

        left, _ = lax.fori_loop(0, owned, leave, (0, 0), unroll=True)
        count_all = owned - left

        def list_chunks(place, n):
            fill = fill_ref[place]
            to = lane_sums_row(place, pack, stride)

            def one(k, n):
                at_ref[n] = place * chunks + k
                live_ref[n] = fill - k * blk
                to_ref[n] = to
                return n + 1

            return lax.fori_loop(0, lax.shift_right_logical(fill + (blk - 1), blk_log), one, n)

        listed = lax.fori_loop(0, count_all, list_chunks, 0)
        for i in range(SIDES - 1):
            for ref in (at_ref, live_ref, to_ref):
                ref[listed + i] = 0

        def keep_chunks(i, n):
            place = owned - 1 - i
            fill = fill_ref[place]
            to = lane_sums_row(i, pack, stride)

            def one(k, n):
                live = lane < fill - k * blk
                kept_v[n] = jnp.where(live, buf_v[place * chunks + k], 0.0)
                kept_c[n] = jnp.where(live[0:4], buf_c[place * chunks + k], 0.0)
                kept_ref[head + n] = to
                return n + 1

            return lax.fori_loop(0, lax.shift_right_logical(fill + (blk - 1), blk_log), one, n)

        kept = lax.fori_loop(0, owned - count_all, keep_chunks, 0)
        for i in range(SIDES - 1):
            kept_v[kept + i] = jnp.zeros(shape, F32)
            kept_c[kept + i] = jnp.zeros((4, blk), F32)
            kept_ref[head + kept + i] = 0
        kept_ref[0] = kept
        kept_ref[1] = owned - count_all

    unit = rowf * step
    first = row == 0
    dims = (((1,), (1,)), ((), ()))

    def chunk(number, side):
        if inside:
            vis, coords, to = kept_v[number], kept_c[number], kept_ref[head + number]
        else:
            at, to = at_ref[number], to_ref[number]
            live = lane < live_ref[number]
            vis = jnp.where(live, buf_v[at], 0.0)
            coords = jnp.where(live[0:4], buf_c[at], 0.0)
        u, v, w = coords[0:1], coords[1:2], coords[2:3]
        far = jnp.where(
            row < 2,
            u * jnp.where(row == 0, 8 * step, half * step),
            jnp.where(row < 4, v * jnp.where(row == 2, 8 * step, half * step), w * n_corner),
        )
        cos_f, sin_f = cos_sin_turns(far)
        cos_f, sin_f = [[x[i : i + 1] for i in range(5)] for x in (cos_f, sin_f)]

        def line(t, c8, s8):
            c, s = cos_sin_turns(t * unit)
            return [c, c * c8 - s * s8], [s, s * c8 + c * s8]

        cos_a, sin_a = line(u, cos_f[0], sin_f[0])
        cos_b, sin_b = line(v, cos_f[2], sin_f[2])
        for i in range(2):
            b_ref[side, 0, 8 * i : 8 * i + 8] = cos_b[i]
            b_ref[side, 1, 8 * i : 8 * i + 8] = sin_b[i]
        b_ref[side, 0, half : half + 1] = cos_f[3]
        b_ref[side, 1, half : half + 1] = sin_f[3]
        ca16, sa16 = cos_f[1], sin_f[1]

        for j in range(8):
            both = cos_sin_turns(w * n_ref[8 + j])
            for i in range(2):
                w_ref[side, i, 1, 8 * j : 8 * j + 8] = both[i]
                w_ref[side, i, 2, 8 * j : 8 * j + 8] = both[i]
        diagonal = cos_sin_turns(w * n_ref[16])
        for j in range(8):
            for i in range(2):
                w_ref[side, i, 2, 9 * j : 9 * j + 1] = diagonal[i][j : j + 1]
        edge = [cos_sin_turns(w * n_ref[17 + i]) for i in range(2)]
        for i in range(2):
            cw, sw = edge[i]
            x16_ref[side, 0, 8 * i : 8 * i + 8] = cw * ca16 + sw * sa16
            x16_ref[side, 1, 8 * i : 8 * i + 8] = sw * ca16 - cw * sa16
        x16_ref[side, 0, half : half + 1] = cos_f[4] * ca16 + sin_f[4] * sa16
        x16_ref[side, 1, half : half + 1] = sin_f[4] * ca16 - cos_f[4] * sa16
        turned = -sign * pltpu.roll(vis, 4, 0)
        to = pl.ds(pl.multiple_of(to, 8), 8)

        def add(g, cw, sw):
            q1 = [cw[i] * cos_a[i] for i in range(2)]
            q2 = [sw[i] * cos_a[i] for i in range(2)]
            q3 = [cw[i] * sin_a[i] for i in range(2)]
            q4 = [sw[i] * sin_a[i] for i in range(2)]
            q3[0] = jnp.where(first, x16_ref[side, 1, g : g + 1], q3[0])
            q4[0] = jnp.where(first, x16_ref[side, 0, g : g + 1], q4[0])
            right = jnp.concatenate(split(jnp.concatenate(q1 + q2 + q3 + q4, 0)), 1)
            straight, across = vis * b_ref[side, 0, g : g + 1], turned * b_ref[side, 1, g : g + 1]
            left = jnp.concatenate(split(jnp.concatenate([straight, across], 0)), 0)
            out = lax.dot_general(
                jnp.concatenate([left, left], 1), right, dims, preferred_element_type=F32
            )
            sums_ref[0, g, to] += out[0:8] + out[16:24]
            if g > 0:
                sums_ref[1, g, to] += out[8:16] + out[24:32]

        add(half, [edge[i][0] for i in range(2)], [edge[i][1] for i in range(2)])
        for j in range(8):
            own, across = pl.ds(8 * j, 8), pl.ds(j, 8, stride=8)
            far_pair = cos_sin_turns(w * n_ref[j])
            pairs = []
            for i in range(2):
                w_ref[side, i, 0, 8 * j : 8 * j + 8] = far_pair[i]
                near = jnp.where(row >= j, w_ref[side, i, 1, own], w_ref[side, i, 1, across])
                pairs.append([near, far_pair[i]])
            add(j, *pairs)
        for j in range(8):
            own, across = pl.ds(8 * j, 8), pl.ds(j, 8, stride=8)
            pairs = []
            for i in range(2):
                far_one = jnp.where(row <= j, w_ref[side, i, 2, own], w_ref[side, i, 2, across])
                pairs.append([w_ref[side, i, 0, across], far_one])
            add(8 + j, *pairs)

    def some_chunks(i, carry):
        for side in range(SIDES):
            chunk(SIDES * i + side, side)
        return carry

    lax.fori_loop(0, lax.div(listed + (SIDES - 1), SIDES), some_chunks, 0)

    def transform_x(used):
        def along_x(y):
            sums = []
            for i in range(pack):
                at = pl.ds(i * stride, used)
                straight, across = sums_ref[0, abs(y - half), at], sums_ref[1, abs(y - half), at]
                sums.append(straight + across if y >= half else straight - across)
            high, low = split(jnp.concatenate(sums, 1))
            right = jnp.concatenate([table_ref[0, y], table_ref[0, y]], 0)
            z_ref[y, 0:used] = jnp.dot(
                jnp.concatenate([high, low], 1), right, preferred_element_type=F32
            ) + jnp.dot(high, table_ref[1, y], preferred_element_type=F32)

        for y in range(sub):
            along_x(y)

    groups = lax.div(count_all + (pack - 1), pack)
    if inside:
        few = stride // 2

        @pl.when(groups * 8 <= few)
        def _():
            transform_x(few)

        @pl.when(groups * 8 > few)
        def _():
            transform_x(stride)
    else:
        transform_x(stride)

    def times(x, k, count):
        if k == 0:
            return x
        k = k * (sub // count)
        cosine = math.cos(2 * math.pi * k / sub)
        sine = n_ref[half + 2 + min(k, sub // 2 - k)]
        turned = sine * pltpu.roll(x, 4, 0)
        return -turned if k == sub // 4 else cosine * x - turned

    top_row = tile_ref.shape[0] - sub

    def put(group):
        def one(i, ky, turn, here, corner_row):
            moved = jnp.where(here, pltpu.roll(lines_ref[ky], turn, 1), 0.0)
            tile_ref[corner_row + ky] += moved

        steps = []
        for i in range(pack):
            slot = (kept_ref if inside else order_ref)[group * pack + i + (2 if inside else 0)]
            corner_row, corner_col = offset_ref[slot, 0], offset_ref[slot, 1]
            if inside:
                corner_row = jnp.clip(corner_row - first_row, 0, top_row)
            here = (lane >= corner_col) & (lane < corner_col + sub)
            turn = (corner_col + (LANES - i * sub)) & (LANES - 1)
            steps += [functools.partial(one, i, ky, turn, here, corner_row) for ky in range(sub)]
        return steps

    def place(group, carry):
        steps = put(jnp.maximum(group - 1, 0))
        at = pl.ds(pl.multiple_of(group * 8, 8), 8)
        lines = []
        for y in range(sub):
            for step_of in steps[y * pack : (y + 1) * pack]:
                step_of()
            pair = z_ref[y, at]
            imag = pltpu.roll(pair, LANES // 2, 1)
            lines.append(pair + sign * pltpu.roll(imag, 4, 0))
        lines = fourier(lines, times)
        for ky in range(sub):
            lines_ref[ky] = lines[ky]
        return carry

    lines_ref[...] = jnp.zeros_like(lines_ref)
    lax.fori_loop(0, groups, place, 0)
    for step_of in put(jnp.maximum(groups - 1, 0)):
        step_of()

    if inside:
        out_ref[...] = tile_ref[0:keep_rows]
    else:
        for p in range(parts):
            which = lax.rem(part_ref[0] + p, parts)
            outs[p][...] = tile_ref[pl.ds(which * keep_rows, keep_rows)]


def tile_rows(offsets, part, given, table, cap, parts, base=None):
    inside = base is not None
    owned = offsets.shape[0]
    sub = table[0].shape[1]
    half = sub // 2
    blk = LANES
    smem = pl.BlockSpec(memory_space=pltpu.SMEM)
    vmem = pl.BlockSpec(memory_space=pltpu.VMEM)
    rows = TILE // parts
    shape = jax.ShapeDtypeStruct((rows, COMPS, TILE), F32)
    scratch, chunks = [], None
    if inside:
        operands = [*given, *table, base]
        in_specs = [smem] + [vmem] * 5
        out_shape, out_specs = shape, vmem
    else:
        owners, _, _, blk = given.shape
        chunks = owners * cap + 1
        most = owners * cap + SIDES
        index = pltpu.SMEM((owned + 1,), jnp.int32)
        listing = pltpu.SMEM((most,), jnp.int32)
        operands = [given, *table]
        in_specs = [vmem] * 3
        out_shape = [shape] * parts + [
            jax.ShapeDtypeStruct((owned + 3 + most,), jnp.int32),
            jax.ShapeDtypeStruct((most, 8, blk), F32),
            jax.ShapeDtypeStruct((most, 4, blk), F32),
        ]
        out_specs = [vmem] * parts + [smem, vmem, vmem]
        scratch = [
            pltpu.SMEM((owners, blk), F32),
            index,
            index,
            index,
            listing,
            listing,
            listing,
            pltpu.VMEM((owned * chunks + 1, 8, blk), F32),
            pltpu.VMEM((owned * chunks + 1, 4, blk), F32),
            pltpu.SemaphoreType.DMA,
        ]
    return pl.pallas_call(
        functools.partial(tile_kernel, inside=inside, cap=cap, sub=sub, parts=parts, chunks=chunks),
        out_shape=out_shape,
        in_specs=[smem, smem, *in_specs],
        out_specs=out_specs,
        scratch_shapes=scratch
        + [
            pltpu.VMEM((SIDES, 2, half + 8, blk), F32),
            pltpu.VMEM((SIDES, 2, 3, 64, blk), F32),
            pltpu.VMEM((SIDES, 2, half + 8, blk), F32),
            pltpu.VMEM((2, half + 1, owned * 8, 4 * half), F32),
            pltpu.VMEM((sub, owned * 2 * sub * 8 // LANES, LANES), F32),
            pltpu.VMEM((sub, 8, LANES), F32),
            pltpu.VMEM((rows + sub if inside else TILE, COMPS, TILE), F32),
        ],
        name="inner" if inside else "tile",
        compiler_params=pltpu.CompilerParams(vmem_limit_bytes=20 << 20),
    )(offsets, part, *operands)


def shards(
    visibility, uv_offset, w_offset, taper, row_count, block_owner, block_slot, subgrid_offset
):
    blocks_here, blk = visibility.shape[1], visibility.shape[3]
    owners = lax.axis_size("uv")
    parts = lax.axis_size("freq")
    cap = 2 * blocks_here // owners
    sent = pack(
        row_count[0],
        block_owner[0, :, 0],
        block_slot[0],
        visibility[0],
        uv_offset[0],
        w_offset[0],
        owners,
        cap,
    )
    recv = lax.all_to_all(in_vmem(sent), "uv", split_axis=0, concat_axis=0, tiled=True)
    recv = in_vmem(recv)
    table = [in_vmem(x) for x in tables(taper, blk)]
    part = lax.axis_index("freq").astype(jnp.int32).reshape(1)
    *pieces, kept, kept_v, kept_c = tile_rows(subgrid_offset, part, recv, table, cap, parts)
    moved = [
        lax.ppermute(pieces[s], "freq", [(i, (i + s) % parts) for i in range(parts)])
        for s in range(1, parts)
    ]
    total = tile_rows(
        subgrid_offset,
        part,
        (kept, in_vmem(kept_v), in_vmem(kept_c)),
        table,
        cap,
        parts,
        in_vmem(pieces[0]),
    )
    for piece in moved:
        total = total + piece
    return total


def solution(mesh):
    placed = (
        P("freq", "uv", None, None),
        P("freq", "uv", None, None),
        P("freq", "uv", None),
        P(),
        P("freq", "uv"),
        P("freq", "uv", None),
        P("freq", "uv"),
        P("uv", None),
    )
    return jax.shard_map(
        shards, mesh=mesh, in_specs=placed, out_specs=P(("uv", "freq"), None, None), check_vma=False
    )
```

```python
import functools
import math

import jax
import jax.numpy as jnp
import numpy as np
from jax import lax
from jax.experimental import pallas as pl
from jax.experimental.pallas import tpu as pltpu
from jax.sharding import PartitionSpec as P

TILE = 128
LANES = 128
COMPS = 8
SIDES = 3
BESIDE = 8
field_width = 0.5

F32 = jnp.float32
BF16 = jnp.bfloat16


def fit_even(function, degree):
    points = np.cos(np.pi * (np.arange(400) + 0.5) / 400) * 0.125 + 0.125
    fit = np.polynomial.chebyshev.Chebyshev.fit(points, function(np.sqrt(points)), degree, domain=[0, 0.25])
    return [float(c) for c in fit.convert(kind=np.polynomial.Polynomial).coef]


SIN_COEF = fit_even(lambda f: math.sqrt(2) * np.sin(np.pi * f) / f, 3)
COS_COEF = fit_even(lambda f: math.sqrt(2) * np.cos(np.pi * f), 4)


def cos_sin_turns(turns):
    frac = turns - jnp.round(turns)
    square = frac * frac
    cos_half = COS_COEF[-1] * square + COS_COEF[-2]
    sin_half = SIN_COEF[-1] * square + SIN_COEF[-2]
    for c in COS_COEF[-3::-1]:
        cos_half = cos_half * square + c
    for c in SIN_COEF[-3::-1]:
        sin_half = sin_half * square + c
    sin_half = sin_half * frac
    return 1.0 - sin_half * sin_half, sin_half * cos_half


def split(x):
    high = x.astype(BF16)
    return high, (x - high.astype(F32)).astype(BF16)


def in_vmem(x):
    return pltpu.with_memory_space_constraint(x, pltpu.VMEM)


def iota(shape, axis):
    return lax.broadcasted_iota(jnp.int32, shape, axis)


def pack_kernel(*refs, cap):
    given, out_ref, held, used_ref, sems = refs[:6], refs[6], refs[7:13], refs[13], refs[14]
    count_ref, owner_ref, slot_ref, vis_ref, uv_ref, w_ref = held
    copies = [pltpu.make_async_copy(a, b, sems.at[i]) for i, (a, b) in enumerate(zip(given, held))]
    for copy in copies:
        copy.start()
    owners = out_ref.shape[0]
    blk = vis_ref.shape[2]
    blocks = vis_ref.shape[0]
    extra = out_ref.shape[1] - cap
    shape = (8, blk)
    row, lane = iota(shape, 0), iota(shape, 1)

    def clear(o, carry):
        used_ref[o] = 0
        for t in range(extra):
            out_ref[o, cap + t] = jnp.zeros(shape, F32)
        return carry

    lax.fori_loop(0, owners, clear, 0)
    for copy in copies:
        copy.wait()

    def place(j, carry):
        o = owner_ref[j]
        r = used_ref[o]
        used_ref[o] = r + 1
        count = count_ref[j]
        out_ref[o, r] = vis_ref[j]
        u, v, w = uv_ref[j, 0:1, :], uv_ref[j, 1:2, :], w_ref[pl.ds(j, 1), :]
        part = row % 4
        coords = jnp.where(part == 0, u, jnp.where(part == 1, v, w))
        t = cap + r // 2
        mine = (row // 4 == r % 2) & (part < 3)
        out_ref[o, t] = jnp.where(mine, coords, out_ref[o, t])
        meta = jnp.where(lane == 2 * r, count.astype(F32), slot_ref[j].astype(F32))
        here = (row == 3) & (lane // 2 == r)
        out_ref[o, cap] = jnp.where(here, meta, out_ref[o, cap])
        return carry

    lax.fori_loop(0, blocks, place, 0, unroll=4)


def pack(counts, owner, slot, vis, uv, w, owners, cap):
    extra = (cap + 1) // 2
    blk = vis.shape[2]
    operands = (counts, owner, slot, vis, uv, w)
    return pl.pallas_call(
        functools.partial(pack_kernel, cap=cap),
        out_shape=jax.ShapeDtypeStruct((owners, cap + extra, 8, blk), F32),
        in_specs=[pl.BlockSpec(memory_space=pltpu.HBM)] * 6,
        out_specs=pl.BlockSpec(memory_space=pltpu.VMEM),
        scratch_shapes=[pltpu.SMEM(x.shape, x.dtype) for x in operands[:3]]
        + [pltpu.VMEM(x.shape, x.dtype) for x in operands[3:]]
        + [pltpu.SMEM((owners,), jnp.int32), pltpu.SemaphoreType.DMA((6,))],
        name="pack",
    )(*operands)


def transform_constants(sub, blk, pack):
    half = sub // 2
    scale = 1.0 / math.sqrt(blk) / sub
    k = np.arange(sub)
    both = np.zeros((2, 4, half, sub), np.complex128)
    pick = np.zeros((2, 4, half, sub), np.float32)
    for a in range(half):
        up = np.exp(-2j * np.pi * k * (half + a) / sub) * scale
        down = np.exp(-2j * np.pi * k * (half - a) / sub) * scale
        pick[0, :, a, half + a] = 1
        pick[1, :, a, half - a if a else 0] = 1
        if a == 0:
            both[0, 0, 0], both[0, 1, 0] = up, -1j * up
            both[1, 2, 0], both[1, 3, 0] = -1j * scale, scale
        else:
            both[0, :, a] = [up, -1j * up, -1j * up, -up]
            both[1, :, a] = [down, -1j * down, 1j * down, down]
    both = both.reshape(2, 4 * half, sub)
    coef = np.zeros((2, pack, 4 * half, LANES), np.float32)
    for i in range(pack):
        for part, values in enumerate((both.real, both.imag)):
            at = (part * pack + i) * sub
            coef[:, i, :, at : at + sub] = values
    return coef, pick.reshape(2, 4 * half, sub)


def twiddle_sines(sub):
    return [math.sin(2 * math.pi * k / sub) for k in range(1, sub // 4 + 1)]


def tables_kernel(taper_ref, coef_ref, pick_ref, table_ref, n_ref):
    sub = taper_ref.shape[0]
    half = sub // 2
    row = iota((8, LANES), 0)
    step = field_width / sub
    rowf = row.astype(F32)

    def n_of(y, x):
        s = (x * x + y * y) * (step * step)
        return s / (1.0 + jnp.sqrt(1.0 - s))

    for j in range(8):
        n_ref[j] = n_of(float(j), rowf + 8.0)
        shifted = jnp.where(row >= j, 0.0, 8.0)
        n_ref[8 + j] = n_of(float(j) + shifted, rowf + shifted)
    n_ref[16] = n_of(rowf + 8.0, rowf + 8.0)
    n_ref[17] = n_of(float(half), rowf)
    n_ref[18] = n_of(float(half), rowf + 8.0)
    for i, value in enumerate(twiddle_sines(sub)):
        n_ref[half + 3 + i] = value * jnp.where(row < 4, -1.0, 1.0)
    pack, rows = coef_ref.shape[1], coef_ref.shape[2]
    dims = (((1,), (1,)), ((), ()))
    plus, minus = [
        lax.dot_general(pick_ref[i], taper_ref[...], dims, precision=lax.Precision.HIGHEST)
        for i in range(2)
    ]
    for y in range(sub):
        up = jnp.broadcast_to(plus[:, y : y + 1], (rows, LANES))
        down = jnp.broadcast_to(minus[:, y : y + 1], (rows, LANES))
        for i in range(pack):
            at = pl.ds(i * rows, rows)
            table_ref[0, y, at], table_ref[1, y, at] = split(up * coef_ref[0, i] + down * coef_ref[1, i])


def tables(taper, blk):
    sub = taper.shape[0]
    pack = LANES // (2 * sub)
    coef, pick = transform_constants(sub, blk, pack)
    vmem = pl.BlockSpec(memory_space=pltpu.VMEM)
    return pl.pallas_call(
        tables_kernel,
        out_shape=[
            jax.ShapeDtypeStruct((2, sub, LANES, LANES), BF16),
            jax.ShapeDtypeStruct((sub // 2 + 3 + sub // 4, 8, LANES), F32),
        ],
        in_specs=[vmem] * 3,
        out_specs=[vmem] * 2,
        name="tables",
        compiler_params=pltpu.CompilerParams(vmem_limit_bytes=16 << 20),
    )(taper, jnp.asarray(coef), jnp.asarray(pick))


def fourier(values, times):
    count = len(values)
    if count == 1:
        return values
    even, odd = fourier(values[0::2], times), fourier(values[1::2], times)
    odd = [times(x, k, count) for k, x in enumerate(odd)]
    return [e + o for e, o in zip(even, odd)] + [e - o for e, o in zip(even, odd)]


def lane_sums_row(place, pack, stride):
    return lax.rem(place, pack) * stride + lax.div(place, pack) * 8


def tile_kernel(*refs, inside, cap, sub, parts, chunks):
    if inside:
        offset_ref, part_ref, kept_ref, kept_v, kept_c, table_ref, n_ref, base_ref, out_ref, *rest = refs
    else:
        offset_ref, part_ref, recv_ref, table_ref, n_ref = refs[:5]
        outs = refs[5 : 5 + parts]
        kept_ref, kept_v, kept_c, *rest = refs[5 + parts :]
        meta_ref, order_ref, place_ref, fill_ref, at_ref, live_ref, to_ref, buf_v, buf_c, sem, *rest = rest
        owners = recv_ref.shape[0]
    (
        b_ref, w_ref, x16_ref, sums_ref, z_ref, lines_ref, tile_ref,
    ) = rest
    owned = offset_ref.shape[0]
    blk = kept_v.shape[2]
    half = sub // 2
    pack = LANES // (2 * sub)
    stride = owned // pack * 8
    keep_rows = TILE // parts
    head = owned + 3
    shape = (8, blk)
    row, lane = iota(shape, 0), iota(shape, 1)
    blk_log = blk.bit_length() - 1
    assert half == 16 and blk == 1 << blk_log
    if not inside:
        meta_copy = pltpu.make_async_copy(recv_ref.at[:, cap, 3], meta_ref, sem)
        meta_copy.start()

    first_row = part_ref[0] * keep_rows
    if inside:
        listed, count_all = kept_ref[0], kept_ref[1]
    else:

        def clear(s, carry):
            fill_ref[s] = 0
            order_ref[s] = 0
            kept_ref[2 + s] = 0
            return carry

        lax.fori_loop(0, owned + 1, clear, 0, unroll=True)

        def choose(s, n):
            corner = offset_ref[s, 0]
            within = (corner >= first_row) & (corner + sub <= first_row + keep_rows)
            place_ref[s] = jnp.where(within, owned - 1 - (s - n), n)
            order_ref[n] = s
            kept_ref[2 + s - n] = s
            return n + jnp.where(within, 0, 1)

        others = lax.fori_loop(0, owned, choose, 0, unroll=True)

    step = field_width / sub
    rowf = row.astype(F32)
    s_corner = 2.0 * half * half * step * step
    n_corner = s_corner / (1.0 + math.sqrt(1.0 - s_corner))
    sign = jnp.where(row < 4, -1.0, 1.0)
    if inside:
        tile_ref[0:keep_rows] = base_ref[...]
        tile_ref[keep_rows:] = jnp.zeros((sub, COMPS, TILE), F32)
    else:
        tile_ref[...] = jnp.zeros_like(tile_ref)

    def clear_sums(group, carry):
        for i in range(pack):
            at = pl.ds(pl.multiple_of(i * stride + group * 8, 8), 8)
            for part in range(2):
                for g in range(half + 1):
                    sums_ref[part, g, at] = jnp.zeros((8, 4 * half), F32)
        return carry

    lax.fori_loop(0, lax.div(count_all + (pack - 1), pack) if inside else owned // pack, clear_sums, 0)
    if not inside:
        meta_copy.wait()

        def gather(src, carry):
            moved = []
            for r in range(cap):
                count = meta_ref[src, 2 * r].astype(jnp.int32)
                place = place_ref[meta_ref[src, 2 * r + 1].astype(jnp.int32)]
                p = fill_ref[place]
                fill_ref[place] = p + count
                shift = p & (blk - 1)
                rows = (r % 2) * 4
                v = pltpu.roll(recv_ref[src, r], shift, 1)
                c = pltpu.roll(recv_ref[src, cap + r // 2], shift, 1)[rows : rows + 4]
                moved.append((place * chunks + lax.shift_right_logical(p, blk_log), lane < shift, v, c))
            for at, keep, v, c in moved:
                buf_v[at] = jnp.where(keep, buf_v[at], v)
                buf_c[at] = jnp.where(keep[0:4], buf_c[at], c)
                buf_v[at + 1] = v
                buf_c[at + 1] = c
            return carry

        lax.fori_loop(0, owners, gather, 0, unroll=8)

        def leave(i, carry):
            left, load = carry
            used = lax.shift_right_logical(fill_ref[owned - 1 - i] + (blk - 1), blk_log)
            stays = (load < BESIDE) & (i < owned - others)
            order_ref[owned - 1 - i] = jnp.where(stays | (i >= owned - others), order_ref[owned - 1 - i], kept_ref[2 + i])
            return jnp.where(stays, i + 1, left), load + used

        left, _ = lax.fori_loop(0, owned, leave, (0, 0), unroll=True)
        count_all = owned - left

        def list_chunks(place, n):
            fill = fill_ref[place]
            to = lane_sums_row(place, pack, stride)

            def one(k, n):
                at_ref[n] = place * chunks + k
                live_ref[n] = fill - k * blk
                to_ref[n] = to
                return n + 1

            return lax.fori_loop(0, lax.shift_right_logical(fill + (blk - 1), blk_log), one, n)

        listed = lax.fori_loop(0, count_all, list_chunks, 0)
        for i in range(SIDES - 1):
            for ref in (at_ref, live_ref, to_ref):
                ref[listed + i] = 0

        def keep_chunks(i, n):
            place = owned - 1 - i
            fill = fill_ref[place]
            to = lane_sums_row(i, pack, stride)

            def one(k, n):
                live = lane < fill - k * blk
                kept_v[n] = jnp.where(live, buf_v[place * chunks + k], 0.0)
                kept_c[n] = jnp.where(live[0:4], buf_c[place * chunks + k], 0.0)
                kept_ref[head + n] = to
                return n + 1

            return lax.fori_loop(0, lax.shift_right_logical(fill + (blk - 1), blk_log), one, n)

        kept = lax.fori_loop(0, owned - count_all, keep_chunks, 0)
        for i in range(SIDES - 1):
            kept_v[kept + i] = jnp.zeros(shape, F32)
            kept_c[kept + i] = jnp.zeros((4, blk), F32)
            kept_ref[head + kept + i] = 0
        kept_ref[0] = kept
        kept_ref[1] = owned - count_all

    unit = rowf * step
    first = row == 0
    dims = (((1,), (1,)), ((), ()))

    def chunk(number, side):
        if inside:
            vis, coords, to = kept_v[number], kept_c[number], kept_ref[head + number]
        else:
            at, to = at_ref[number], to_ref[number]
            live = lane < live_ref[number]
            vis = jnp.where(live, buf_v[at], 0.0)
            coords = jnp.where(live[0:4], buf_c[at], 0.0)
        u, v, w = coords[0:1], coords[1:2], coords[2:3]
        far = jnp.where(
            row < 2,
            u * jnp.where(row == 0, 8 * step, half * step),
            jnp.where(row < 4, v * jnp.where(row == 2, 8 * step, half * step), w * n_corner),
        )
        cos_f, sin_f = cos_sin_turns(far)
        cos_f, sin_f = [[x[i : i + 1] for i in range(5)] for x in (cos_f, sin_f)]

        def line(t, c8, s8):
            c, s = cos_sin_turns(t * unit)
            return [c, c * c8 - s * s8], [s, s * c8 + c * s8]

        cos_a, sin_a = line(u, cos_f[0], sin_f[0])
        cos_b, sin_b = line(v, cos_f[2], sin_f[2])
        for i in range(2):
            b_ref[side, 0, 8 * i : 8 * i + 8] = cos_b[i]
            b_ref[side, 1, 8 * i : 8 * i + 8] = sin_b[i]
        b_ref[side, 0, half : half + 1] = cos_f[3]
        b_ref[side, 1, half : half + 1] = sin_f[3]
        ca16, sa16 = cos_f[1], sin_f[1]

        for j in range(8):
            both = cos_sin_turns(w * n_ref[8 + j])
            for i in range(2):
                w_ref[side, i, 1, 8 * j : 8 * j + 8] = both[i]
                w_ref[side, i, 2, 8 * j : 8 * j + 8] = both[i]
        diagonal = cos_sin_turns(w * n_ref[16])
        for j in range(8):
            for i in range(2):
                w_ref[side, i, 2, 9 * j : 9 * j + 1] = diagonal[i][j : j + 1]
        edge = [cos_sin_turns(w * n_ref[17 + i]) for i in range(2)]
        for i in range(2):
            cw, sw = edge[i]
            x16_ref[side, 0, 8 * i : 8 * i + 8] = cw * ca16 + sw * sa16
            x16_ref[side, 1, 8 * i : 8 * i + 8] = sw * ca16 - cw * sa16
        x16_ref[side, 0, half : half + 1] = cos_f[4] * ca16 + sin_f[4] * sa16
        x16_ref[side, 1, half : half + 1] = sin_f[4] * ca16 - cos_f[4] * sa16
        turned = -sign * pltpu.roll(vis, 4, 0)
        to = pl.ds(pl.multiple_of(to, 8), 8)

        def add(g, cw, sw):
            q1 = [cw[i] * cos_a[i] for i in range(2)]
            q2 = [sw[i] * cos_a[i] for i in range(2)]
            q3 = [cw[i] * sin_a[i] for i in range(2)]
            q4 = [sw[i] * sin_a[i] for i in range(2)]
            q3[0] = jnp.where(first, x16_ref[side, 1, g : g + 1], q3[0])
            q4[0] = jnp.where(first, x16_ref[side, 0, g : g + 1], q4[0])
            right = jnp.concatenate(split(jnp.concatenate(q1 + q2 + q3 + q4, 0)), 1)
            straight, across = vis * b_ref[side, 0, g : g + 1], turned * b_ref[side, 1, g : g + 1]
            left = jnp.concatenate(split(jnp.concatenate([straight, across], 0)), 0)
            out = lax.dot_general(
                jnp.concatenate([left, left], 1), right, dims, preferred_element_type=F32
            )
            sums_ref[0, g, to] += out[0:8] + out[16:24]
            if g > 0:
                sums_ref[1, g, to] += out[8:16] + out[24:32]

        add(half, [edge[i][0] for i in range(2)], [edge[i][1] for i in range(2)])
        for j in range(8):
            own, across = pl.ds(8 * j, 8), pl.ds(j, 8, stride=8)
            far_pair = cos_sin_turns(w * n_ref[j])
            pairs = []
            for i in range(2):
                w_ref[side, i, 0, 8 * j : 8 * j + 8] = far_pair[i]
                near = jnp.where(row >= j, w_ref[side, i, 1, own], w_ref[side, i, 1, across])
                pairs.append([near, far_pair[i]])
            add(j, *pairs)
        for j in range(8):
            own, across = pl.ds(8 * j, 8), pl.ds(j, 8, stride=8)
            pairs = []
            for i in range(2):
                far_one = jnp.where(row <= j, w_ref[side, i, 2, own], w_ref[side, i, 2, across])
                pairs.append([w_ref[side, i, 0, across], far_one])
            add(8 + j, *pairs)

    def some_chunks(i, carry):
        for side in range(SIDES):
            chunk(SIDES * i + side, side)
        return carry

    lax.fori_loop(0, lax.div(listed + (SIDES - 1), SIDES), some_chunks, 0)

    def transform_x(used):
        def along_x(y):
            sums = []
            for i in range(pack):
                at = pl.ds(i * stride, used)
                straight, across = sums_ref[0, abs(y - half), at], sums_ref[1, abs(y - half), at]
                sums.append(straight + across if y >= half else straight - across)
            high, low = split(jnp.concatenate(sums, 1))
            right = jnp.concatenate([table_ref[0, y], table_ref[0, y]], 0)
            z_ref[y, 0:used] = jnp.dot(
                jnp.concatenate([high, low], 1), right, preferred_element_type=F32
            ) + jnp.dot(high, table_ref[1, y], preferred_element_type=F32)

        for y in range(sub):
            along_x(y)

    groups = lax.div(count_all + (pack - 1), pack)
    if inside:
        few = stride // 2

        @pl.when(groups * 8 <= few)
        def _():
            transform_x(few)

        @pl.when(groups * 8 > few)
        def _():
            transform_x(stride)
    else:
        transform_x(stride)

    def times(x, k, count):
        if k == 0:
            return x
        k = k * (sub // count)
        cosine = math.cos(2 * math.pi * k / sub)
        sine = n_ref[half + 2 + min(k, sub // 2 - k)]
        turned = sine * pltpu.roll(x, 4, 0)
        return -turned if k == sub // 4 else cosine * x - turned

    top_row = tile_ref.shape[0] - sub

    def put(group):
        def one(i, ky, turn, here, corner_row):
            moved = jnp.where(here, pltpu.roll(lines_ref[ky], turn, 1), 0.0)
            tile_ref[corner_row + ky] += moved

        steps = []
        for i in range(pack):
            slot = (kept_ref if inside else order_ref)[group * pack + i + (2 if inside else 0)]
            corner_row, corner_col = offset_ref[slot, 0], offset_ref[slot, 1]
            if inside:
                corner_row = jnp.clip(corner_row - first_row, 0, top_row)
            here = (lane >= corner_col) & (lane < corner_col + sub)
            turn = (corner_col + (LANES - i * sub)) & (LANES - 1)
            steps += [functools.partial(one, i, ky, turn, here, corner_row) for ky in range(sub)]
        return steps

    def place(group, carry):
        steps = put(jnp.maximum(group - 1, 0))
        at = pl.ds(pl.multiple_of(group * 8, 8), 8)
        lines = []
        for y in range(sub):
            for step_of in steps[y * pack : (y + 1) * pack]:
                step_of()
            pair = z_ref[y, at]
            imag = pltpu.roll(pair, LANES // 2, 1)
            lines.append(pair + sign * pltpu.roll(imag, 4, 0))
        lines = fourier(lines, times)
        for ky in range(sub):
            lines_ref[ky] = lines[ky]
        return carry

    lines_ref[...] = jnp.zeros_like(lines_ref)
    lax.fori_loop(0, groups, place, 0)
    for step_of in put(jnp.maximum(groups - 1, 0)):
        step_of()

    if inside:
        out_ref[...] = tile_ref[0:keep_rows]
    else:
        for p in range(parts):
            which = lax.rem(part_ref[0] + p, parts)
            outs[p][...] = tile_ref[pl.ds(which * keep_rows, keep_rows)]


def tile_rows(offsets, part, given, table, cap, parts, base=None):
    inside = base is not None
    owned = offsets.shape[0]
    sub = table[0].shape[1]
    half = sub // 2
    blk = LANES
    smem = pl.BlockSpec(memory_space=pltpu.SMEM)
    vmem = pl.BlockSpec(memory_space=pltpu.VMEM)
    rows = TILE // parts
    shape = jax.ShapeDtypeStruct((rows, COMPS, TILE), F32)
    scratch, chunks = [], None
    if inside:
        operands = [*given, *table, base]
        in_specs = [smem] + [vmem] * 5
        out_shape, out_specs = shape, vmem
    else:
        owners, _, _, blk = given.shape
        chunks = owners * cap + 1
        most = owners * cap + SIDES
        index = pltpu.SMEM((owned + 1,), jnp.int32)
        listing = pltpu.SMEM((most,), jnp.int32)
        operands = [given, *table]
        in_specs = [vmem] * 3
        out_shape = [shape] * parts + [
            jax.ShapeDtypeStruct((owned + 3 + most,), jnp.int32),
            jax.ShapeDtypeStruct((most, 8, blk), F32),
            jax.ShapeDtypeStruct((most, 4, blk), F32),
        ]
        out_specs = [vmem] * parts + [smem, vmem, vmem]
        scratch = [
            pltpu.SMEM((owners, blk), F32),
            index,
            index,
            index,
            listing,
            listing,
            listing,
            pltpu.VMEM((owned * chunks + 1, 8, blk), F32),
            pltpu.VMEM((owned * chunks + 1, 4, blk), F32),
            pltpu.SemaphoreType.DMA,
        ]
    return pl.pallas_call(
        functools.partial(tile_kernel, inside=inside, cap=cap, sub=sub, parts=parts, chunks=chunks),
        out_shape=out_shape,
        in_specs=[smem, smem, *in_specs],
        out_specs=out_specs,
        scratch_shapes=scratch
        + [
            pltpu.VMEM((SIDES, 2, half + 8, blk), F32),
            pltpu.VMEM((SIDES, 2, 3, 64, blk), F32),
            pltpu.VMEM((SIDES, 2, half + 8, blk), F32),
            pltpu.VMEM((2, half + 1, owned * 8, 4 * half), F32),
            pltpu.VMEM((sub, owned * 2 * sub * 8 // LANES, LANES), F32),
            pltpu.VMEM((sub, 8, LANES), F32),
            pltpu.VMEM((rows + sub if inside else TILE, COMPS, TILE), F32),
        ],
        name="inner" if inside else "tile",
        compiler_params=pltpu.CompilerParams(vmem_limit_bytes=20 << 20),
    )(offsets, part, *operands)


def shards(
    visibility, uv_offset, w_offset, taper, row_count, block_owner, block_slot, subgrid_offset
):
    blocks_here, blk = visibility.shape[1], visibility.shape[3]
    owners = lax.axis_size("uv")
    parts = lax.axis_size("freq")
    cap = 2 * blocks_here // owners
    sent = pack(
        row_count[0],
        block_owner[0, :, 0],
        block_slot[0],
        visibility[0],
        uv_offset[0],
        w_offset[0],
        owners,
        cap,
    )
    recv = lax.all_to_all(in_vmem(sent), "uv", split_axis=0, concat_axis=0, tiled=True)
    recv = in_vmem(recv)
    table = [in_vmem(x) for x in tables(taper, blk)]
    part = lax.axis_index("freq").astype(jnp.int32).reshape(1)
    *pieces, kept, kept_v, kept_c = tile_rows(subgrid_offset, part, recv, table, cap, parts)
    moved = [
        lax.ppermute(pieces[s], "freq", [(i, (i + s) % parts) for i in range(parts)])
        for s in range(1, parts)
    ]
    total = tile_rows(
        subgrid_offset,
        part,
        (kept, in_vmem(kept_v), in_vmem(kept_c)),
        table,
        cap,
        parts,
        in_vmem(pieces[0]),
    )
    for piece in moved:
        total = total + piece
    return total


def solution(mesh):
    placed = (
        P("freq", "uv", None, None),
        P("freq", "uv", None, None),
        P("freq", "uv", None),
        P(),
        P("freq", "uv"),
        P("freq", "uv", None),
        P("freq", "uv"),
        P("uv", None),
    )
    return jax.shard_map(
        shards, mesh=mesh, in_specs=placed, out_specs=P(("uv", "freq"), None, None), check_vma=False
    )
```
